32 devices in a mesh: section: 4 (over z), expert: 4 (over y, x), dp: 2 (over core).
Axes of the slice: x: 2, y: 2, z: 4, core: 2. Of those that a mesh axis runs over, the one named last changes fastest.
Arguments:
- tokens: bfloat16 [2, 512, 2048], P(None, ('expert', 'dp')), may hold values from -24 to 24
- expert_ids: int32 [4, 2, 512, 4], P('section', None, ('expert', 'dp')), may hold values from 0 to 7, all different within a row; in each aligned block of 64 rows (0 to 63, 64 to 127, ..., all dimensions but the last counted through in order) at most 64 rows name the same one
- labels: int32 [2, 512], P(None, ('expert', 'dp')), may hold values from 0 to 127
- router: bfloat16 [4, 2048, 8], P('section'), may hold values from -0.125 to 0.125
- class_head: bfloat16 [2048, 128], replicated, may hold values from -0.5 to 0.5
- w_gate: bfloat16 [4, 8, 2048, 768], P('section', ('expert', 'dp')), may hold values from -0.125 to 0.125
- w_up: bfloat16 [4, 8, 2048, 768], P('section', ('expert', 'dp')), may hold values from -0.125 to 0.125
- w_down: bfloat16 [4, 8, 768, 2048], P('section', ('expert', 'dp')), may hold values from -0.21875 to 0.21875
Outputs:
- mean_loss: float32 [], replicated
- grad_head: float32 [2048, 128], replicated
- grad_router: float32 [4, 2048, 8], P('section')
- grad_gate: bfloat16 [4, 8, 2048, 768], P('section', ('expert', 'dp'))
- grad_up: bfloat16 [4, 8, 2048, 768], P('section', ('expert', 'dp'))
- grad_down: bfloat16 [4, 8, 768, 2048], P('section', ('expert', 'dp'))
The draws below stay inside these ranges and needn't reach their ends.
Inputs may be any that keep to these rules, and one draw needn't show every extreme that they name: `expert_ids`: each token names 4 different experts; among the 64 tokens of one device in one micro-batch and layer no expert is named more than 64 times, a bound that some block reaches.
All inputs are finite; a program needn't handle non-finite values.
Results may differ from the reference program's by a relative error of at most 0.025.
Values may be sent and summed in bfloat16 or wider, within the bound.
A program may use at most 320 MiB of HBM per device.

```python
import math
import jax
import jax.numpy as jnp
import numpy as np
from jax import lax

D = 2048
FFE = 768
NCLASS = 128
TOPK = 4
MB = 2
TOK_MB = 64
EXPERTS = 8
TOKENS = 512
CAP = 64
N_SECTION = 4


def draw_tokens(key, part):
    key_cols, key_rows, key_base = jax.random.split(key, 3)
    col_scale = jnp.exp(jax.random.uniform(key_cols, (1, 1, D), jnp.float32, math.log(0.3), math.log(3.0)))
    row_scale = jnp.exp(jax.random.uniform(key_rows, (MB, TOKENS, 1), jnp.float32, math.log(0.5), math.log(2.0)))
    base_draw = jax.random.normal(key_base, (MB, TOKENS, D), jnp.float32)
    return jnp.clip(base_draw * row_scale * col_scale, -24.0, 24.0).astype(jnp.bfloat16)


def with_ends(values, rng, smallest, high):
    extent = values.shape
    place = [jax.random.randint(jax.random.fold_in(rng, axis), (), 0, extent[axis]) for axis in range(len(extent))]
    values = values.at[tuple(place)].set(smallest)
    longest = extent.index(max(extent))
    place[longest] = (place[longest] + 1) % extent[longest]
    return values.at[tuple(place)].set(high)


def block_levels(stream_key, shape, pieces, least, largest):
    def one(position, blocks):
        draws = jax.random.uniform(jax.random.fold_in(jax.random.fold_in(stream_key, 6), position), (blocks,), jnp.float32, least / len(pieces), largest / len(pieces))
        return jnp.repeat(jnp.exp(draws), shape[position] // blocks).reshape((-1,) + (1,) * (len(shape) - position - 1))

    loudness = one(*pieces[0])
    for cut in pieces[1:]:
        loudness = loudness * one(*cut)
    return loudness


def deal_out(own_key, own, number, rows, count, top, most, slope):
    ranking = jax.random.permutation(own_key, count)
    crowded, common = portions_of(count, rows * top, most, slope, True), portions_of(count, rows * top, most, slope, False)
    places = jnp.arange(count)

    def named(lengths, rotation):
        used = int((lengths > 0).sum())
        fixed = max(1, used // 4)
        shifted = fixed + (places - fixed + rotation * (used - fixed)) % max(1, count - fixed)
        return jnp.zeros((count,), jnp.int32).at[ranking[jnp.where(places < fixed, places, shifted)]].set(jnp.asarray(lengths, jnp.int32))

    lengths = jnp.where(number % 4 == 0, named(crowded, number // 4), named(common, number - number // 4 - 1))
    mixed = jax.random.permutation(jax.random.fold_in(own, 3), count)
    source_of, taker = mixed[0:count // 2 * 2:2], mixed[1:count // 2 * 2:2]
    margin = jnp.minimum(lengths[source_of] - 1, most - lengths[taker]) // 2
    margin = jnp.where((source_of == ranking[0]) | (taker == ranking[0]) | (lengths[taker] == 0), 0, jnp.maximum(margin, 0))
    shifted = jax.random.randint(jax.random.fold_in(own, 4), (count // 2,), 0, 1 << 20) % (margin + 1)
    lengths = lengths.at[source_of].add(-shifted).at[taker].add(shifted)
    items = jnp.searchsorted(jnp.cumsum(lengths), jnp.arange(rows * top), side="right").astype(jnp.int32)
    table = items.reshape(top, rows).T
    table = table[jax.random.permutation(jax.random.fold_in(own, 1), rows)]
    rotation = jax.random.randint(jax.random.fold_in(own, 2), (rows, 1), 0, top)
    return jnp.take_along_axis(table, (jnp.arange(top)[None, :] + rotation) % top, axis=1)


def portions_of(number_of, total, bound, slope, full):
    weights = [(1 << 20) // math.isqrt(standing ** slope) + 1 for standing in range(1, number_of + 1)]
    largest = bound if full else min(bound, max(-(-total // number_of), total * weights[0] // sum(weights)))
    least = 1 if total - largest >= number_of - 1 else 0
    holding, spare = [largest] + [least] * (number_of - 1), total - largest - least * (number_of - 1)
    while spare > 0:
        candidates = [i for i in range(1, number_of) if holding[i] < largest] or [i for i in range(1, number_of) if holding[i] < bound]
        pool, remaining = sum([weights[i] for i in candidates]), spare
        for i in candidates:
            extra = min(bound - holding[i], max(1, remaining * weights[i] // pool), spare)
            holding[i] = holding[i] + extra
            spare = spare - extra
    return np.array(holding)


def scatter_about(own_key, shape, scale, most, pieces=(), kind=jnp.bfloat16):
    gain = block_levels(own_key, shape, pieces, -0.22, 0.18) if pieces else 1.0
    result = jax.random.normal(own_key, shape, jnp.float32) * scale * gain
    return jnp.minimum(jnp.maximum(result, -most), most).astype(kind)


def setup_inputs(seed: int = 0) -> dict:
    seeds = jax.random.split(jax.random.key(seed), 9)
    tokens = draw_tokens(jax.random.fold_in(seeds[8], 71), 0)
    expert_ids_keys = jax.random.split(jax.random.fold_in(seeds[1], 1), N_SECTION * MB * TOKENS // TOK_MB)
    expert_ids_turns = jax.random.permutation(jax.random.fold_in(seeds[1], 3), N_SECTION * MB * TOKENS // TOK_MB)
    expert_ids = jax.vmap(lambda own, number: deal_out(jax.random.fold_in(seeds[1], 2), own, number, TOK_MB, EXPERTS, TOPK, CAP, 2))(expert_ids_keys, expert_ids_turns).reshape((N_SECTION, MB, TOKENS, TOPK))
    labels = with_ends(jax.random.randint(seeds[2], (MB, TOKENS), 0, NCLASS), jax.random.fold_in(seeds[2], 1), 0, NCLASS - 1).astype(jnp.int32)
    router = scatter_about(seeds[3], (N_SECTION, D, EXPERTS), D ** -0.5, 0.125, ((0, 4),))
    class_head = scatter_about(seeds[4], (D, NCLASS), (D // 16) ** -0.5, 0.5)
    w_gate = scatter_about(seeds[5], (N_SECTION, EXPERTS, D, FFE), D ** -0.5, 0.125, ((0, 4), (1, 8)))
    w_up = scatter_about(seeds[6], (N_SECTION, EXPERTS, D, FFE), D ** -0.5, 0.125, ((0, 4), (1, 8)))
    w_down = scatter_about(seeds[7], (N_SECTION, EXPERTS, FFE, D), FFE ** -0.5, 0.21875, ((0, 4), (1, 8)))
    return dict(tokens=tokens, expert_ids=expert_ids, labels=labels, router=router, class_head=class_head, w_gate=w_gate, w_up=w_up, w_down=w_down)


soft_cap = 30.0
norm_eps = 1e-06

def capped(values):
    return soft_cap * jnp.tanh(values / soft_cap)

def normalize(layer_in):
    hidden_f = layer_in.astype(jnp.float32)
    inv_rms = lax.rsqrt(lax.optimization_barrier(jnp.mean(hidden_f * hidden_f, axis=-1, keepdims=True)) + norm_eps)
    return (hidden_f, inv_rms, (hidden_f * inv_rms).astype(jnp.bfloat16))

def gate_probs(normed, ids_now, router_w):
    logits = jnp.dot(normed, router_w, preferred_element_type=jnp.float32)
    one_hot = (ids_now[:, :, None] == jnp.arange(router_w.shape[1], dtype=jnp.int32)[None, None, :]).astype(jnp.float32)
    chosen = capped(lax.optimization_barrier(jnp.sum(one_hot * logits[:, None, :], axis=-1)))
    weights = jnp.exp(chosen)
    return (one_hot, chosen, weights / lax.optimization_barrier(jnp.sum(weights, axis=-1, keepdims=True)))

def expert_lists(flat_ids):

    def pick_rows(expert):
        return jnp.nonzero(flat_ids == expert, size=CAP * EXPERTS, fill_value=flat_ids.shape[0])[0].astype(jnp.int32)
    return lax.map(pick_rows, jnp.arange(EXPERTS, dtype=jnp.int32))

def contract_first(left, right):
    return lax.dot_general(left, right, (((0,), (0,)), ((), ())), preferred_element_type=jnp.float32)

def contract_last(left, right):
    return lax.dot_general(left, right, (((1,), (1,)), ((), ())), preferred_element_type=jnp.float32)

def moe_forward(layer_in, ids_now, router_w, gate_w, up_w, down_w):
    hidden_f, inv_rms, normed = normalize(layer_in)
    one_hot, chosen, probs = gate_probs(normed, ids_now, router_w)
    row_total = ids_now.shape[0] * TOPK
    row_lists = expert_lists(ids_now.reshape(-1))

    def one_expert(operands):
        picked, gate_e, up_e, down_e = operands
        tile_in = normed[jnp.minimum(picked, row_total - 1) // TOPK]
        gate_act = jnp.dot(tile_in, gate_e, preferred_element_type=jnp.float32)
        up_act = jnp.dot(tile_in, up_e, preferred_element_type=jnp.float32)
        hidden_act = (gate_act * jax.nn.sigmoid(gate_act) * up_act).astype(jnp.bfloat16)
        return jnp.dot(hidden_act, down_e, preferred_element_type=jnp.float32).astype(jnp.bfloat16)
    results = lax.map(one_expert, (row_lists, gate_w, up_w, down_w))
    expert_out = jnp.zeros((row_total, D), jnp.bfloat16).at[row_lists.reshape(-1)].set(results.reshape(-1, D), mode='drop')
    expert_out = expert_out.reshape(-1, TOPK, D)
    layer_out = (hidden_f + lax.optimization_barrier(jnp.sum(probs[:, :, None] * expert_out.astype(jnp.float32), axis=1))).astype(jnp.bfloat16)
    return (layer_out, expert_out)

def moe_backward(grad_out, layer_in, expert_out, ids_now, router_w, gate_w, up_w, down_w):
    hidden_f, inv_rms, normed = normalize(layer_in)
    one_hot, chosen, probs = gate_probs(normed, ids_now, router_w)
    grad_f = grad_out.astype(jnp.float32)
    grad_prob = lax.optimization_barrier(jnp.sum(grad_f[:, None, :] * expert_out.astype(jnp.float32), axis=-1))
    grad_rows = (probs[:, :, None] * grad_f[:, None, :]).astype(jnp.bfloat16).reshape(-1, D)
    row_total = grad_rows.shape[0]
    row_lists = expert_lists(ids_now.reshape(-1))

    def one_expert(operands):
        picked, gate_e, up_e, down_e = operands
        is_valid = (picked < row_total)[:, None]
        safe_rows = jnp.minimum(picked, row_total - 1)
        tile_in = jnp.where(is_valid, normed[safe_rows // TOPK], jnp.zeros((), jnp.bfloat16))
        tile_grad = jnp.where(is_valid, grad_rows[safe_rows], jnp.zeros((), jnp.bfloat16))
        gate_act = jnp.dot(tile_in, gate_e, preferred_element_type=jnp.float32)
        up_act = jnp.dot(tile_in, up_e, preferred_element_type=jnp.float32)
        sigmoid_gate = jax.nn.sigmoid(gate_act)
        silu_gate = gate_act * sigmoid_gate
        hidden_act = (silu_gate * up_act).astype(jnp.bfloat16)
        grad_down_e = contract_first(hidden_act, tile_grad)
        grad_hidden = contract_last(tile_grad, down_e)
        grad_gate_act = (grad_hidden * up_act * sigmoid_gate * (1.0 + gate_act * (1.0 - sigmoid_gate))).astype(jnp.bfloat16)
        grad_up_act = (grad_hidden * silu_gate).astype(jnp.bfloat16)
        grad_gate_e = contract_first(tile_in, grad_gate_act)
        grad_up_e = contract_first(tile_in, grad_up_act)
        grad_in_rows = (contract_last(grad_gate_act, gate_e) + contract_last(grad_up_act, up_e)).astype(jnp.bfloat16)
        return (grad_gate_e, grad_up_e, grad_down_e, grad_in_rows)
    grad_gate, grad_up, grad_down, grad_in_rows = lax.map(one_expert, (row_lists, gate_w, up_w, down_w))
    grad_parts = jnp.zeros((row_total, D), jnp.bfloat16).at[row_lists.reshape(-1)].set(grad_in_rows.reshape(-1, D), mode='drop')
    grad_parts = grad_parts.reshape(-1, TOPK, D)
    scaled = chosen / soft_cap
    grad_chosen = probs * (grad_prob - lax.optimization_barrier(jnp.sum(probs * grad_prob, axis=-1, keepdims=True))) * (1.0 - scaled * scaled)
    grad_route = lax.optimization_barrier(jnp.sum(grad_chosen[:, :, None] * one_hot, axis=1)).astype(jnp.bfloat16)
    grad_router = contract_first(normed, grad_route)
    grad_normed = lax.optimization_barrier(jnp.sum(grad_parts.astype(jnp.float32), axis=1)) + contract_last(grad_route, router_w)
    normed_f = hidden_f * inv_rms
    grad_in = (grad_f + inv_rms * (grad_normed - normed_f * lax.optimization_barrier(jnp.mean(grad_normed * normed_f, axis=-1, keepdims=True)))).astype(jnp.bfloat16)
    return (grad_in, grad_router, grad_gate, grad_up, grad_down)

def reference(tokens, expert_ids, labels, router, class_head, w_gate, w_up, w_down):
    section_inputs = []
    section_outputs = []
    finals = []
    for micro_num in range(MB):
        layer_in = tokens[micro_num]
        saved_in = []
        saved_out = []
        for section_num in range(N_SECTION):
            saved_in.append(layer_in)
            layer_in, expert_out = moe_forward(layer_in, expert_ids[section_num, micro_num], router[section_num], w_gate[section_num], w_up[section_num], w_down[section_num])
            saved_out.append(expert_out)
        section_inputs.append(saved_in)
        section_outputs.append(saved_out)
        finals.append(layer_in)
    final_rows = jnp.stack(finals).reshape(-1, D)
    class_logits = capped(jnp.dot(final_rows, class_head, preferred_element_type=jnp.float32))
    class_weights = jnp.exp(class_logits)
    class_total = lax.optimization_barrier(jnp.sum(class_weights, axis=-1, keepdims=True))
    label_hot = (labels.reshape(-1)[:, None] == jnp.arange(NCLASS, dtype=jnp.int32)[None, :]).astype(jnp.float32)
    mean_loss = jnp.mean(jnp.log(class_total[:, 0]) - lax.optimization_barrier(jnp.sum(label_hot * class_logits, axis=-1)))
    scaled = class_logits / soft_cap
    grad_logits = ((class_weights / class_total - label_hot) * (1.0 - scaled * scaled)).astype(jnp.bfloat16)
    grad_head = contract_first(final_rows, grad_logits)
    grad_top = contract_last(grad_logits, class_head).astype(jnp.bfloat16).reshape(MB, -1, D)
    grad_list = [grad_top[micro_num] for micro_num in range(MB)]
    router_list = []
    gate_list = []
    up_list = []
    down_list = []
    for section_num in reversed(range(N_SECTION)):
        router_sum = jnp.zeros((D, EXPERTS), jnp.float32)
        gate_sum = jnp.zeros((EXPERTS, D, FFE), jnp.float32)
        up_sum = jnp.zeros((EXPERTS, D, FFE), jnp.float32)
        down_sum = jnp.zeros((EXPERTS, FFE, D), jnp.float32)
        for micro_num in range(MB):
            grad_cur, grad_r, grad_g, grad_u, grad_d = moe_backward(grad_list[micro_num], section_inputs[micro_num][section_num], section_outputs[micro_num][section_num], expert_ids[section_num, micro_num], router[section_num], w_gate[section_num], w_up[section_num], w_down[section_num])
            grad_list[micro_num] = grad_cur
            router_sum = router_sum + grad_r
            gate_sum = gate_sum + grad_g
            up_sum = up_sum + grad_u
            down_sum = down_sum + grad_d
        router_list.append(router_sum)
        gate_list.append(gate_sum.astype(jnp.bfloat16))
        up_list.append(up_sum.astype(jnp.bfloat16))
        down_list.append(down_sum.astype(jnp.bfloat16))
    grad_router = jnp.stack(router_list[::-1])
    grad_gate = jnp.stack(gate_list[::-1])
    grad_up = jnp.stack(up_list[::-1])
    grad_down = jnp.stack(down_list[::-1])
    return (mean_loss, grad_head, grad_router, grad_gate, grad_up, grad_down)
```

```python
import functools

import jax
import jax.numpy as jnp
from jax import lax
from jax.experimental import pallas as pl
from jax.experimental.pallas import tpu as pltpu
from jax.sharding import PartitionSpec as P

soft_cap = 30.0
norm_eps = 1e-06
lanes = 128
row_step = 16
MESH = pl.DeviceIdType.MESH
group = ("expert", "dp")
dma = pltpu.SemaphoreType.DMA
bf16 = jnp.bfloat16
f32 = jnp.float32


def capped(values):
    return soft_cap * jnp.tanh(values / soft_cap)


def dot_plain(left, right):
    return jnp.dot(left, right, preferred_element_type=f32)


def contract_first(left, right):
    return lax.dot_general(left, right, (((0,), (0,)), ((), ())), preferred_element_type=f32)


def contract_last(left, right):
    return lax.dot_general(left, right, (((1,), (1,)), ((), ())), preferred_element_type=f32)


def partner(e, k, count):
    total, bit = 0, 1
    while bit < count:
        a, b = (e // bit) % 2, (k // bit) % 2
        total = total + (a + b - 2 * a * b) * bit
        bit *= 2
    return total


class Exchange:
    def __init__(self, sizes, own, gath, parts, stage, sums, back, sems):
        self.sizes, self.own, self.gath = sizes, own, gath
        self.parts, self.stage, self.sums, self.back = parts, stage, sums, back
        (self.x_send, self.x_recv, self.d_send, self.d_recv, self.f_send, self.f_recv,
         self.p_send, self.p_recv, self.r_send, self.r_recv) = sems
        self.e, self.d = lax.axis_index("expert"), lax.axis_index("dp")
        self.me = self.e * 2 + self.d

    def chip(self, k):
        return partner(self.e, k, self.sizes[1])

    def across(self, m, k):
        slot = m % 2
        return pltpu.make_async_remote_copy(
            src_ref=self.own.at[m], dst_ref=self.gath.at[slot, self.me],
            send_sem=self.x_send.at[slot, k - 1], recv_sem=self.x_recv.at[slot, k - 1],
            device_id={"expert": self.chip(k)}, device_id_type=MESH)

    def beside(self, m):
        slot = m % 2
        return pltpu.make_async_remote_copy(
            src_ref=self.own.at[m], dst_ref=self.gath.at[slot, self.me],
            send_sem=self.d_send.at[slot], recv_sem=self.d_recv.at[slot],
            device_id={"dp": 1 - self.d}, device_id_type=MESH)

    def onward(self, m, k):
        slot = m % 2
        block = self.chip(k) * 2 + self.d
        return pltpu.make_async_remote_copy(
            src_ref=self.gath.at[slot, block], dst_ref=self.gath.at[slot, block],
            send_sem=self.f_send.at[slot, k - 1], recv_sem=self.f_recv.at[slot, k - 1],
            device_id={"dp": 1 - self.d}, device_id_type=MESH)

    def share(self, m, k):
        slot = m % 2
        return pltpu.make_async_remote_copy(
            src_ref=self.parts.at[slot, k, 1 - self.d], dst_ref=self.stage.at[slot, k],
            send_sem=self.p_send.at[slot, k], recv_sem=self.p_recv.at[slot, k],
            device_id={"dp": 1 - self.d}, device_id_type=MESH)

    def give(self, m, k):
        slot = m % 2
        return pltpu.make_async_remote_copy(
            src_ref=self.sums.at[slot, k - 1], dst_ref=self.back.at[slot, k - 1],
            send_sem=self.r_send.at[slot, k - 1], recv_sem=self.r_recv.at[slot, k - 1],
            device_id={"expert": self.chip(k)}, device_id_type=MESH)

    def spread(self, m):
        for k in range(1, self.sizes[1]):
            self.across(m, k).start()
        self.beside(m).start()
        self.gath[m % 2, self.me] = self.own[m]

    def arrive(self, m, k):
        @pl.when(k == 0)
        def _():
            self.beside(m).wait_recv()

        def pass_on(j):
            self.across(m, j).wait_recv()
            self.onward(m, j).start()

        @pl.when(k == 1)
        def _():
            pass_on(k)

        @pl.when((k >= 1) & (k + 1 < self.sizes[1]))
        def _():
            pass_on(k + 1)

        @pl.when(k >= 1)
        def _():
            self.onward(m, k).wait_recv()

    def settle(self, m, k, keep_own):
        slot = m % 2
        rows = self.own.shape[1]
        self.share(m, k).wait_recv()

        @pl.when(k == 0)
        def _():
            def step(r, _):
                at = pl.ds(r * row_step, row_step)
                keep_own(at, self.parts[slot, k, self.d, at].astype(f32) + self.stage[slot, k, at].astype(f32))
                return 0
            lax.fori_loop(0, rows // row_step, step, 0)

        @pl.when(k >= 1)
        def _():
            def step(r, _):
                at = pl.ds(r * row_step, row_step)
                self.sums[slot, k - 1, at] = (
                    self.parts[slot, k, self.d, at].astype(f32) + self.stage[slot, k, at].astype(f32)
                ).astype(bf16)
                return 0
            lax.fori_loop(0, rows // row_step, step, 0)
            self.onward(m, k).wait_send()
            self.give(m, k).start()

    def passed_on(self, m):
        for k in range(1, self.sizes[1]):
            self.onward(m, k).wait_send()

    def gathered(self, m):
        self.beside(m).wait_send()
        for k in range(1, self.sizes[1]):
            self.across(m, k).wait_send()

    def returned(self, m):
        for k in range(self.sizes[1]):
            self.share(m, k).wait_send()
        for k in range(1, self.sizes[1]):
            self.give(m, k).wait_send()


def meet(sizes, step, everyone):
    sections, experts, cores = sizes
    s, e, d = lax.axis_index("section"), lax.axis_index("expert"), lax.axis_index("dp")
    me = e * cores + d
    first, last = (0, sections - 1) if step > 0 else (sections - 1, 0)
    barrier = pltpu.get_barrier_semaphore()
    if everyone:
        count = experts * cores - 1
        for off in range(1, experts * cores):
            other = lax.rem(me + off, experts * cores)
            pl.semaphore_signal(
                barrier, inc=1, device_id={"expert": other // cores, "dp": lax.rem(other, cores)},
                device_id_type=MESH)
    else:
        count = experts
        for k in range(1, experts):
            pl.semaphore_signal(barrier, inc=1, device_id={"expert": partner(e, k, experts)}, device_id_type=MESH)
        pl.semaphore_signal(barrier, inc=1, device_id={"dp": 1 - d}, device_id_type=MESH)

    @pl.when(s != first)
    def _():
        pl.semaphore_signal(barrier, inc=1, device_id={"section": s - step}, device_id_type=MESH)

    pl.semaphore_wait(barrier, count + (s != last).astype(jnp.int32))


def forward_kernel(sizes, tokens, mask, gate, up, down, router, head, hot,
                   normed_o, hid_o, dgate_o, dup_o, fac_o, own, mix, slope_o, top_o, head_o,
                   gate_v, up_v, down_v, mask_all, gath, parts, stage, sums, back, out_rows,
                   normed_t, hid_t, dgate_t, dup_t, fac_t, slope_t,
                   w_sem, k_send, k_recv, t_sem, z_send, z_recv, o_sem, *sems):
    sections, experts, cores = sizes
    units, rows, width = own.shape
    hidden_dim = gate_v.shape[1]
    s = lax.axis_index("section")
    last = sections - 1
    ex = Exchange(sizes, own, gath, parts, stage, sums, back, sems)
    e, d, me = ex.e, ex.d, ex.me
    members = experts * cores
    chunk = cores * rows

    loads = [pltpu.make_async_copy(a, b, w_sem.at[n])
             for n, (a, b) in enumerate(((gate, gate_v), (up, up_v), (down, down_v)))]
    for load in loads:
        load.start()

    def take(m):
        return pltpu.make_async_copy(tokens.at[m], own.at[m], t_sem.at[m])

    @pl.when(s == 0)
    def _():
        for m in range(units):
            take(m).start()

    meet(sizes, 1, True)

    def tell(off):
        other = lax.rem(me + off, members)
        return pltpu.make_async_remote_copy(
            src_ref=mask, dst_ref=mask_all.at[me], send_sem=k_send.at[off - 1], recv_sem=k_recv.at[off - 1],
            device_id={"expert": other // cores, "dp": lax.rem(other, cores)}, device_id_type=MESH)

    def shift(m):
        return pltpu.make_async_remote_copy(
            src_ref=out_rows.at[m], dst_ref=own.at[m], send_sem=z_send.at[m], recv_sem=z_recv.at[m],
            device_id={"section": lax.rem(s + 1, sections)}, device_id_type=MESH)

    def begin(m):
        @pl.when(s == 0)
        def _():
            take(m).wait()

        @pl.when(s != 0)
        def _():
            shift(m).wait_recv()

        ex.spread(m)

    def writes(m, k, side):
        q = ex.chip(k)
        pairs = ((normed_t, normed_o), (hid_t, hid_o), (dgate_t, dgate_o), (dup_t, dup_o), (fac_t, fac_o))
        return [pltpu.make_async_copy(a.at[side], b.at[m, q], o_sem.at[n, side])
                for n, (a, b) in enumerate(pairs)]

    lane = lax.broadcasted_iota(jnp.int32, (chunk, lanes), 1)

    def compute(m, k):
        slot = m % 2
        q = ex.chip(k)
        turn = m * experts + k
        side = turn % 2

        @pl.when(turn >= 2)
        def _():
            for copy in writes(m, k, side):
                copy.wait()

        for c in range(cores):
            def norm(r, _):
                at = pl.ds(pl.multiple_of(r * row_step, row_step), row_step)
                values = gath[slot, q * cores + c, at].astype(f32)
                inv = lax.rsqrt(jnp.mean(values * values, axis=-1, keepdims=True) + norm_eps)
                normed_t[side, pl.ds(pl.multiple_of(c * rows + r * row_step, row_step), row_step)] = (
                    values * inv).astype(bf16)
                return 0
            lax.fori_loop(0, rows // row_step, norm, 0)
        chosen = capped(dot_plain(normed_t[side], router[...]))
        named = mask_all[pl.ds(q * cores, cores), m].reshape(chunk, lanes).astype(f32)
        weights = jnp.exp(chosen) * named
        probs = weights / jnp.sum(weights, axis=-1, keepdims=True)
        scaled = chosen / soft_cap
        bend = 1.0 - scaled * scaled
        mine = jnp.sum(jnp.where(lane == me, probs, 0.0), axis=-1, keepdims=True)
        fac_t[side] = jnp.broadcast_to(
            jnp.sum(jnp.where(lane == me, bend, 0.0), axis=-1, keepdims=True), (chunk, lanes))

        @pl.when(k == 0)
        def _():
            slope_t[...] = (probs * bend).reshape(cores, rows, lanes)
            slope_o[m] = slope_t[d]

        wide = 256 if hidden_dim % 256 == 0 else hidden_dim
        for j in range(0, hidden_dim, wide):
            cols = slice(j, j + wide)
            gate_act = dot_plain(normed_t[side], gate_v[:, cols])
            up_act = dot_plain(normed_t[side], up_v[:, cols])
            sig = jax.nn.sigmoid(gate_act)
            silu = mine * (gate_act * sig)
            hid_t[side, :, cols] = (silu * up_act).astype(bf16)
            dgate_t[side, :, cols] = (mine * up_act * sig * (1.0 + gate_act * (1.0 - sig))).astype(bf16)
            dup_t[side, :, cols] = silu.astype(bf16)
        wide = 512 if width % 512 == 0 else width
        for j in range(0, width, wide):
            cols = slice(j, j + wide)
            part = dot_plain(hid_t[side], down_v[:, cols]).astype(bf16)
            parts[slot, k, :, :, cols] = part.reshape(cores, rows, wide)
        ex.share(m, k).start()
        for copy in writes(m, k, side):
            copy.start()

    def keep(m):
        def put(at, values):
            mix[m, at] = values
        return put

    mask_all[me] = mask[...]
    for off in range(1, members):
        tell(off).start()
    begin(0)
    for load in loads:
        load.wait()
    for off in range(1, members):
        tell(off).wait()

    def unit(m, _):
        slot = m % 2

        def part(k, _):
            ex.arrive(m, k)

            @pl.when(k >= 1)
            def _():
                ex.settle(m, k - 1, keep(m))

            compute(m, k)
            return 0

        lax.fori_loop(0, experts, part, 0)
        ex.settle(m, experts - 1, keep(m))

        @pl.when(m + 1 < units)
        def _():
            begin(m + 1)

        for k in range(1, experts):
            ex.give(m, k).wait_recv()

        def total(r, _):
            at = pl.ds(pl.multiple_of(r * row_step, row_step), row_step)
            value = mix[m, at]
            for k in range(1, experts):
                value = value + back[slot, k - 1, at].astype(f32)
            mix[m, at] = value
            out_rows[m, at] = (own[m, at].astype(f32) + value).astype(bf16)
            return 0
        lax.fori_loop(0, rows // row_step, total, 0)

        @pl.when(s != last)
        def _():
            shift(m).start()

        ex.gathered(m)
        ex.returned(m)
        return 0

    lax.fori_loop(0, units, unit, 0)

    @pl.when(s != last)
    def _():
        head_o[...] = jnp.zeros_like(head_o)
        for m in range(units):
            shift(m).wait_send()

    @pl.when(s == last)
    def _():
        final = out_rows[...].reshape(units * rows, width)
        class_logits = capped(dot_plain(final, head[...]))
        class_weights = jnp.exp(class_logits)
        class_total = jnp.sum(class_weights, axis=-1, keepdims=True)
        label_hot = hot[...]
        loss = jnp.log(class_total) - jnp.sum(label_hot * class_logits, axis=-1, keepdims=True)
        scaled = class_logits / soft_cap
        grad_logits = ((class_weights / class_total - label_hot) * (1.0 - scaled * scaled)).astype(bf16)
        top_o[...] = contract_last(grad_logits, head[...]).astype(bf16).reshape(units, rows, width)
        head_o[pl.ds(0, width)] = contract_first(final, grad_logits)
        head_o[pl.ds(width, 8)] = jnp.full((8, head_o.shape[1]), jnp.sum(loss), f32)

    for back_by in (2, 1):
        turn = units * experts - back_by
        for copy in writes(turn // experts, turn % experts, turn % 2):
            copy.wait()


def exchange_scratch(experts, cores, rows, width):
    return [
        pltpu.VMEM((2, experts * cores, rows, width), bf16),
        pltpu.VMEM((2, experts, cores, rows, width), bf16),
        pltpu.VMEM((2, experts, rows, width), bf16),
        pltpu.VMEM((2, experts - 1, rows, width), bf16),
        pltpu.VMEM((2, experts - 1, rows, width), bf16),
    ], [
        dma((2, experts - 1)), dma((2, experts - 1)), dma((2,)), dma((2,)),
        dma((2, experts - 1)), dma((2, experts - 1)), dma((2, experts)), dma((2, experts)),
        dma((2, experts - 1)), dma((2, experts - 1)),
    ]


def forward(sizes, tokens, mask, gate_w, up_w, down_w, router_p, head, hot):
    sections, experts, cores = sizes
    units, rows, width = tokens.shape
    hidden_dim = gate_w.shape[1]
    members, chunk = experts * cores, cores * rows
    vmem, hbm = pl.BlockSpec(memory_space=pltpu.VMEM), pl.BlockSpec(memory_space=pl.ANY)
    buffers, sems = exchange_scratch(experts, cores, rows, width)

    def shaped(shape, dtype):
        return jax.ShapeDtypeStruct(shape, dtype)

    acts = (units, experts, chunk, hidden_dim)
    return pl.pallas_call(
        functools.partial(forward_kernel, sizes),
        out_shape=(
            shaped((units, experts, chunk, width), bf16), shaped(acts, bf16), shaped(acts, bf16),
            shaped(acts, bf16), shaped((units, experts, chunk, lanes), f32),
            shaped((units, rows, width), bf16), shaped((units, rows, width), f32),
            shaped((units, rows, lanes), f32), shaped((units, rows, width), bf16),
            shaped((width + 8, head.shape[1]), f32),
        ),
        in_specs=[hbm, vmem, hbm, hbm, hbm, vmem, vmem, vmem],
        out_specs=(hbm,) * 5 + (vmem,) * 5,
        scratch_shapes=[
            pltpu.VMEM(gate_w.shape, bf16), pltpu.VMEM(up_w.shape, bf16), pltpu.VMEM(down_w.shape, bf16),
            pltpu.VMEM((members, units, rows, lanes), bf16),
            *buffers,
            pltpu.VMEM((units, rows, width), bf16),
            pltpu.VMEM((2, chunk, width), bf16), pltpu.VMEM((2, chunk, hidden_dim), bf16),
            pltpu.VMEM((2, chunk, hidden_dim), bf16), pltpu.VMEM((2, chunk, hidden_dim), bf16),
            pltpu.VMEM((2, chunk, lanes), f32), pltpu.VMEM((cores, rows, lanes), f32),
            dma((3,)), dma((members - 1,)), dma((members - 1,)), dma((units,)),
            dma((units,)), dma((units,)), dma((5, 2)),
            *sems,
        ],
        cost_estimate=pl.CostEstimate(
            flops=6 * units * members * rows * width * hidden_dim, bytes_accessed=500_000_000, transcendentals=0),
        compiler_params=pltpu.CompilerParams(
            collective_id=0, has_side_effects=True, vmem_limit_bytes=56 * 1024 * 1024),
    )(tokens, mask, gate_w, up_w, down_w, router_p, head, hot)


def backward_kernel(sizes, top, hid, dgate, dup, fac, own_in, mix, slope, gate, up, down, router, my_row,
                    grad_o, agate_o, aup_o, route_o, common_o,
                    gate_v, up_v, down_v, hid_v, dgate_v, dup_v, fac_v, own,
                    gath, parts, stage, sums, back, out_rows, total_v,
                    agate_t, aup_t, route_t,
                    w_sem, t_sem, z_send, z_recv, o_sem, *sems):
    sections, experts, cores = sizes
    units, rows, width = own.shape
    hidden_dim = gate_v.shape[1]
    s = lax.axis_index("section")
    last = sections - 1
    ex = Exchange(sizes, own, gath, parts, stage, sums, back, sems)
    e, d, me = ex.e, ex.d, ex.me
    chunk = cores * rows

    loads = [pltpu.make_async_copy(a, b, w_sem.at[n]) for n, (a, b) in enumerate((
        (down, down_v), (hid, hid_v), (dgate, dgate_v), (dup, dup_v), (fac, fac_v), (gate, gate_v), (up, up_v)))]
    for load in loads:
        load.start()

    def take(m):
        return pltpu.make_async_copy(top.at[m], own.at[m], t_sem.at[m])

    @pl.when(s == last)
    def _():
        for m in range(units):
            take(m).start()

    meet(sizes, -1, False)

    def shift(m):
        return pltpu.make_async_remote_copy(
            src_ref=out_rows.at[m], dst_ref=own.at[m], send_sem=z_send.at[m], recv_sem=z_recv.at[m],
            device_id={"section": lax.rem(s + sections - 1, sections)}, device_id_type=MESH)

    def begin(m):
        @pl.when(s == last)
        def _():
            take(m).wait()

        @pl.when(s != last)
        def _():
            shift(m).wait_recv()

        ex.spread(m)

    def writes(m, k, side):
        q = ex.chip(k)
        pairs = ((agate_t, agate_o), (aup_t, aup_o), (route_t, route_o))
        return [pltpu.make_async_copy(a.at[side], b.at[m, q], o_sem.at[n, side])
                for n, (a, b) in enumerate(pairs)]

    def keep_grad(m, k):
        q = ex.chip(k)
        return pltpu.make_async_copy(
            gath.at[m % 2, pl.ds(q * cores, cores)], grad_o.at[m, pl.ds(q * cores, cores)], o_sem.at[3, k % 2])

    lane = lax.broadcasted_iota(jnp.int32, (chunk, lanes), 1)

    def compute(m, k):
        slot = m % 2
        q = ex.chip(k)
        turn = m * experts + k
        side = turn % 2
        keep_grad(m, k).start()

        @pl.when(turn >= 2)
        def _():
            for copy in writes(m, k, side):
                copy.wait()

        grads = gath[slot, pl.ds(q * cores, cores)].reshape(chunk, width)
        gain = jnp.zeros((chunk, 1), f32)
        wide = 256 if hidden_dim % 256 == 0 else hidden_dim
        for j in range(0, hidden_dim, wide):
            cols = slice(j, j + wide)
            down_grad = contract_last(grads, down_v[cols, :])
            agate_t[side, :, cols] = (down_grad * dgate_v[m, q, :, cols].astype(f32)).astype(bf16)
            aup_t[side, :, cols] = (down_grad * dup_v[m, q, :, cols].astype(f32)).astype(bf16)
            gain = gain + jnp.sum(down_grad * hid_v[m, q, :, cols].astype(f32), axis=-1, keepdims=True)
        route = jnp.where(lane == me, gain * fac_v[m, q], 0.0).astype(bf16)
        route_t[side] = route

        @pl.when(s != 0)
        def _():
            through = jnp.sum(route.astype(f32), axis=-1, keepdims=True)
            wide = 512 if width % 512 == 0 else width
            for j in range(0, width, wide):
                cols = slice(j, j + wide)
                part = (contract_last(agate_t[side], gate_v[cols, :])
                        + contract_last(aup_t[side], up_v[cols, :])
                        + through * my_row[:, cols])
                parts[slot, k, :, :, cols] = part.astype(bf16).reshape(cores, rows, wide)
            ex.share(m, k).start()

        for copy in writes(m, k, side):
            copy.start()
        keep_grad(m, k).wait()

    def keep(at, values):
        total_v[at] = values

    begin(0)
    for load in loads:
        load.wait()

    def unit(m, _):
        slot = m % 2

        def part(k, _):
            ex.arrive(m, k)

            @pl.when((k >= 1) & (s != 0))
            def _():
                ex.settle(m, k - 1, keep)

            compute(m, k)
            return 0

        lax.fori_loop(0, experts, part, 0)

        @pl.when(s != 0)
        def _():
            ex.settle(m, experts - 1, keep)

        @pl.when(s == 0)
        def _():
            ex.passed_on(m)

        @pl.when(m + 1 < units)
        def _():
            begin(m + 1)

        def weigh(r, _):
            at = pl.ds(pl.multiple_of(r * row_step, row_step), row_step)
            shared = jnp.sum(own[m, at].astype(f32) * mix[m, at], axis=-1, keepdims=True)
            common_o[m, at] = (slope[m, at] * shared).astype(bf16)
            return 0
        lax.fori_loop(0, rows // row_step, weigh, 0)

        @pl.when(s != 0)
        def _():
            for k in range(1, experts):
                ex.give(m, k).wait_recv()

            def total(r, _):
                at = pl.ds(pl.multiple_of(r * row_step, row_step), row_step)
                grad_normed = total_v[at]
                for k in range(1, experts):
                    grad_normed = grad_normed + back[slot, k - 1, at].astype(f32)
                grad_normed = grad_normed - contract_last(common_o[m, at], router[...])
                hidden_f = own_in[m, at].astype(f32)
                inv_rms = lax.rsqrt(jnp.mean(hidden_f * hidden_f, axis=-1, keepdims=True) + norm_eps)
                normed_f = hidden_f * inv_rms
                out_rows[m, at] = (
                    own[m, at].astype(f32)
                    + inv_rms * (grad_normed
                                 - normed_f * jnp.mean(grad_normed * normed_f, axis=-1, keepdims=True))
                ).astype(bf16)
                return 0
            lax.fori_loop(0, rows // row_step, total, 0)
            shift(m).start()
            ex.returned(m)

        ex.gathered(m)
        return 0

    lax.fori_loop(0, units, unit, 0)

    @pl.when(s != 0)
    def _():
        for m in range(units):
            shift(m).wait_send()

    for back_by in (2, 1):
        turn = units * experts - back_by
        for copy in writes(turn // experts, turn % experts, turn % 2):
            copy.wait()


def backward(sizes, top, hid, dgate, dup, fac, own_in, mix, slope, gate_w, up_w, down_w, router_p, my_row):
    sections, experts, cores = sizes
    units, rows, width = top.shape
    hidden_dim = gate_w.shape[1]
    members, chunk = experts * cores, cores * rows
    vmem, hbm = pl.BlockSpec(memory_space=pltpu.VMEM), pl.BlockSpec(memory_space=pl.ANY)
    buffers, sems = exchange_scratch(experts, cores, rows, width)

    def shaped(shape, dtype):
        return jax.ShapeDtypeStruct(shape, dtype)

    acts = (units, experts, chunk, hidden_dim)
    return pl.pallas_call(
        functools.partial(backward_kernel, sizes),
        out_shape=(
            shaped((units, members, rows, width), bf16), shaped(acts, bf16), shaped(acts, bf16),
            shaped((units, experts, chunk, lanes), bf16), shaped((units, rows, lanes), bf16),
        ),
        in_specs=[hbm] * 5 + [vmem] * 3 + [hbm] * 3 + [vmem] * 2,
        out_specs=(hbm,) * 4 + (vmem,),
        scratch_shapes=[
            pltpu.VMEM(gate_w.shape, bf16), pltpu.VMEM(up_w.shape, bf16), pltpu.VMEM(down_w.shape, bf16),
            pltpu.VMEM(acts, bf16), pltpu.VMEM(acts, bf16), pltpu.VMEM(acts, bf16),
            pltpu.VMEM(fac.shape, f32), pltpu.VMEM((units, rows, width), bf16),
            *buffers,
            pltpu.VMEM((units, rows, width), bf16), pltpu.VMEM((rows, width), f32),
            pltpu.VMEM((2, chunk, hidden_dim), bf16), pltpu.VMEM((2, chunk, hidden_dim), bf16),
            pltpu.VMEM((2, chunk, lanes), bf16),
            dma((7,)), dma((units,)), dma((units,)), dma((units,)), dma((4, 2)),
            *sems,
        ],
        cost_estimate=pl.CostEstimate(
            flops=6 * units * members * rows * width * hidden_dim, bytes_accessed=500_000_000, transcendentals=0),
        compiler_params=pltpu.CompilerParams(
            collective_id=1, has_side_effects=True, vmem_limit_bytes=56 * 1024 * 1024),
    )(top, hid, dgate, dup, fac, own_in, mix, slope, gate_w, up_w, down_w, router_p, my_row)


def give_back_kernel(sizes, parts_ref, out_ref, stage_ref, sum_ref, d_send, d_recv, x_send, x_recv):
    sections, experts, cores = sizes
    e, d = lax.axis_index("expert"), lax.axis_index("dp")

    barrier = pltpu.get_barrier_semaphore()
    for off in range(1, experts):
        pl.semaphore_signal(barrier, inc=1, device_id={"expert": lax.rem(e + off, experts)}, device_id_type=MESH)
    for off in range(1, cores):
        pl.semaphore_signal(barrier, inc=1, device_id={"dp": lax.rem(d + off, cores)}, device_id_type=MESH)
    pl.semaphore_wait(barrier, experts + cores - 2)

    def beside(off, core_off):
        to_d = lax.rem(d + core_off, cores)
        return pltpu.make_async_remote_copy(
            src_ref=parts_ref.at[lax.rem(e + off, experts) * cores + to_d],
            dst_ref=stage_ref.at[core_off - 1, off],
            send_sem=d_send.at[core_off - 1, off], recv_sem=d_recv.at[core_off - 1, off],
            device_id={"dp": to_d}, device_id_type=MESH)

    def across(off):
        return pltpu.make_async_remote_copy(
            src_ref=sum_ref.at[off - 1], dst_ref=out_ref.at[e],
            send_sem=x_send.at[off - 1], recv_sem=x_recv.at[off - 1],
            device_id={"expert": lax.rem(e + off, experts)}, device_id_type=MESH)

    order = [off for off in range(experts - 1, 0, -1)] + [0]
    for off in order:
        for core_off in range(1, cores):
            beside(off, core_off).start()
    for n, off in enumerate(order):
        total = parts_ref[lax.rem(e + off, experts) * cores + d].astype(jnp.float32)
        for core_off in range(1, cores):
            beside(off, core_off).wait_recv()
            total = total + stage_ref[core_off - 1, off].astype(jnp.float32)
        if off == 0:
            out_ref[e] = total.astype(out_ref.dtype)
        else:
            sum_ref[off - 1] = total.astype(out_ref.dtype)
        if n > 0:
            across(order[n - 1]).start()
    for off in range(1, experts):
        across(off).wait()
    for off in order:
        for core_off in range(1, cores):
            beside(off, core_off).wait_send()


def give_back(sizes, parts, call_id):
    sections, experts, cores = sizes
    block = parts.shape[1:]
    return pl.pallas_call(
        functools.partial(give_back_kernel, sizes),
        out_shape=jax.ShapeDtypeStruct((experts,) + block, parts.dtype),
        in_specs=[pl.BlockSpec(memory_space=pltpu.VMEM)],
        out_specs=pl.BlockSpec(memory_space=pltpu.VMEM),
        scratch_shapes=[
            pltpu.VMEM((cores - 1, experts) + block, parts.dtype),
            pltpu.VMEM((experts - 1,) + block, parts.dtype),
            dma((cores - 1, experts)), dma((cores - 1, experts)),
            dma((experts - 1,)), dma((experts - 1,)),
        ],
        cost_estimate=pl.CostEstimate(flops=0, bytes_accessed=30 * parts.size * 2, transcendentals=0),
        compiler_params=pltpu.CompilerParams(collective_id=call_id, has_side_effects=True),
    )(parts)


def shards(sizes, tokens, expert_ids, labels, router, class_head, w_gate, w_up, w_down):
    sections, experts, cores = sizes
    members = experts * cores
    me = lax.axis_index("expert") * cores + lax.axis_index("dp")
    micro_count, tok_rows, width = tokens.shape
    router_w = router[0]
    expert_count = router_w.shape[1]
    gate_w, up_w, down_w = w_gate[0, 0], w_up[0, 0], w_down[0, 0]
    hidden_dim = gate_w.shape[1]
    rows = max(row_step, min(tok_rows, tok_rows * 8 // members))
    units = micro_count * tok_rows // rows

    router_p = jnp.pad(router_w, ((0, 0), (0, lanes - expert_count)))
    picks = expert_ids[0].reshape(units, rows, -1)
    named = jnp.arange(lanes, dtype=jnp.int32)
    mask = jnp.any(picks[:, :, :, None] == named, axis=2).astype(bf16)
    hot = (labels.reshape(-1)[:, None] == jnp.arange(class_head.shape[1], dtype=jnp.int32)[None, :]).astype(f32)
    my_row = lax.dynamic_index_in_dim(router_w.T, me, 0).astype(f32)

    normed, hid, dgate, dup, fac, own_in, mix, slope, top, head_term = forward(
        sizes, tokens.reshape(units, rows, width), mask, gate_w, up_w, down_w, router_p, class_head, hot)
    summed = lax.psum(head_term, ("section",) + group)
    grad_all, agate, aup, route, common = backward(
        sizes, top, hid, dgate, dup, fac, own_in, mix, slope, gate_w, up_w, down_w, router_p, my_row)

    every = units * members * rows
    normed = normed.reshape(every, width)
    grad_gate = contract_first(normed, agate.reshape(every, hidden_dim)).astype(bf16)
    grad_up = contract_first(normed, aup.reshape(every, hidden_dim)).astype(bf16)
    grad_down = contract_first(hid.reshape(every, hidden_dim), grad_all.reshape(every, width)).astype(bf16)

    own_f = own_in.reshape(-1, width).astype(f32)
    inv_rms = lax.rsqrt(jnp.mean(own_f * own_f, axis=-1, keepdims=True) + norm_eps)
    normed_own = (own_f * inv_rms).astype(bf16)
    router_sum = (contract_first(route.reshape(every, lanes), normed)
                  - contract_first(common.reshape(-1, lanes), normed_own))[:expert_count]
    copies = jnp.broadcast_to(router_sum[None], (members,) + router_sum.shape)
    router_out = jnp.sum(give_back(sizes, copies, 3), axis=0).T[None]
    mean_loss = summed[width, 0] / (micro_count * tok_rows * members)
    return (
        mean_loss,
        summed[:width],
        router_out,
        grad_gate[None, None],
        grad_up[None, None],
        grad_down[None, None],
    )


def solution(mesh):
    sizes = tuple(mesh.shape[axis] for axis in ("section", "expert", "dp"))
    return jax.shard_map(
        functools.partial(shards, sizes),
        mesh=mesh,
        in_specs=(
            P(None, ("expert", "dp"), None),
            P("section", None, ("expert", "dp"), None),
            P(None, ("expert", "dp")),
            P("section", None, None),
            P(),
            P("section", ("expert", "dp"), None, None),
            P("section", ("expert", "dp"), None, None),
            P("section", ("expert", "dp"), None, None),
        ),
        out_specs=(
            P(),
            P(),
            P("section", None, None),
            P("section", ("expert", "dp"), None, None),
            P("section", ("expert", "dp"), None, None),
            P("section", ("expert", "dp"), None, None),
        ),
        check_vma=False,
    )
```

```python
import functools

import jax
import jax.numpy as jnp
from jax import lax
from jax.experimental import pallas as pl
from jax.experimental.pallas import tpu as pltpu
from jax.sharding import PartitionSpec as P

soft_cap = 30.0
norm_eps = 1e-06
lanes = 128
row_step = 16
MESH = pl.DeviceIdType.MESH
group = ("expert", "dp")
dma = pltpu.SemaphoreType.DMA
bf16 = jnp.bfloat16
f32 = jnp.float32


def capped(values):
    return soft_cap * jnp.tanh(values / soft_cap)


def dot_plain(left, right):
    return jnp.dot(left, right, preferred_element_type=f32)


def contract_first(left, right):
    return lax.dot_general(left, right, (((0,), (0,)), ((), ())), preferred_element_type=f32)


def contract_last(left, right):
    return lax.dot_general(left, right, (((1,), (1,)), ((), ())), preferred_element_type=f32)


def partner(e, k, count):
    total, bit = 0, 1
    while bit < count:
        a, b = (e // bit) % 2, (k // bit) % 2
        total = total + (a + b - 2 * a * b) * bit
        bit *= 2
    return total


class Exchange:
    def __init__(self, sizes, own, gath, parts, stage, sums, back, sems):
        self.sizes, self.own, self.gath = sizes, own, gath
        self.parts, self.stage, self.sums, self.back = parts, stage, sums, back
        (self.x_send, self.x_recv, self.d_send, self.d_recv, self.f_send, self.f_recv,
         self.p_send, self.p_recv, self.r_send, self.r_recv) = sems
        self.e, self.d = lax.axis_index("expert"), lax.axis_index("dp")
        self.me = self.e * 2 + self.d
        self.slabs, self.wide = parts.shape[1], parts.shape[-1]

    def chip(self, k):
        return partner(self.e, k, self.sizes[1])

    def across(self, m, k):
        slot = m % 2
        return pltpu.make_async_remote_copy(
            src_ref=self.own.at[m], dst_ref=self.gath.at[slot, self.me],
            send_sem=self.x_send.at[slot, k - 1], recv_sem=self.x_recv.at[slot, k - 1],
            device_id={"expert": self.chip(k)}, device_id_type=MESH)

    def beside(self, m):
        slot = m % 2
        return pltpu.make_async_remote_copy(
            src_ref=self.own.at[m], dst_ref=self.gath.at[slot, self.me],
            send_sem=self.d_send.at[slot], recv_sem=self.d_recv.at[slot],
            device_id={"dp": 1 - self.d}, device_id_type=MESH)

    def onward(self, m, k):
        slot = m % 2
        block = self.chip(k) * 2 + self.d
        return pltpu.make_async_remote_copy(
            src_ref=self.gath.at[slot, block], dst_ref=self.gath.at[slot, block],
            send_sem=self.f_send.at[slot, k - 1], recv_sem=self.f_recv.at[slot, k - 1],
            device_id={"dp": 1 - self.d}, device_id_type=MESH)

    def share(self, m, j):
        slot = m % 2
        return pltpu.make_async_remote_copy(
            src_ref=self.parts.at[slot, j, 1 - self.d], dst_ref=self.stage.at[slot, j],
            send_sem=self.p_send.at[slot, j], recv_sem=self.p_recv.at[slot, j],
            device_id={"dp": 1 - self.d}, device_id_type=MESH)

    def give(self, m, j, k):
        slot = m % 2
        return pltpu.make_async_remote_copy(
            src_ref=self.sums.at[slot, j, k - 1], dst_ref=self.back.at[slot, j, k - 1],
            send_sem=self.r_send.at[slot, j, k - 1], recv_sem=self.r_recv.at[slot, j, k - 1],
            device_id={"expert": self.chip(k)}, device_id_type=MESH)

    def spread(self, m):
        for k in range(1, self.sizes[1]):
            self.across(m, k).start()
        self.beside(m).start()
        self.gath[m % 2, self.me] = self.own[m]

    def arrive(self, m, use):
        experts = self.sizes[1]
        use(self.me)
        self.beside(m).wait_recv()
        use(self.e * 2 + 1 - self.d)
        for k in range(1, experts):
            self.across(m, k).wait_recv()
            self.onward(m, k).start()
            use(self.chip(k) * 2 + self.d)
        for k in range(1, experts):
            self.onward(m, k).wait_recv()
            use(self.chip(k) * 2 + 1 - self.d)

    def passed_on(self, m):
        for k in range(1, self.sizes[1]):
            self.onward(m, k).wait_send()

    def settle(self, m, j, keep_own):
        slot = m % 2
        experts = self.sizes[1]
        self.share(m, j).wait_recv()
        for k in range(experts - 1, -1, -1):
            chip = self.chip(k)
            value = self.parts[slot, j, self.d, chip].astype(f32) + self.stage[slot, j, chip].astype(f32)
            if k == 0:
                keep_own(j, value)
            else:
                self.sums[slot, j, k - 1] = value.astype(bf16)
                self.give(m, j, k).start()

    def gathered(self, m):
        self.beside(m).wait_send()
        for k in range(1, self.sizes[1]):
            self.across(m, k).wait_send()

    def given(self, m):
        for j in range(self.slabs):
            for k in range(1, self.sizes[1]):
                self.give(m, j, k).wait_recv()

    def returned(self, m):
        for j in range(self.slabs):
            self.share(m, j).wait_send()
            for k in range(1, self.sizes[1]):
                self.give(m, j, k).wait_send()


def meet(sizes, step, everyone):
    sections, experts, cores = sizes
    s, e, d = lax.axis_index("section"), lax.axis_index("expert"), lax.axis_index("dp")
    me = e * cores + d
    first, last = (0, sections - 1) if step > 0 else (sections - 1, 0)
    barrier = pltpu.get_barrier_semaphore()
    if everyone:
        count = experts * cores - 1
        for off in range(1, experts * cores):
            other = lax.rem(me + off, experts * cores)
            pl.semaphore_signal(
                barrier, inc=1, device_id={"expert": other // cores, "dp": lax.rem(other, cores)},
                device_id_type=MESH)
    else:
        count = experts
        for k in range(1, experts):
            pl.semaphore_signal(barrier, inc=1, device_id={"expert": partner(e, k, experts)}, device_id_type=MESH)
        pl.semaphore_signal(barrier, inc=1, device_id={"dp": 1 - d}, device_id_type=MESH)

    @pl.when(s != first)
    def _():
        pl.semaphore_signal(barrier, inc=1, device_id={"section": s - step}, device_id_type=MESH)

    pl.semaphore_wait(barrier, count + (s != last).astype(jnp.int32))


def forward_kernel(sizes, tokens, mask, gate, up, down, router, head, hot,
                   normed_o, hid_o, dgate_o, dup_o, fac_o, own, mix, slope_o, top_o, head_o,
                   gate_v, up_v, down_v, mask_all, gath, parts, stage, sums, back, out_rows,
                   normed_t, hid_t, dgate_t, dup_t, fac_t, slope_t,
                   w_sem, k_send, k_recv, t_sem, z_send, z_recv, o_sem, *sems):
    sections, experts, cores = sizes
    units, rows, width = own.shape
    hidden_dim = gate_v.shape[1]
    s = lax.axis_index("section")
    last = sections - 1
    ex = Exchange(sizes, own, gath, parts, stage, sums, back, sems)
    e, d, me = ex.e, ex.d, ex.me
    members = experts * cores
    every = members * rows
    slabs, slab = ex.slabs, ex.wide

    loads = [pltpu.make_async_copy(a, b, w_sem.at[n])
             for n, (a, b) in enumerate(((gate, gate_v), (up, up_v), (down, down_v)))]
    for load in loads:
        load.start()

    def take(m):
        return pltpu.make_async_copy(tokens.at[m], own.at[m], t_sem.at[m])

    @pl.when(s == 0)
    def _():
        for m in range(units):
            take(m).start()

    meet(sizes, 1, True)

    def tell(off):
        other = lax.rem(me + off, members)
        return pltpu.make_async_remote_copy(
            src_ref=mask, dst_ref=mask_all.at[me], send_sem=k_send.at[off - 1], recv_sem=k_recv.at[off - 1],
            device_id={"expert": other // cores, "dp": lax.rem(other, cores)}, device_id_type=MESH)

    def shift(m):
        return pltpu.make_async_remote_copy(
            src_ref=out_rows.at[m], dst_ref=own.at[m], send_sem=z_send.at[m], recv_sem=z_recv.at[m],
            device_id={"section": lax.rem(s + 1, sections)}, device_id_type=MESH)

    def begin(m):
        @pl.when(s == 0)
        def _():
            take(m).wait()

        @pl.when(s != 0)
        def _():
            shift(m).wait_recv()

        ex.spread(m)

    def writes(m):
        side = m % 2
        pairs = ((normed_t, normed_o), (hid_t, hid_o), (dgate_t, dgate_o), (dup_t, dup_o), (fac_t, fac_o))
        return [pltpu.make_async_copy(a.at[side], b.at[m], o_sem.at[n, side])
                for n, (a, b) in enumerate(pairs)]

    lane = lax.broadcasted_iota(jnp.int32, (every, lanes), 1)

    def widen(m):
        slot = m % 2

        @pl.when(m >= 2)
        def _():
            for copy in writes(m):
                copy.wait()

        def norm_block(block):
            def norm(r, _):
                at = pl.ds(pl.multiple_of(r * row_step, row_step), row_step)
                values = gath[slot, block, at].astype(f32)
                inv = lax.rsqrt(jnp.mean(values * values, axis=-1, keepdims=True) + norm_eps)
                normed_t[slot, pl.ds(pl.multiple_of(block * rows + r * row_step, row_step), row_step)] = (
                    values * inv).astype(bf16)
                return 0
            lax.fori_loop(0, rows // row_step, norm, 0)

        ex.arrive(m, norm_block)
        chosen = capped(dot_plain(normed_t[slot], router[...]))
        named = mask_all[:, m].reshape(every, lanes).astype(f32)
        weights = jnp.exp(chosen) * named
        probs = weights / jnp.sum(weights, axis=-1, keepdims=True)
        scaled = chosen / soft_cap
        bend = 1.0 - scaled * scaled
        mine = jnp.sum(jnp.where(lane == me, probs, 0.0), axis=-1, keepdims=True)
        fac_t[slot] = jnp.broadcast_to(
            jnp.sum(jnp.where(lane == me, bend, 0.0), axis=-1, keepdims=True), (every, lanes))
        slope_t[...] = (probs * bend).reshape(members, rows, lanes)
        slope_o[m] = slope_t[me]

        wide = 256 if hidden_dim % 256 == 0 else hidden_dim
        for j in range(0, hidden_dim, wide):
            cols = slice(j, j + wide)
            gate_act = dot_plain(normed_t[slot], gate_v[:, cols])
            up_act = dot_plain(normed_t[slot], up_v[:, cols])
            sig = jax.nn.sigmoid(gate_act)
            silu = mine * (gate_act * sig)
            hid_t[slot, :, cols] = (silu * up_act).astype(bf16)
            dgate_t[slot, :, cols] = (mine * up_act * sig * (1.0 + gate_act * (1.0 - sig))).astype(bf16)
            dup_t[slot, :, cols] = silu.astype(bf16)
        for copy in writes(m):
            copy.start()

    def narrow(m):
        slot = m % 2

        def keep(j, value):
            mix[m, :, j * slab:(j + 1) * slab] = value

        tile = 512 if slab % 512 == 0 else slab
        for j in range(slabs):
            for i in range(0, slab, tile):
                part = dot_plain(hid_t[slot], down_v[:, j * slab + i:j * slab + i + tile]).astype(bf16)
                part = part.reshape(experts, cores, rows, tile)
                for c in range(cores):
                    parts[slot, j, c, :, :, i:i + tile] = part[:, c]
            ex.share(m, j).start()
        for j in range(slabs):
            ex.settle(m, j, keep)

    def finish(m):
        slot = m % 2
        ex.given(m)

        def total(r, _):
            at = pl.ds(pl.multiple_of(r * row_step, row_step), row_step)
            for j in range(slabs):
                cols = slice(j * slab, (j + 1) * slab)
                value = mix[m, at, cols]
                for k in range(1, experts):
                    value = value + back[slot, j, k - 1, at].astype(f32)
                mix[m, at, cols] = value
                out_rows[m, at, cols] = (own[m, at, cols].astype(f32) + value).astype(bf16)
            return 0
        lax.fori_loop(0, rows // row_step, total, 0)

        @pl.when(s != last)
        def _():
            shift(m).start()

        ex.gathered(m)
        ex.returned(m)

    mask_all[me] = mask[...]
    for off in range(1, members):
        tell(off).start()
    begin(0)
    for off in range(1, members):
        tell(off).wait()
    for load in loads:
        load.wait()

    def unit(m, _):
        widen(m)

        @pl.when(m >= 1)
        def _():
            finish(m - 1)

        ex.passed_on(m)

        @pl.when(m + 1 < units)
        def _():
            begin(m + 1)

        narrow(m)
        return 0

    lax.fori_loop(0, units, unit, 0)
    finish(units - 1)

    @pl.when(s != last)
    def _():
        head_o[...] = jnp.zeros_like(head_o)
        for m in range(units):
            shift(m).wait_send()

    @pl.when(s == last)
    def _():
        final = out_rows[...].reshape(units * rows, width)
        class_logits = capped(dot_plain(final, head[...]))
        class_weights = jnp.exp(class_logits)
        class_total = jnp.sum(class_weights, axis=-1, keepdims=True)
        label_hot = hot[...]
        loss = jnp.log(class_total) - jnp.sum(label_hot * class_logits, axis=-1, keepdims=True)
        scaled = class_logits / soft_cap
        grad_logits = ((class_weights / class_total - label_hot) * (1.0 - scaled * scaled)).astype(bf16)
        top_o[...] = contract_last(grad_logits, head[...]).astype(bf16).reshape(units, rows, width)
        head_o[pl.ds(0, width)] = contract_first(final, grad_logits)
        head_o[pl.ds(width, 8)] = jnp.full((8, head_o.shape[1]), jnp.sum(loss), f32)

    for m in range(max(0, units - 2), units):
        for copy in writes(m):
            copy.wait()


def exchange_scratch(experts, cores, rows, width):
    slabs = 2 if width % 256 == 0 else 1
    slab = width // slabs
    return [
        pltpu.VMEM((2, experts * cores, rows, width), bf16),
        pltpu.VMEM((2, slabs, cores, experts, rows, slab), bf16),
        pltpu.VMEM((2, slabs, experts, rows, slab), bf16),
        pltpu.VMEM((2, slabs, experts - 1, rows, slab), bf16),
        pltpu.VMEM((2, slabs, experts - 1, rows, slab), bf16),
    ], [
        dma((2, experts - 1)), dma((2, experts - 1)), dma((2,)), dma((2,)),
        dma((2, experts - 1)), dma((2, experts - 1)), dma((2, slabs)), dma((2, slabs)),
        dma((2, slabs, experts - 1)), dma((2, slabs, experts - 1)),
    ]


def forward(sizes, tokens, mask, gate_w, up_w, down_w, router_p, head, hot):
    sections, experts, cores = sizes
    units, rows, width = tokens.shape
    hidden_dim = gate_w.shape[1]
    members = experts * cores
    every = members * rows
    vmem, hbm = pl.BlockSpec(memory_space=pltpu.VMEM), pl.BlockSpec(memory_space=pl.ANY)
    buffers, sems = exchange_scratch(experts, cores, rows, width)

    def shaped(shape, dtype):
        return jax.ShapeDtypeStruct(shape, dtype)

    acts = (units, every, hidden_dim)
    return pl.pallas_call(
        functools.partial(forward_kernel, sizes),
        out_shape=(
            shaped((units, every, width), bf16), shaped(acts, bf16), shaped(acts, bf16),
            shaped(acts, bf16), shaped((units, every, lanes), f32),
            shaped((units, rows, width), bf16), shaped((units, rows, width), f32),
            shaped((units, rows, lanes), f32), shaped((units, rows, width), bf16),
            shaped((width + 8, head.shape[1]), f32),
        ),
        in_specs=[hbm, vmem, hbm, hbm, hbm, vmem, vmem, vmem],
        out_specs=(hbm,) * 5 + (vmem,) * 5,
        scratch_shapes=[
            pltpu.VMEM(gate_w.shape, bf16), pltpu.VMEM(up_w.shape, bf16), pltpu.VMEM(down_w.shape, bf16),
            pltpu.VMEM((members, units, rows, lanes), bf16),
            *buffers,
            pltpu.VMEM((units, rows, width), bf16),
            pltpu.VMEM((2, every, width), bf16), pltpu.VMEM((2, every, hidden_dim), bf16),
            pltpu.VMEM((2, every, hidden_dim), bf16), pltpu.VMEM((2, every, hidden_dim), bf16),
            pltpu.VMEM((2, every, lanes), f32), pltpu.VMEM((members, rows, lanes), f32),
            dma((3,)), dma((members - 1,)), dma((members - 1,)), dma((units,)),
            dma((units,)), dma((units,)), dma((5, 2)),
            *sems,
        ],
        cost_estimate=pl.CostEstimate(
            flops=6 * units * members * rows * width * hidden_dim, bytes_accessed=500_000_000, transcendentals=0),
        compiler_params=pltpu.CompilerParams(
            collective_id=0, has_side_effects=True, vmem_limit_bytes=56 * 1024 * 1024),
    )(tokens, mask, gate_w, up_w, down_w, router_p, head, hot)


def backward_kernel(sizes, top, hid, dgate, dup, fac, own_in, mix, slope, gate, up, down, router, my_row,
                    grad_o, agate_o, aup_o, route_o, common_o,
                    gate_v, up_v, down_v, hid_v, dgate_v, dup_v, fac_v, own,
                    gath, parts, stage, sums, back, out_rows, total_v,
                    agate_t, aup_t, route_t,
                    w_sem, t_sem, z_send, z_recv, o_sem, *sems):
    sections, experts, cores = sizes
    units, rows, width = own.shape
    hidden_dim = gate_v.shape[1]
    s = lax.axis_index("section")
    last = sections - 1
    ex = Exchange(sizes, own, gath, parts, stage, sums, back, sems)
    e, d, me = ex.e, ex.d, ex.me
    members = experts * cores
    every = members * rows
    slabs, slab = ex.slabs, ex.wide

    loads = [pltpu.make_async_copy(a, b, w_sem.at[n]) for n, (a, b) in enumerate((
        (down, down_v), (hid, hid_v), (dgate, dgate_v), (dup, dup_v), (fac, fac_v), (gate, gate_v), (up, up_v)))]
    for load in loads:
        load.start()

    def take(m):
        return pltpu.make_async_copy(top.at[m], own.at[m], t_sem.at[m])

    @pl.when(s == last)
    def _():
        for m in range(units):
            take(m).start()

    meet(sizes, -1, False)

    def shift(m):
        return pltpu.make_async_remote_copy(
            src_ref=out_rows.at[m], dst_ref=own.at[m], send_sem=z_send.at[m], recv_sem=z_recv.at[m],
            device_id={"section": lax.rem(s + sections - 1, sections)}, device_id_type=MESH)

    def begin(m):
        @pl.when(s == last)
        def _():
            take(m).wait()

        @pl.when(s != last)
        def _():
            shift(m).wait_recv()

        ex.spread(m)

    def writes(m):
        side = m % 2
        pairs = ((agate_t, agate_o), (aup_t, aup_o), (route_t, route_o))
        return [pltpu.make_async_copy(a.at[side], b.at[m], o_sem.at[n, side])
                for n, (a, b) in enumerate(pairs)]

    def keep_grad(m):
        return pltpu.make_async_copy(gath.at[m % 2], grad_o.at[m], o_sem.at[3, m % 2])

    lane = lax.broadcasted_iota(jnp.int32, (every, lanes), 1)

    def widen(m):
        slot = m % 2

        @pl.when(m >= 2)
        def _():
            for copy in writes(m):
                copy.wait()

        ex.arrive(m, lambda block: None)
        keep_grad(m).start()
        grads = gath[slot].reshape(every, width)
        gain = jnp.zeros((every, 1), f32)
        wide = 256 if hidden_dim % 256 == 0 else hidden_dim
        for j in range(0, hidden_dim, wide):
            cols = slice(j, j + wide)
            down_grad = contract_last(grads, down_v[cols, :])
            agate_t[slot, :, cols] = (down_grad * dgate_v[m, :, cols].astype(f32)).astype(bf16)
            aup_t[slot, :, cols] = (down_grad * dup_v[m, :, cols].astype(f32)).astype(bf16)
            gain = gain + jnp.sum(down_grad * hid_v[m, :, cols].astype(f32), axis=-1, keepdims=True)
        route_t[slot] = jnp.where(lane == me, gain * fac_v[m], 0.0).astype(bf16)
        for copy in writes(m):
            copy.start()

    def narrow(m):
        slot = m % 2

        def keep(j, value):
            total_v[slot, :, j * slab:(j + 1) * slab] = value

        through = jnp.sum(route_t[slot].astype(f32), axis=-1, keepdims=True)
        tile = 512 if slab % 512 == 0 else slab
        for j in range(slabs):
            for i in range(0, slab, tile):
                cols = slice(j * slab + i, j * slab + i + tile)
                part = (contract_last(agate_t[slot], gate_v[cols, :])
                        + contract_last(aup_t[slot], up_v[cols, :])
                        + through * my_row[:, cols])
                part = part.astype(bf16).reshape(experts, cores, rows, tile)
                for c in range(cores):
                    parts[slot, j, c, :, :, i:i + tile] = part[:, c]
            ex.share(m, j).start()
        for j in range(slabs):
            ex.settle(m, j, keep)

    def finish(m):
        slot = m % 2

        def weigh(r, _):
            at = pl.ds(pl.multiple_of(r * row_step, row_step), row_step)
            shared = jnp.sum(own[m, at].astype(f32) * mix[m, at], axis=-1, keepdims=True)
            common_o[m, at] = (slope[m, at] * shared).astype(bf16)
            return 0
        lax.fori_loop(0, rows // row_step, weigh, 0)

        @pl.when(s != 0)
        def _():
            total_v[slot] = total_v[slot] - contract_last(common_o[m], router[...])
            ex.given(m)

            def total(r, _):
                at = pl.ds(pl.multiple_of(r * row_step, row_step), row_step)
                values = []
                for j in range(slabs):
                    value = total_v[slot, at, j * slab:(j + 1) * slab]
                    for k in range(1, experts):
                        value = value + back[slot, j, k - 1, at].astype(f32)
                    values.append(value)
                grad_normed = jnp.concatenate(values, axis=-1)
                hidden_f = own_in[m, at].astype(f32)
                inv_rms = lax.rsqrt(jnp.mean(hidden_f * hidden_f, axis=-1, keepdims=True) + norm_eps)
                normed_f = hidden_f * inv_rms
                out_rows[m, at] = (
                    own[m, at].astype(f32)
                    + inv_rms * (grad_normed
                                 - normed_f * jnp.mean(grad_normed * normed_f, axis=-1, keepdims=True))
                ).astype(bf16)
                return 0
            lax.fori_loop(0, rows // row_step, total, 0)
            shift(m).start()
            ex.returned(m)

        ex.gathered(m)

    begin(0)
    for load in loads:
        load.wait()

    def unit(m, _):
        widen(m)

        @pl.when(m >= 1)
        def _():
            finish(m - 1)

        ex.passed_on(m)
        keep_grad(m).wait()

        @pl.when(m + 1 < units)
        def _():
            begin(m + 1)

        @pl.when(s != 0)
        def _():
            narrow(m)
        return 0

    lax.fori_loop(0, units, unit, 0)
    finish(units - 1)

    @pl.when(s != 0)
    def _():
        for m in range(units):
            shift(m).wait_send()

    for m in range(max(0, units - 2), units):
        for copy in writes(m):
            copy.wait()


def backward(sizes, top, hid, dgate, dup, fac, own_in, mix, slope, gate_w, up_w, down_w, router_p, my_row):
    sections, experts, cores = sizes
    units, rows, width = top.shape
    hidden_dim = gate_w.shape[1]
    members = experts * cores
    every = members * rows
    vmem, hbm = pl.BlockSpec(memory_space=pltpu.VMEM), pl.BlockSpec(memory_space=pl.ANY)
    buffers, sems = exchange_scratch(experts, cores, rows, width)

    def shaped(shape, dtype):
        return jax.ShapeDtypeStruct(shape, dtype)

    acts = (units, every, hidden_dim)
    return pl.pallas_call(
        functools.partial(backward_kernel, sizes),
        out_shape=(
            shaped((units, members, rows, width), bf16), shaped(acts, bf16), shaped(acts, bf16),
            shaped((units, every, lanes), bf16), shaped((units, rows, lanes), bf16),
        ),
        in_specs=[hbm] * 5 + [vmem] * 3 + [hbm] * 3 + [vmem] * 2,
        out_specs=(hbm,) * 4 + (vmem,),
        scratch_shapes=[
            pltpu.VMEM(gate_w.shape, bf16), pltpu.VMEM(up_w.shape, bf16), pltpu.VMEM(down_w.shape, bf16),
            pltpu.VMEM(acts, bf16), pltpu.VMEM(acts, bf16), pltpu.VMEM(acts, bf16),
            pltpu.VMEM(fac.shape, f32), pltpu.VMEM((units, rows, width), bf16),
            *buffers,
            pltpu.VMEM((units, rows, width), bf16), pltpu.VMEM((2, rows, width), f32),
            pltpu.VMEM((2, every, hidden_dim), bf16), pltpu.VMEM((2, every, hidden_dim), bf16),
            pltpu.VMEM((2, every, lanes), bf16),
            dma((7,)), dma((units,)), dma((units,)), dma((units,)), dma((4, 2)),
            *sems,
        ],
        cost_estimate=pl.CostEstimate(
            flops=6 * units * members * rows * width * hidden_dim, bytes_accessed=500_000_000, transcendentals=0),
        compiler_params=pltpu.CompilerParams(
            collective_id=1, has_side_effects=True, vmem_limit_bytes=56 * 1024 * 1024),
    )(top, hid, dgate, dup, fac, own_in, mix, slope, gate_w, up_w, down_w, router_p, my_row)


def give_back_kernel(sizes, parts_ref, out_ref, stage_ref, sum_ref, d_send, d_recv, x_send, x_recv):
    sections, experts, cores = sizes
    e, d = lax.axis_index("expert"), lax.axis_index("dp")

    barrier = pltpu.get_barrier_semaphore()
    for off in range(1, experts):
        pl.semaphore_signal(barrier, inc=1, device_id={"expert": lax.rem(e + off, experts)}, device_id_type=MESH)
    for off in range(1, cores):
        pl.semaphore_signal(barrier, inc=1, device_id={"dp": lax.rem(d + off, cores)}, device_id_type=MESH)
    pl.semaphore_wait(barrier, experts + cores - 2)

    def beside(off, core_off):
        to_d = lax.rem(d + core_off, cores)
        return pltpu.make_async_remote_copy(
            src_ref=parts_ref.at[lax.rem(e + off, experts) * cores + to_d],
            dst_ref=stage_ref.at[core_off - 1, off],
            send_sem=d_send.at[core_off - 1, off], recv_sem=d_recv.at[core_off - 1, off],
            device_id={"dp": to_d}, device_id_type=MESH)

    def across(off):
        return pltpu.make_async_remote_copy(
            src_ref=sum_ref.at[off - 1], dst_ref=out_ref.at[e],
            send_sem=x_send.at[off - 1], recv_sem=x_recv.at[off - 1],
            device_id={"expert": lax.rem(e + off, experts)}, device_id_type=MESH)

    order = [off for off in range(experts - 1, 0, -1)] + [0]
    for off in order:
        for core_off in range(1, cores):
            beside(off, core_off).start()
    for n, off in enumerate(order):
        total = parts_ref[lax.rem(e + off, experts) * cores + d].astype(jnp.float32)
        for core_off in range(1, cores):
            beside(off, core_off).wait_recv()
            total = total + stage_ref[core_off - 1, off].astype(jnp.float32)
        if off == 0:
            out_ref[e] = total.astype(out_ref.dtype)
        else:
            sum_ref[off - 1] = total.astype(out_ref.dtype)
        if n > 0:
            across(order[n - 1]).start()
    for off in range(1, experts):
        across(off).wait()
    for off in order:
        for core_off in range(1, cores):
            beside(off, core_off).wait_send()


def give_back(sizes, parts, call_id):
    sections, experts, cores = sizes
    block = parts.shape[1:]
    return pl.pallas_call(
        functools.partial(give_back_kernel, sizes),
        out_shape=jax.ShapeDtypeStruct((experts,) + block, parts.dtype),
        in_specs=[pl.BlockSpec(memory_space=pltpu.VMEM)],
        out_specs=pl.BlockSpec(memory_space=pltpu.VMEM),
        scratch_shapes=[
            pltpu.VMEM((cores - 1, experts) + block, parts.dtype),
            pltpu.VMEM((experts - 1,) + block, parts.dtype),
            dma((cores - 1, experts)), dma((cores - 1, experts)),
            dma((experts - 1,)), dma((experts - 1,)),
        ],
        cost_estimate=pl.CostEstimate(flops=0, bytes_accessed=30 * parts.size * 2, transcendentals=0),
        compiler_params=pltpu.CompilerParams(collective_id=call_id, has_side_effects=True),
    )(parts)


def shards(sizes, tokens, expert_ids, labels, router, class_head, w_gate, w_up, w_down):
    sections, experts, cores = sizes
    members = experts * cores
    me = lax.axis_index("expert") * cores + lax.axis_index("dp")
    micro_count, tok_rows, width = tokens.shape
    router_w = router[0]
    expert_count = router_w.shape[1]
    gate_w, up_w, down_w = w_gate[0, 0], w_up[0, 0], w_down[0, 0]
    hidden_dim = gate_w.shape[1]
    rows = max(row_step, min(tok_rows, tok_rows * 2 // members))
    units = micro_count * tok_rows // rows

    router_p = jnp.pad(router_w, ((0, 0), (0, lanes - expert_count)))
    picks = expert_ids[0].reshape(units, rows, -1)
    named = jnp.arange(lanes, dtype=jnp.int32)
    mask = jnp.any(picks[:, :, :, None] == named, axis=2).astype(bf16)
    hot = (labels.reshape(-1)[:, None] == jnp.arange(class_head.shape[1], dtype=jnp.int32)[None, :]).astype(f32)
    my_row = lax.dynamic_index_in_dim(router_w.T, me, 0).astype(f32)

    normed, hid, dgate, dup, fac, own_in, mix, slope, top, head_term = forward(
        sizes, tokens.reshape(units, rows, width), mask, gate_w, up_w, down_w, router_p, class_head, hot)
    summed = lax.psum(head_term, ("section",) + group)
    grad_all, agate, aup, route, common = backward(
        sizes, top, hid, dgate, dup, fac, own_in, mix, slope, gate_w, up_w, down_w, router_p, my_row)

    every = units * members * rows
    normed = normed.reshape(every, width)
    grad_gate = contract_first(normed, agate.reshape(every, hidden_dim)).astype(bf16)
    grad_up = contract_first(normed, aup.reshape(every, hidden_dim)).astype(bf16)
    grad_down = contract_first(hid.reshape(every, hidden_dim), grad_all.reshape(every, width)).astype(bf16)

    own_f = own_in.reshape(-1, width).astype(f32)
    inv_rms = lax.rsqrt(jnp.mean(own_f * own_f, axis=-1, keepdims=True) + norm_eps)
    normed_own = (own_f * inv_rms).astype(bf16)
    router_sum = (contract_first(route.reshape(every, lanes), normed)
                  - contract_first(common.reshape(-1, lanes), normed_own))[:expert_count]
    copies = jnp.broadcast_to(router_sum[None], (members,) + router_sum.shape)
    router_out = jnp.sum(give_back(sizes, copies, 3), axis=0).T[None]
    mean_loss = summed[width, 0] / (micro_count * tok_rows * members)
    return (
        mean_loss,
        summed[:width],
        router_out,
        grad_gate[None, None],
        grad_up[None, None],
        grad_down[None, None],
    )


def solution(mesh):
    sizes = tuple(mesh.shape[axis] for axis in ("section", "expert", "dp"))
    return jax.shard_map(
        functools.partial(shards, sizes),
        mesh=mesh,
        in_specs=(
            P(None, ("expert", "dp"), None),
            P("section", None, ("expert", "dp"), None),
            P(None, ("expert", "dp")),
            P("section", None, None),
            P(),
            P("section", ("expert", "dp"), None, None),
            P("section", ("expert", "dp"), None, None),
            P("section", ("expert", "dp"), None, None),
        ),
        out_specs=(
            P(),
            P(),
            P("section", None, None),
            P("section", ("expert", "dp"), None, None),
            P("section", ("expert", "dp"), None, None),
            P("section", ("expert", "dp"), None, None),
        ),
        check_vma=False,
    )
```

```python
import functools

import jax
import jax.numpy as jnp
from jax import lax
from jax.experimental import pallas as pl
from jax.experimental.pallas import tpu as pltpu
from jax.sharding import PartitionSpec as P

soft_cap = 30.0
norm_eps = 1e-06
lanes = 128
row_step = 16
MESH = pl.DeviceIdType.MESH
dma = pltpu.SemaphoreType.DMA
bf16 = jnp.bfloat16
f32 = jnp.float32


def capped(values):
    return soft_cap * jnp.tanh(values / soft_cap)


def dot_plain(left, right):
    return jnp.dot(left, right, preferred_element_type=f32)


def contract_first(left, right):
    return lax.dot_general(left, right, (((0,), (0,)), ((), ())), preferred_element_type=f32)


def contract_last(left, right):
    return lax.dot_general(left, right, (((1,), (1,)), ((), ())), preferred_element_type=f32)


def partner(e, k, count):
    total, bit = 0, 1
    while bit < count:
        a, b = (e // bit) % 2, (k // bit) % 2
        total = total + (a + b - 2 * a * b) * bit
        bit *= 2
    return total


class Exchange:
    def __init__(self, sizes, own, gath, parts, stage, sums, back, sems):
        self.sizes, self.own, self.gath = sizes, own, gath
        self.parts, self.stage, self.sums, self.back = parts, stage, sums, back
        (self.x_send, self.x_recv, self.d_send, self.d_recv, self.f_send, self.f_recv,
         self.p_send, self.p_recv, self.r_send, self.r_recv) = sems
        self.e, self.d = lax.axis_index("expert"), lax.axis_index("dp")
        self.me = self.e * 2 + self.d
        self.slabs, self.wide = parts.shape[1], parts.shape[-1]

    def chip(self, k):
        return partner(self.e, k, self.sizes[1])

    def across(self, m, k):
        slot = m % 3
        return pltpu.make_async_remote_copy(
            src_ref=self.own.at[m], dst_ref=self.gath.at[slot, self.me],
            send_sem=self.x_send.at[slot, k - 1], recv_sem=self.x_recv.at[slot, k - 1],
            device_id={"expert": self.chip(k)}, device_id_type=MESH)

    def beside(self, m):
        slot = m % 3
        return pltpu.make_async_remote_copy(
            src_ref=self.own.at[m], dst_ref=self.gath.at[slot, self.me],
            send_sem=self.d_send.at[slot], recv_sem=self.d_recv.at[slot],
            device_id={"dp": 1 - self.d}, device_id_type=MESH)

    def onward(self, m, k):
        slot = m % 3
        block = self.chip(k) * 2 + self.d
        return pltpu.make_async_remote_copy(
            src_ref=self.gath.at[slot, block], dst_ref=self.gath.at[slot, block],
            send_sem=self.f_send.at[slot, k - 1], recv_sem=self.f_recv.at[slot, k - 1],
            device_id={"dp": 1 - self.d}, device_id_type=MESH)

    def share(self, m, j):
        slot = m % 2
        return pltpu.make_async_remote_copy(
            src_ref=self.parts.at[slot, j, 1 - self.d], dst_ref=self.stage.at[slot, j],
            send_sem=self.p_send.at[slot, j], recv_sem=self.p_recv.at[slot, j],
            device_id={"dp": 1 - self.d}, device_id_type=MESH)

    def give(self, m, j, k):
        slot = m % 2
        return pltpu.make_async_remote_copy(
            src_ref=self.sums.at[slot, j, k - 1], dst_ref=self.back.at[slot, j, k - 1],
            send_sem=self.r_send.at[slot, j, k - 1], recv_sem=self.r_recv.at[slot, j, k - 1],
            device_id={"expert": self.chip(k)}, device_id_type=MESH)

    def spread(self, m):
        for k in range(1, self.sizes[1]):
            self.across(m, k).start()
        self.beside(m).start()
        self.gath[m % 3, self.me] = self.own[m]

    def arrive(self, m, use):
        experts = self.sizes[1]
        use(self.me)
        self.beside(m).wait_recv()
        use(self.e * 2 + 1 - self.d)
        for k in range(1, experts):
            self.across(m, k).wait_recv()
            self.onward(m, k).start()
            use(self.chip(k) * 2 + self.d)
        for k in range(1, experts):
            self.onward(m, k).wait_recv()
            use(self.chip(k) * 2 + 1 - self.d)

    def passed_on(self, m):
        for k in range(1, self.sizes[1]):
            self.onward(m, k).wait_send()

    def settle(self, m, j, keep_own):
        slot = m % 2
        experts = self.sizes[1]
        self.share(m, j).wait_recv()
        for k in range(experts - 1, -1, -1):
            chip = self.chip(k)
            value = self.parts[slot, j, self.d, chip].astype(f32) + self.stage[slot, j, chip].astype(f32)
            if k == 0:
                keep_own(j, value)
            else:
                self.sums[slot, j, k - 1] = value.astype(bf16)
                self.give(m, j, k).start()

    def gathered(self, m):
        self.beside(m).wait_send()
        for k in range(1, self.sizes[1]):
            self.across(m, k).wait_send()

    def given(self, m):
        for j in range(self.slabs):
            for k in range(1, self.sizes[1]):
                self.give(m, j, k).wait_recv()

    def returned(self, m):
        for j in range(self.slabs):
            self.share(m, j).wait_send()
            for k in range(1, self.sizes[1]):
                self.give(m, j, k).wait_send()


def tall(router_t):
    rows = router_t[...].astype(f32)
    return jnp.concatenate([rows, jnp.zeros((lanes - rows.shape[0], rows.shape[1]), f32)], axis=0).astype(bf16)


def meet(sizes, step):
    sections, experts, cores = sizes
    s, e, d = lax.axis_index("section"), lax.axis_index("expert"), lax.axis_index("dp")
    me = e * cores + d
    first, last = (0, sections - 1) if step > 0 else (sections - 1, 0)
    barrier = pltpu.get_barrier_semaphore()
    count = experts * cores - 1
    for off in range(1, experts * cores):
        other = lax.rem(me + off, experts * cores)
        pl.semaphore_signal(
            barrier, inc=1, device_id={"expert": other // cores, "dp": lax.rem(other, cores)},
            device_id_type=MESH)

    @pl.when(s != first)
    def _():
        pl.semaphore_signal(barrier, inc=1, device_id={"section": s - step}, device_id_type=MESH)

    pl.semaphore_wait(barrier, count + (s != last).astype(jnp.int32))


def forward_kernel(sizes, tokens, ids, gate, up, down, router_t, head, labels,
                   normed_o, hid_o, dgate_o, dup_o, fac_o, own, mix, slope_o, top_o, head_o, loss_o,
                   gate_v, up_v, down_v, mask, mask_all, router, gath, parts, stage, sums, back, out_rows,
                   normed_t, hid_t, dgate_t, dup_t, fac_t, slope_t,
                   w_sem, k_send, k_recv, t_sem, z_send, z_recv, o_sem, *sems):
    sections, experts, cores = sizes
    units, rows, width = own.shape
    hidden_dim = gate_v.shape[1]
    s = lax.axis_index("section")
    last = sections - 1
    ex = Exchange(sizes, own, gath, parts, stage, sums, back, sems)
    e, d, me = ex.e, ex.d, ex.me
    members = experts * cores
    every = members * rows
    slabs, slab = ex.slabs, ex.wide

    loads = [pltpu.make_async_copy(a, b, w_sem.at[n])
             for n, (a, b) in enumerate(((gate, gate_v), (up, up_v), (down, down_v)))]
    for load in loads:
        load.start()

    def take(m):
        return pltpu.make_async_copy(tokens.at[m], own.at[m], t_sem.at[m])

    @pl.when(s == 0)
    def _():
        for m in range(units):
            take(m).start()

    named_lane = lax.broadcasted_iota(jnp.int32, (units * rows, lanes), 1)
    named = named_lane == ids[:, 0:1]
    for k in range(1, ids.shape[1]):
        named = named | (named_lane == ids[:, k:k + 1])
    mask[...] = jnp.where(named, 1.0, 0.0).astype(bf16).reshape(units, rows, lanes)
    router[...] = tall(router_t)
    meet(sizes, 1)

    def tell(off):
        other = lax.rem(me + off, members)
        return pltpu.make_async_remote_copy(
            src_ref=mask, dst_ref=mask_all.at[me], send_sem=k_send.at[off - 1], recv_sem=k_recv.at[off - 1],
            device_id={"expert": other // cores, "dp": lax.rem(other, cores)}, device_id_type=MESH)

    def shift(m):
        return pltpu.make_async_remote_copy(
            src_ref=out_rows.at[m], dst_ref=own.at[m], send_sem=z_send.at[m], recv_sem=z_recv.at[m],
            device_id={"section": lax.rem(s + 1, sections)}, device_id_type=MESH)

    def begin(m):
        @pl.when(s == 0)
        def _():
            take(m).wait()

        @pl.when(s != 0)
        def _():
            shift(m).wait_recv()

        ex.spread(m)

    def writes(m):
        side = m % 2
        pairs = ((normed_t, normed_o), (hid_t, hid_o), (dgate_t, dgate_o), (dup_t, dup_o), (fac_t, fac_o))
        return [pltpu.make_async_copy(a.at[side], b.at[m], o_sem.at[n, side])
                for n, (a, b) in enumerate(pairs)]

    lane = lax.broadcasted_iota(jnp.int32, (every, lanes), 1)

    def enter(m):
        slot = m % 2

        @pl.when(m >= 2)
        def _():
            for copy in writes(m):
                copy.wait()

        def norm_block(block):
            def norm(r, _):
                at = pl.ds(pl.multiple_of(r * row_step, row_step), row_step)
                values = gath[m % 3, block, at].astype(f32)
                inv = lax.rsqrt(jnp.mean(values * values, axis=-1, keepdims=True) + norm_eps)
                normed_t[slot, pl.ds(pl.multiple_of(block * rows + r * row_step, row_step), row_step)] = (
                    values * inv).astype(bf16)
                return 0
            lax.fori_loop(0, rows // row_step, norm, 0)

        ex.arrive(m, norm_block)
        ex.passed_on(m)

    def widen(m):
        slot = m % 2
        chosen = capped(contract_last(normed_t[slot], router[...]))
        named = mask_all[:, m].reshape(every, lanes).astype(f32)
        weights = jnp.exp(chosen) * named
        probs = weights / jnp.sum(weights, axis=-1, keepdims=True)
        scaled = chosen / soft_cap
        bend = 1.0 - scaled * scaled
        mine = jnp.sum(jnp.where(lane == me, probs, 0.0), axis=-1, keepdims=True)
        fac_t[slot] = jnp.broadcast_to(
            jnp.sum(jnp.where(lane == me, bend, 0.0), axis=-1, keepdims=True), (every, lanes))
        slope_t[...] = (probs * bend).reshape(members, rows, lanes)
        slope_o[m] = slope_t[me]

        wide = 256 if hidden_dim % 256 == 0 else hidden_dim
        for j in range(0, hidden_dim, wide):
            cols = slice(j, j + wide)
            gate_act = dot_plain(normed_t[slot], gate_v[:, cols])
            up_act = dot_plain(normed_t[slot], up_v[:, cols])
            sig = jax.nn.sigmoid(gate_act)
            silu = mine * (gate_act * sig)
            hid_t[slot, :, cols] = (silu * up_act).astype(bf16)
            dgate_t[slot, :, cols] = (mine * up_act * sig * (1.0 + gate_act * (1.0 - sig))).astype(bf16)
            dup_t[slot, :, cols] = silu.astype(bf16)
        for copy in writes(m):
            copy.start()

    def narrow(m):
        slot = m % 2

        def keep(j, value):
            mix[m, :, j * slab:(j + 1) * slab] = value

        tile = 512 if slab % 512 == 0 else slab
        for j in range(slabs):
            for i in range(0, slab, tile):
                part = dot_plain(hid_t[slot], down_v[:, j * slab + i:j * slab + i + tile]).astype(bf16)
                part = part.reshape(experts, cores, rows, tile)
                for c in range(cores):
                    parts[slot, j, c, :, :, i:i + tile] = part[:, c]
            ex.share(m, j).start()
        for j in range(slabs):
            ex.settle(m, j, keep)

    def finish(m):
        slot = m % 2
        ex.given(m)

        def total(r, _):
            at = pl.ds(pl.multiple_of(r * row_step, row_step), row_step)
            for j in range(slabs):
                cols = slice(j * slab, (j + 1) * slab)
                value = mix[m, at, cols]
                for k in range(1, experts):
                    value = value + back[slot, j, k - 1, at].astype(f32)
                mix[m, at, cols] = value
                out_rows[m, at, cols] = (own[m, at, cols].astype(f32) + value).astype(bf16)
            return 0
        lax.fori_loop(0, rows // row_step, total, 0)

        @pl.when(s != last)
        def _():
            shift(m).start()

        ex.gathered(m)
        ex.returned(m)

    mask_all[me] = mask[...]
    for off in range(1, members):
        tell(off).start()
    begin(0)
    for off in range(1, members):
        tell(off).wait()
    for load in loads:
        load.wait()

    def unit(m, _):
        enter(m)

        @pl.when(m + 1 < units)
        def _():
            begin(m + 1)

        widen(m)

        @pl.when(m >= 1)
        def _():
            finish(m - 1)

        narrow(m)
        return 0

    lax.fori_loop(0, units, unit, 0)
    finish(units - 1)

    @pl.when(s != last)
    def _():
        head_o[...] = jnp.zeros_like(head_o)
        loss_o[...] = jnp.zeros_like(loss_o)
        for m in range(units):
            shift(m).wait_send()

    @pl.when(s == last)
    def _():
        final = out_rows[...].reshape(units * rows, width)
        class_logits = capped(dot_plain(final, head[...]))
        class_weights = jnp.exp(class_logits)
        class_total = jnp.sum(class_weights, axis=-1, keepdims=True)
        label_hot = (
            lax.broadcasted_iota(jnp.int32, class_logits.shape, 1) == labels[...]).astype(f32)
        loss = jnp.log(class_total) - jnp.sum(label_hot * class_logits, axis=-1, keepdims=True)
        scaled = class_logits / soft_cap
        grad_logits = ((class_weights / class_total - label_hot) * (1.0 - scaled * scaled)).astype(bf16)
        top_o[...] = contract_last(grad_logits, head[...]).astype(bf16).reshape(units, rows, width)
        head_o[...] = contract_first(final, grad_logits).reshape(head_o.shape).astype(bf16)
        loss_o[...] = jnp.full(loss_o.shape, jnp.sum(loss), f32)

    for m in range(max(0, units - 2), units):
        for copy in writes(m):
            copy.wait()


def exchange_scratch(experts, cores, rows, width):
    slabs = 2 if width % 256 == 0 else 1
    slab = width // slabs
    return [
        pltpu.VMEM((3, experts * cores, rows, width), bf16),
        pltpu.VMEM((2, slabs, cores, experts, rows, slab), bf16),
        pltpu.VMEM((2, slabs, experts, rows, slab), bf16),
        pltpu.VMEM((2, slabs, experts - 1, rows, slab), bf16),
        pltpu.VMEM((2, slabs, experts - 1, rows, slab), bf16),
    ], [
        dma((3, experts - 1)), dma((3, experts - 1)), dma((3,)), dma((3,)),
        dma((3, experts - 1)), dma((3, experts - 1)), dma((2, slabs)), dma((2, slabs)),
        dma((2, slabs, experts - 1)), dma((2, slabs, experts - 1)),
    ]


def forward(sizes, tokens, ids, gate_w, up_w, down_w, router_t, head, labels):
    sections, experts, cores = sizes
    units, rows, width = tokens.shape
    hidden_dim = gate_w.shape[1]
    members = experts * cores
    every = members * rows
    vmem, hbm = pl.BlockSpec(memory_space=pltpu.VMEM), pl.BlockSpec(memory_space=pl.ANY)
    buffers, sems = exchange_scratch(experts, cores, rows, width)

    def shaped(shape, dtype):
        return jax.ShapeDtypeStruct(shape, dtype)

    acts = (units, every, hidden_dim)
    return pl.pallas_call(
        functools.partial(forward_kernel, sizes),
        out_shape=(
            shaped((units, every, width), bf16), shaped(acts, bf16), shaped(acts, bf16),
            shaped(acts, bf16), shaped((units, every, lanes), f32),
            shaped((units, rows, width), bf16), shaped((units, rows, width), f32),
            shaped((units, rows, lanes), f32), shaped((units, rows, width), bf16),
            shaped((members, width // members, head.shape[1]), bf16), shaped((8, lanes), f32),
        ),
        in_specs=[hbm, vmem, hbm, hbm, hbm, vmem, vmem, vmem],
        out_specs=(hbm,) * 5 + (vmem,) * 6,
        scratch_shapes=[
            pltpu.VMEM(gate_w.shape, bf16), pltpu.VMEM(up_w.shape, bf16), pltpu.VMEM(down_w.shape, bf16),
            pltpu.VMEM((units, rows, lanes), bf16), pltpu.VMEM((members, units, rows, lanes), bf16),
            pltpu.VMEM((lanes, width), bf16),
            *buffers,
            pltpu.VMEM((units, rows, width), bf16),
            pltpu.VMEM((2, every, width), bf16), pltpu.VMEM((2, every, hidden_dim), bf16),
            pltpu.VMEM((2, every, hidden_dim), bf16), pltpu.VMEM((2, every, hidden_dim), bf16),
            pltpu.VMEM((2, every, lanes), f32), pltpu.VMEM((members, rows, lanes), f32),
            dma((3,)), dma((members - 1,)), dma((members - 1,)), dma((units,)),
            dma((units,)), dma((units,)), dma((5, 2)),
            *sems,
        ],
        cost_estimate=pl.CostEstimate(
            flops=6 * units * members * rows * width * hidden_dim, bytes_accessed=500_000_000, transcendentals=0),
        compiler_params=pltpu.CompilerParams(
            collective_id=0, has_side_effects=True, vmem_limit_bytes=56 * 1024 * 1024),
    )(tokens, ids, gate_w, up_w, down_w, router_t, head, labels)


def backward_kernel(sizes, top, hid, dgate, dup, fac, normed, own_in, mix, slope, gate, up, down, router_t, head_in, loss_in,
                    grad_o, agate_o, aup_o, router_o, head_o, loss_o,
                    gate_v, up_v, down_v, hid_v, dgate_v, dup_v, fac_v, normed_v, own, router, common, normed_own,
                    routed, parted, parted_all, head_part, head_all, loss_all,
                    gath, parts, stage, sums, back, out_rows, total_v,
                    agate_t, aup_t, route_t,
                    w_sem, i_sem, t_sem, z_send, z_recv, o_sem, q_send, q_recv, h_send, h_recv, l_send, l_recv,
                    b_send, b_recv, c_send, c_recv, *sems):
    sections, experts, cores = sizes
    units, rows, width = own.shape
    hidden_dim = gate_v.shape[1]
    expert_count = router_t.shape[0]
    s = lax.axis_index("section")
    last = sections - 1
    ex = Exchange(sizes, own, gath, parts, stage, sums, back, sems)
    e, d, me = ex.e, ex.d, ex.me
    members = experts * cores
    every = members * rows
    slabs, slab = ex.slabs, ex.wide

    loads = [pltpu.make_async_copy(a, b, w_sem.at[n]) for n, (a, b) in enumerate((
        (down, down_v), (gate, gate_v), (up, up_v)))]

    def reads(m):
        side = m % 2
        pairs = ((hid, hid_v), (dgate, dgate_v), (dup, dup_v), (fac, fac_v), (normed, normed_v))
        return [pltpu.make_async_copy(a.at[m], b.at[side], i_sem.at[n, side]) for n, (a, b) in enumerate(pairs)]

    for load in loads:
        load.start()
    for m in range(min(2, units)):
        for copy in reads(m):
            copy.start()

    def take(m):
        return pltpu.make_async_copy(top.at[m], own.at[m], t_sem.at[m])

    @pl.when(s == last)
    def _():
        for m in range(units):
            take(m).start()

    router[...] = tall(router_t)
    routed[...] = jnp.zeros_like(routed)
    meet(sizes, -1)

    def other(off):
        to = lax.rem(me + off, members)
        return to, {"expert": to // cores, "dp": lax.rem(to, cores)}

    def head_piece(off):
        to, device = other(off)
        return pltpu.make_async_remote_copy(
            src_ref=head_in.at[to], dst_ref=head_part.at[me], send_sem=h_send.at[off - 1],
            recv_sem=h_recv.at[off - 1], device_id=device, device_id_type=MESH)

    def loss_piece(off):
        to, device = other(off)
        return pltpu.make_async_remote_copy(
            src_ref=loss_in, dst_ref=loss_all.at[me], send_sem=l_send.at[off - 1],
            recv_sem=l_recv.at[off - 1], device_id=device, device_id_type=MESH)

    def head_whole(off):
        to, device = other(off)
        return pltpu.make_async_remote_copy(
            src_ref=head_all.at[me], dst_ref=head_all.at[me], send_sem=b_send.at[off - 1],
            recv_sem=b_recv.at[off - 1], device_id=device, device_id_type=MESH)

    def router_part(off):
        to, device = other(off)
        return pltpu.make_async_remote_copy(
            src_ref=parted, dst_ref=parted_all.at[me], send_sem=q_send.at[off - 1],
            recv_sem=q_recv.at[off - 1], device_id=device, device_id_type=MESH)

    down_section = {"section": lax.rem(s + sections - 1, sections)}

    def chain():
        return [
            pltpu.make_async_remote_copy(
                src_ref=head_all.at[me], dst_ref=head_all.at[me], send_sem=c_send.at[0], recv_sem=c_recv.at[0],
                device_id=down_section, device_id_type=MESH),
            pltpu.make_async_remote_copy(
                src_ref=loss_o, dst_ref=loss_o, send_sem=c_send.at[1], recv_sem=c_recv.at[1],
                device_id=down_section, device_id_type=MESH),
        ]

    def head_sums():
        @pl.when(s == last)
        def _():
            for off in range(1, members):
                head_piece(off).start()
                loss_piece(off).start()
            head_part[me] = head_in[me]
            loss_all[me] = loss_in[...]
            for off in range(1, members):
                head_piece(off).wait()
                loss_piece(off).wait()
            value, loss = head_part[0].astype(f32), loss_all[0]
            for n in range(1, members):
                value, loss = value + head_part[n].astype(f32), loss + loss_all[n]
            head_all[me] = value.astype(bf16)
            loss_o[...] = loss

        @pl.when(s != last)
        def _():
            for copy in chain():
                copy.wait_recv()

        @pl.when(s != 0)
        def _():
            for copy in chain():
                copy.start()

        for off in range(1, members):
            head_whole(off).start()

    def shift(m):
        return pltpu.make_async_remote_copy(
            src_ref=out_rows.at[m], dst_ref=own.at[m], send_sem=z_send.at[m], recv_sem=z_recv.at[m],
            device_id={"section": lax.rem(s + sections - 1, sections)}, device_id_type=MESH)

    def begin(m):
        @pl.when(s == last)
        def _():
            take(m).wait()

        @pl.when(s != last)
        def _():
            shift(m).wait_recv()

        ex.spread(m)

    def writes(m):
        side = m % 2
        pairs = ((agate_t, agate_o), (aup_t, aup_o))
        return [pltpu.make_async_copy(a.at[side], b.at[m], o_sem.at[n, side])
                for n, (a, b) in enumerate(pairs)]

    def keep_grad(m):
        return pltpu.make_async_copy(gath.at[m % 3], grad_o.at[m], o_sem.at[2, 0])

    lane = lax.broadcasted_iota(jnp.int32, (every, lanes), 1)

    def widen(m):
        slot = m % 2

        @pl.when(m >= 2)
        def _():
            for copy in writes(m):
                copy.wait()

        for copy in reads(m):
            copy.wait()
        grads = gath[m % 3].reshape(every, width)
        gain = jnp.zeros((every, 1), f32)
        wide = 256 if hidden_dim % 256 == 0 else hidden_dim
        for j in range(0, hidden_dim, wide):
            cols = slice(j, j + wide)
            down_grad = contract_last(grads, down_v[cols, :])
            agate_t[slot, :, cols] = (down_grad * dgate_v[slot, :, cols].astype(f32)).astype(bf16)
            aup_t[slot, :, cols] = (down_grad * dup_v[slot, :, cols].astype(f32)).astype(bf16)
            gain = gain + jnp.sum(down_grad * hid_v[slot, :, cols].astype(f32), axis=-1, keepdims=True)
        route_t[slot] = jnp.where(lane == me, gain * fac_v[slot], 0.0).astype(bf16)
        for copy in writes(m):
            copy.start()
        tile = 512 if width % 512 == 0 else width
        for i in range(0, width, tile):
            cols = slice(i, i + tile)
            routed[:, cols] = routed[:, cols] + contract_first(route_t[slot], normed_v[slot, :, cols])

        @pl.when(m + 2 < units)
        def _():
            for copy in reads(m + 2):
                copy.start()

    def narrow(m):
        slot = m % 2

        def keep(j, value):
            total_v[slot, :, j * slab:(j + 1) * slab] = value

        tile = 512 if slab % 512 == 0 else slab
        for j in range(slabs):
            for i in range(0, slab, tile):
                cols = slice(j * slab + i, j * slab + i + tile)
                part = (contract_last(agate_t[slot], gate_v[cols, :])
                        + contract_last(aup_t[slot], up_v[cols, :])
                        + dot_plain(route_t[slot], router[:, cols]))
                part = part.astype(bf16).reshape(experts, cores, rows, tile)
                for c in range(cores):
                    parts[slot, j, c, :, :, i:i + tile] = part[:, c]
            ex.share(m, j).start()
        for j in range(slabs):
            ex.settle(m, j, keep)

    def finish(m):
        slot = m % 2

        grad_f = own[m].astype(f32)
        shared = jnp.sum(grad_f * mix[m], axis=-1, keepdims=True)
        common[m] = (slope[m] * shared).astype(bf16)
        hidden_f = own_in[m].astype(f32)
        inv_rms = lax.rsqrt(jnp.mean(hidden_f * hidden_f, axis=-1, keepdims=True) + norm_eps)
        normed_f = hidden_f * inv_rms
        normed_own[m] = normed_f.astype(bf16)

        @pl.when(s != 0)
        def _():
            total_v[slot] = total_v[slot] - dot_plain(common[m], router[...])
            ex.given(m)
            values = []
            for j in range(slabs):
                value = total_v[slot, :, j * slab:(j + 1) * slab]
                for k in range(1, experts):
                    value = value + back[slot, j, k - 1].astype(f32)
                values.append(value)
            grad_normed = jnp.concatenate(values, axis=-1)
            out_rows[m] = (
                own[m].astype(f32)
                + inv_rms * (grad_normed
                             - normed_f * jnp.mean(grad_normed * normed_f, axis=-1, keepdims=True))
            ).astype(bf16)
            shift(m).start()
            ex.returned(m)

        ex.gathered(m)

    begin(0)
    for load in loads:
        load.wait()

    def unit(m, _):
        ex.arrive(m, lambda block: None)
        ex.passed_on(m)
        keep_grad(m).start()

        @pl.when(m + 1 < units)
        def _():
            begin(m + 1)

        @pl.when((s == 0) & (m == units - 1))
        def _():
            head_sums()

        widen(m)
        keep_grad(m).wait()

        @pl.when(m >= 1)
        def _():
            finish(m - 1)

        @pl.when(s != 0)
        def _():
            narrow(m)
        return 0

    lax.fori_loop(0, units, unit, 0)
    finish(units - 1)

    mine = routed[pl.ds(0, expert_count)] - contract_first(
        common[...].reshape(units * rows, lanes), normed_own[...].reshape(units * rows, width))[:expert_count]
    half = width // 2
    parted[...] = jnp.concatenate([mine[:, :half], mine[:, half:]], axis=0).astype(bf16)
    parted_all[me] = parted[...]
    for off in range(1, members):
        router_part(off).start()

    @pl.when(s != 0)
    def _():
        head_sums()
        for m in range(units):
            shift(m).wait_send()
        for copy in chain():
            copy.wait_send()

    for off in range(1, members):
        head_whole(off).wait()
    head_o[...] = head_all[...].astype(f32)
    for off in range(1, members):
        router_part(off).wait()
    value = parted_all[0].astype(f32)
    for n in range(1, members):
        value = value + parted_all[n].astype(f32)
    router_o[:, :half] = value[:expert_count]
    router_o[:, half:] = value[expert_count:]

    for m in range(max(0, units - 2), units):
        for copy in writes(m):
            copy.wait()


def backward(sizes, top, hid, dgate, dup, fac, normed, own_in, mix, slope, gate_w, up_w, down_w, router_t, head, loss):
    sections, experts, cores = sizes
    units, rows, width = top.shape
    hidden_dim = gate_w.shape[1]
    members = experts * cores
    every = members * rows
    vmem, hbm = pl.BlockSpec(memory_space=pltpu.VMEM), pl.BlockSpec(memory_space=pl.ANY)
    buffers, sems = exchange_scratch(experts, cores, rows, width)

    def shaped(shape, dtype):
        return jax.ShapeDtypeStruct(shape, dtype)

    acts = (units, every, hidden_dim)
    return pl.pallas_call(
        functools.partial(backward_kernel, sizes),
        out_shape=(
            shaped((units, members, rows, width), bf16), shaped(acts, bf16), shaped(acts, bf16),
            shaped(router_t.shape, f32), shaped(head.shape, f32), shaped(loss.shape, f32),
        ),
        in_specs=[hbm] * 6 + [vmem] * 3 + [hbm] * 3 + [vmem] * 3,
        out_specs=(hbm,) * 3 + (vmem,) * 3,
        scratch_shapes=[
            pltpu.VMEM(gate_w.shape, bf16), pltpu.VMEM(up_w.shape, bf16), pltpu.VMEM(down_w.shape, bf16),
            pltpu.VMEM((2, every, hidden_dim), bf16), pltpu.VMEM((2, every, hidden_dim), bf16),
            pltpu.VMEM((2, every, hidden_dim), bf16), pltpu.VMEM((2, every, lanes), f32),
            pltpu.VMEM((2, every, width), bf16), pltpu.VMEM((units, rows, width), bf16),
            pltpu.VMEM((lanes, width), bf16), pltpu.VMEM((units, rows, lanes), bf16),
            pltpu.VMEM((units, rows, width), bf16),
            pltpu.VMEM((lanes, width), f32), pltpu.VMEM((2 * router_t.shape[0], width // 2), bf16),
            pltpu.VMEM((members, 2 * router_t.shape[0], width // 2), bf16),
            pltpu.VMEM(head.shape, bf16), pltpu.VMEM(head.shape, bf16), pltpu.VMEM((members,) + loss.shape, f32),
            *buffers,
            pltpu.VMEM((units, rows, width), bf16), pltpu.VMEM((2, rows, width), f32),
            pltpu.VMEM((2, every, hidden_dim), bf16), pltpu.VMEM((2, every, hidden_dim), bf16),
            pltpu.VMEM((2, every, lanes), bf16),
            dma((3,)), dma((5, 2)), dma((units,)), dma((units,)), dma((units,)), dma((3, 2)),
            *[dma((members - 1,))] * 8, dma((2,)), dma((2,)),
            *sems,
        ],
        cost_estimate=pl.CostEstimate(
            flops=6 * units * members * rows * width * hidden_dim, bytes_accessed=500_000_000, transcendentals=0),
        compiler_params=pltpu.CompilerParams(
            collective_id=1, has_side_effects=True, vmem_limit_bytes=56 * 1024 * 1024),
    )(top, hid, dgate, dup, fac, normed, own_in, mix, slope, gate_w, up_w, down_w, router_t, head, loss)


def shards(sizes, tokens, expert_ids, labels, router, class_head, w_gate, w_up, w_down):
    sections, experts, cores = sizes
    members = experts * cores
    micro_count, tok_rows, width = tokens.shape
    gate_w, up_w, down_w = w_gate[0, 0], w_up[0, 0], w_down[0, 0]
    hidden_dim = gate_w.shape[1]
    rows = max(row_step, min(tok_rows, tok_rows * 2 // members))
    units = micro_count * tok_rows // rows

    router_t = router[0].T
    ids = expert_ids[0].reshape(units * rows, -1)
    normed, hid, dgate, dup, fac, own_in, mix, slope, top, head_term, loss_term = forward(
        sizes, tokens.reshape(units, rows, width), ids, gate_w, up_w, down_w, router_t, class_head,
        labels.reshape(-1, 1))
    grad_all, agate, aup, router_sum, head_total, loss_total = backward(
        sizes, top, hid, dgate, dup, fac, normed, own_in, mix, slope, gate_w, up_w, down_w, router_t,
        head_term, loss_term)

    every = units * members * rows
    normed = normed.reshape(every, width)
    grad_gate = contract_first(normed, agate.reshape(every, hidden_dim)).astype(bf16)
    grad_up = contract_first(normed, aup.reshape(every, hidden_dim)).astype(bf16)
    grad_down = contract_first(hid.reshape(every, hidden_dim), grad_all.reshape(every, width)).astype(bf16)
    mean_loss = loss_total[0, 0] / (micro_count * tok_rows * members)
    return (
        mean_loss,
        head_total.reshape(width, -1),
        router_sum.T[None],
        grad_gate[None, None],
        grad_up[None, None],
        grad_down[None, None],
    )


def solution(mesh):
    sizes = tuple(mesh.shape[axis] for axis in ("section", "expert", "dp"))
    return jax.shard_map(
        functools.partial(shards, sizes),
        mesh=mesh,
        in_specs=(
            P(None, ("expert", "dp"), None),
            P("section", None, ("expert", "dp"), None),
            P(None, ("expert", "dp")),
            P("section", None, None),
            P(),
            P("section", ("expert", "dp"), None, None),
            P("section", ("expert", "dp"), None, None),
            P("section", ("expert", "dp"), None, None),
        ),
        out_specs=(
            P(),
            P(),
            P("section", None, None),
            P("section", ("expert", "dp"), None, None),
            P("section", ("expert", "dp"), None, None),
            P("section", ("expert", "dp"), None, None),
        ),
        check_vma=False,
    )
```

```python
import functools

import jax
import jax.numpy as jnp
from jax import lax
from jax.experimental import pallas as pl
from jax.experimental.pallas import tpu as pltpu
from jax.sharding import PartitionSpec as P

soft_cap = 30.0
norm_eps = 1e-06
lanes = 128
row_step = 16
MESH = pl.DeviceIdType.MESH
dma = pltpu.SemaphoreType.DMA
bf16 = jnp.bfloat16
f32 = jnp.float32


def capped(values):
    return soft_cap * jnp.tanh(values / soft_cap)


def dot_plain(left, right):
    return jnp.dot(left, right, preferred_element_type=f32)


def contract_first(left, right):
    return lax.dot_general(left, right, (((0,), (0,)), ((), ())), preferred_element_type=f32)


def contract_last(left, right):
    return lax.dot_general(left, right, (((1,), (1,)), ((), ())), preferred_element_type=f32)


def partner(e, k, count):
    total, bit = 0, 1
    while bit < count:
        a, b = (e // bit) % 2, (k // bit) % 2
        total = total + (a + b - 2 * a * b) * bit
        bit *= 2
    return total


class Exchange:
    def __init__(self, sizes, own, gath, parts, stage, sums, back, sems):
        self.sizes, self.own, self.gath = sizes, own, gath
        self.parts, self.stage, self.sums, self.back = parts, stage, sums, back
        (self.x_send, self.x_recv, self.d_send, self.d_recv, self.f_send, self.f_recv,
         self.p_send, self.p_recv, self.r_send, self.r_recv) = sems
        self.e, self.d = lax.axis_index("expert"), lax.axis_index("dp")
        self.me = self.e * 2 + self.d
        self.slabs, self.wide = parts.shape[1], parts.shape[-1]

    def chip(self, k):
        return partner(self.e, k, self.sizes[1])

    def across(self, m, k):
        slot = m % 3
        return pltpu.make_async_remote_copy(
            src_ref=self.own.at[m], dst_ref=self.gath.at[slot, self.me],
            send_sem=self.x_send.at[slot, k - 1], recv_sem=self.x_recv.at[slot, k - 1],
            device_id={"expert": self.chip(k)}, device_id_type=MESH)

    def beside(self, m):
        slot = m % 3
        return pltpu.make_async_remote_copy(
            src_ref=self.own.at[m], dst_ref=self.gath.at[slot, self.me],
            send_sem=self.d_send.at[slot], recv_sem=self.d_recv.at[slot],
            device_id={"dp": 1 - self.d}, device_id_type=MESH)

    def onward(self, m, k):
        slot = m % 3
        block = self.chip(k) * 2 + self.d
        return pltpu.make_async_remote_copy(
            src_ref=self.gath.at[slot, block], dst_ref=self.gath.at[slot, block],
            send_sem=self.f_send.at[slot, k - 1], recv_sem=self.f_recv.at[slot, k - 1],
            device_id={"dp": 1 - self.d}, device_id_type=MESH)

    def share(self, m, j):
        slot = m % 2
        return pltpu.make_async_remote_copy(
            src_ref=self.parts.at[slot, j, 1 - self.d], dst_ref=self.stage.at[slot, j],
            send_sem=self.p_send.at[slot, j], recv_sem=self.p_recv.at[slot, j],
            device_id={"dp": 1 - self.d}, device_id_type=MESH)

    def give(self, m, j, k):
        slot = m % 2
        return pltpu.make_async_remote_copy(
            src_ref=self.sums.at[slot, j, k - 1], dst_ref=self.back.at[slot, j, k - 1],
            send_sem=self.r_send.at[slot, j, k - 1], recv_sem=self.r_recv.at[slot, j, k - 1],
            device_id={"expert": self.chip(k)}, device_id_type=MESH)

    def spread(self, m):
        for k in range(1, self.sizes[1]):
            self.across(m, k).start()
        self.beside(m).start()
        self.gath[m % 3, self.me] = self.own[m]

    def arrive(self, m, use):
        experts = self.sizes[1]
        use(self.me)
        self.beside(m).wait_recv()
        use(self.e * 2 + 1 - self.d)
        for k in range(1, experts):
            self.across(m, k).wait_recv()
            self.onward(m, k).start()
            use(self.chip(k) * 2 + self.d)
        for k in range(1, experts):
            self.onward(m, k).wait_recv()
            use(self.chip(k) * 2 + 1 - self.d)

    def passed_on(self, m):
        for k in range(1, self.sizes[1]):
            self.onward(m, k).wait_send()

    def settle(self, m, j, keep_own):
        slot = m % 2
        experts = self.sizes[1]
        self.share(m, j).wait_recv()
        for k in range(experts - 1, -1, -1):
            chip = self.chip(k)
            value = self.parts[slot, j, self.d, chip].astype(f32) + self.stage[slot, j, chip].astype(f32)
            if k == 0:
                keep_own(j, value)
            else:
                self.sums[slot, j, k - 1] = value.astype(bf16)
                self.give(m, j, k).start()

    def gathered(self, m):
        self.beside(m).wait_send()
        for k in range(1, self.sizes[1]):
            self.across(m, k).wait_send()

    def given(self, m):
        for j in range(self.slabs):
            for k in range(1, self.sizes[1]):
                self.give(m, j, k).wait_recv()

    def returned(self, m):
        for j in range(self.slabs):
            self.share(m, j).wait_send()
            for k in range(1, self.sizes[1]):
                self.give(m, j, k).wait_send()


def tall(router_t):
    rows = router_t[...].astype(f32)
    return jnp.concatenate([rows, jnp.zeros((lanes - rows.shape[0], rows.shape[1]), f32)], axis=0).astype(bf16)


def meet(sizes, step):
    sections, experts, cores = sizes
    s, e, d = lax.axis_index("section"), lax.axis_index("expert"), lax.axis_index("dp")
    me = e * cores + d
    first, last = (0, sections - 1) if step > 0 else (sections - 1, 0)
    barrier = pltpu.get_barrier_semaphore()
    count = experts * cores - 1
    for off in range(1, experts * cores):
        other = lax.rem(me + off, experts * cores)
        pl.semaphore_signal(
            barrier, inc=1, device_id={"expert": other // cores, "dp": lax.rem(other, cores)},
            device_id_type=MESH)

    @pl.when(s != first)
    def _():
        pl.semaphore_signal(barrier, inc=1, device_id={"section": s - step}, device_id_type=MESH)

    pl.semaphore_wait(barrier, count + (s != last).astype(jnp.int32))


def forward_kernel(sizes, tokens, ids, gate, up, down, router_t, head, labels,
                   normed_o, hid_o, dgate_o, dup_o, fac_o, gate_o, up_o, down_o, own, mix, slope_o, top_o, head_o, loss_o,
                   gate_v, up_v, down_v, gate_f, up_f, down_f, mask, mask_all, router, gath, parts, stage, sums, back, out_rows,
                   normed_t, hid_t, dgate_t, dup_t, fac_t, slope_t,
                   w_sem, f_sem, k_send, k_recv, t_sem, z_send, z_recv, o_sem, *sems):
    sections, experts, cores = sizes
    units, rows, width = own.shape
    hidden_dim = gate_v.shape[1]
    s = lax.axis_index("section")
    last = sections - 1
    ex = Exchange(sizes, own, gath, parts, stage, sums, back, sems)
    e, d, me = ex.e, ex.d, ex.me
    members = experts * cores
    every = members * rows
    slabs, slab = ex.slabs, ex.wide

    loads = [pltpu.make_async_copy(a, b, w_sem.at[n])
             for n, (a, b) in enumerate(((gate, gate_v), (up, up_v), (down, down_v)))]
    for load in loads:
        load.start()

    def take(m):
        return pltpu.make_async_copy(tokens.at[m], own.at[m], t_sem.at[m])

    @pl.when(s == 0)
    def _():
        for m in range(units):
            take(m).start()

    micro_count, _, micro_rows = ids.shape
    expert_row = lax.broadcasted_iota(jnp.int32, (lanes, micro_rows), 0)
    marks = []
    for n in range(micro_count):
        named = expert_row == ids[n, 0:1]
        for k in range(1, ids.shape[1]):
            named = named | (expert_row == ids[n, k:k + 1])
        marks.append(jnp.where(named, 1.0, 0.0).T)
    mask[...] = jnp.concatenate(marks, axis=0).astype(bf16).reshape(units, rows, lanes)
    router[...] = tall(router_t)
    meet(sizes, 1)

    def tell(off):
        other = lax.rem(me + off, members)
        return pltpu.make_async_remote_copy(
            src_ref=mask, dst_ref=mask_all.at[me], send_sem=k_send.at[off - 1], recv_sem=k_recv.at[off - 1],
            device_id={"expert": other // cores, "dp": lax.rem(other, cores)}, device_id_type=MESH)

    def shift(m):
        return pltpu.make_async_remote_copy(
            src_ref=out_rows.at[m], dst_ref=own.at[m], send_sem=z_send.at[m], recv_sem=z_recv.at[m],
            device_id={"section": lax.rem(s + 1, sections)}, device_id_type=MESH)

    def begin(m):
        @pl.when(s == 0)
        def _():
            take(m).wait()

        @pl.when(s != 0)
        def _():
            shift(m).wait_recv()

        ex.spread(m)

    def writes(m):
        side = m % 2
        pairs = ((normed_t, normed_o), (hid_t, hid_o), (dgate_t, dgate_o), (dup_t, dup_o), (fac_t, fac_o))
        return [pltpu.make_async_copy(a.at[side], b.at[m], o_sem.at[n, side])
                for n, (a, b) in enumerate(pairs)]

    lane = lax.broadcasted_iota(jnp.int32, (every, lanes), 1)

    def enter(m):
        slot = m % 2

        @pl.when(m >= 2)
        def _():
            for copy in writes(m):
                copy.wait()

        def norm_block(block):
            def norm(r, _):
                at = pl.ds(pl.multiple_of(r * row_step, row_step), row_step)
                values = gath[m % 3, block, at].astype(f32)
                inv = lax.rsqrt(jnp.mean(values * values, axis=-1, keepdims=True) + norm_eps)
                normed_t[slot, pl.ds(pl.multiple_of(block * rows + r * row_step, row_step), row_step)] = (
                    values * inv).astype(bf16)
                return 0
            lax.fori_loop(0, rows // row_step, norm, 0)

        ex.arrive(m, norm_block)

    def widen(m):
        slot = m % 2
        chosen = capped(contract_last(normed_t[slot], router[...]))
        named = mask_all[:, m].reshape(every, lanes).astype(f32)
        weights = jnp.exp(chosen) * named
        probs = weights / jnp.sum(weights, axis=-1, keepdims=True)
        scaled = chosen / soft_cap
        bend = 1.0 - scaled * scaled
        mine = jnp.sum(jnp.where(lane == me, probs, 0.0), axis=-1, keepdims=True)

        wide = 256 if hidden_dim % 256 == 0 else hidden_dim
        for j in range(0, hidden_dim, wide):
            cols = slice(j, j + wide)
            gate_act = dot_plain(normed_t[slot], gate_v[:, cols])
            up_act = dot_plain(normed_t[slot], up_v[:, cols])
            sig = jax.nn.sigmoid(gate_act)
            silu = mine * (gate_act * sig)
            hid_t[slot, :, cols] = (silu * up_act).astype(bf16)
            dgate_t[slot, :, cols] = (mine * up_act * sig * (1.0 + gate_act * (1.0 - sig))).astype(bf16)
            dup_t[slot, :, cols] = silu.astype(bf16)
        return probs, bend

    def narrow(m, probs, bend):
        slot = m % 2

        def keep(j, value):
            mix[m, :, j * slab:(j + 1) * slab] = value

        tile = 512 if slab % 512 == 0 else slab
        for j in range(slabs):
            for i in range(0, slab, tile):
                part = dot_plain(hid_t[slot], down_v[:, j * slab + i:j * slab + i + tile]).astype(bf16)
                part = part.reshape(experts, cores, rows, tile)
                for c in range(cores):
                    parts[slot, j, c, :, :, i:i + tile] = part[:, c]
            ex.share(m, j).start()
        fac_t[slot] = jnp.broadcast_to(
            jnp.sum(jnp.where(lane == me, bend, 0.0), axis=-1, keepdims=True), (every, lanes))
        slope_t[...] = (probs * bend).reshape(members, rows, lanes)
        slope_o[m] = slope_t[me]
        for copy in writes(m):
            copy.start()
        for j in range(slabs):
            ex.settle(m, j, keep)
        ex.passed_on(m)

        @pl.when(m >= 1)
        def _():
            ex.gathered(m - 1)
            ex.returned(m - 1)


    def finish(m):
        slot = m % 2
        ex.given(m)

        def total(r, _):
            at = pl.ds(pl.multiple_of(r * row_step, row_step), row_step)
            for j in range(slabs):
                cols = slice(j * slab, (j + 1) * slab)
                value = mix[m, at, cols]
                for k in range(1, experts):
                    value = value + back[slot, j, k - 1, at].astype(f32)
                mix[m, at, cols] = value
                out_rows[m, at, cols] = (own[m, at, cols].astype(f32) + value).astype(bf16)
            return 0
        lax.fori_loop(0, rows // row_step, total, 0)

        @pl.when(s != last)
        def _():
            shift(m).start()

    flips = [pltpu.make_async_copy(a, b, f_sem.at[n])
             for n, (a, b) in enumerate(((gate_f, gate_o), (up_f, up_o), (down_f, down_o)))]

    def turn(source, target):
        tall_by = 256 if source.shape[0] % 256 == 0 else source.shape[0]

        def step(r, _):
            at = pl.ds(pl.multiple_of(r * tall_by, tall_by), tall_by)
            target[:, at] = source[at].astype(f32).T.astype(bf16)
            return 0
        lax.fori_loop(0, source.shape[0] // tall_by, step, 0)

    def flip():
        turn(gate_v, gate_f)
        turn(up_v, up_f)
        turn(down_v, down_f)
        for copy in flips:
            copy.start()

    mask_all[me] = mask[...]
    for off in range(1, members):
        tell(off).start()

    @pl.when(s == 0)
    def _():
        begin(0)

    for load in loads:
        load.wait()

    @pl.when(s != 0)
    def _():
        flip()
        begin(0)

    for off in range(1, members):
        tell(off).wait()

    def unit(m, _):
        enter(m)

        @pl.when(m + 1 < units)
        def _():
            begin(m + 1)

        probs, bend = widen(m)

        @pl.when(m >= 1)
        def _():
            finish(m - 1)

        narrow(m, probs, bend)
        return 0

    lax.fori_loop(0, units, unit, 0)
    finish(units - 1)

    @pl.when(s == 0)
    def _():
        flip()

    ex.gathered(units - 1)
    ex.returned(units - 1)

    @pl.when(s != last)
    def _():
        head_o[...] = jnp.zeros_like(head_o)
        loss_o[...] = jnp.zeros_like(loss_o)
        for m in range(units):
            shift(m).wait_send()

    @pl.when(s == last)
    def _():
        final = out_rows[...].reshape(units * rows, width)
        class_logits = capped(dot_plain(final, head[...]))
        class_weights = jnp.exp(class_logits)
        class_total = jnp.sum(class_weights, axis=-1, keepdims=True)
        class_row = lax.broadcasted_iota(jnp.int32, (class_logits.shape[1], labels.shape[1]), 0)
        label_hot = jnp.concatenate(
            [jnp.where(class_row == labels[n:n + 1], 1.0, 0.0).T for n in range(labels.shape[0])], axis=0)
        loss = jnp.log(class_total) - jnp.sum(label_hot * class_logits, axis=-1, keepdims=True)
        scaled = class_logits / soft_cap
        grad_logits = ((class_weights / class_total - label_hot) * (1.0 - scaled * scaled)).astype(bf16)
        top_o[...] = contract_last(grad_logits, head[...]).astype(bf16).reshape(units, rows, width)
        head_o[...] = contract_first(final, grad_logits).reshape(head_o.shape).astype(bf16)
        loss_o[...] = jnp.full(loss_o.shape, jnp.sum(loss), f32)

    for m in range(max(0, units - 2), units):
        for copy in writes(m):
            copy.wait()
    for copy in flips:
        copy.wait()


def exchange_scratch(experts, cores, rows, width):
    slabs = 2 if width % 256 == 0 else 1
    slab = width // slabs
    return [
        pltpu.VMEM((3, experts * cores, rows, width), bf16),
        pltpu.VMEM((2, slabs, cores, experts, rows, slab), bf16),
        pltpu.VMEM((2, slabs, experts, rows, slab), bf16),
        pltpu.VMEM((2, slabs, experts - 1, rows, slab), bf16),
        pltpu.VMEM((2, slabs, experts - 1, rows, slab), bf16),
    ], [
        dma((3, experts - 1)), dma((3, experts - 1)), dma((3,)), dma((3,)),
        dma((3, experts - 1)), dma((3, experts - 1)), dma((2, slabs)), dma((2, slabs)),
        dma((2, slabs, experts - 1)), dma((2, slabs, experts - 1)),
    ]


def forward(sizes, tokens, ids, gate_w, up_w, down_w, router_t, head, labels):
    sections, experts, cores = sizes
    units, rows, width = tokens.shape
    hidden_dim = gate_w.shape[1]
    members = experts * cores
    every = members * rows
    vmem, hbm = pl.BlockSpec(memory_space=pltpu.VMEM), pl.BlockSpec(memory_space=pl.ANY)
    buffers, sems = exchange_scratch(experts, cores, rows, width)

    def shaped(shape, dtype):
        return jax.ShapeDtypeStruct(shape, dtype)

    acts = (units, every, hidden_dim)
    return pl.pallas_call(
        functools.partial(forward_kernel, sizes),
        out_shape=(
            shaped((units, every, width), bf16), shaped(acts, bf16), shaped(acts, bf16),
            shaped(acts, bf16), shaped((units, every, lanes), f32),
            shaped(gate_w.shape[::-1], bf16), shaped(up_w.shape[::-1], bf16), shaped(down_w.shape[::-1], bf16),
            shaped((units, rows, width), bf16), shaped((units, rows, width), f32),
            shaped((units, rows, lanes), f32), shaped((units, rows, width), bf16),
            shaped((members, width // members, head.shape[1]), bf16), shaped((8, lanes), f32),
        ),
        in_specs=[hbm, vmem, hbm, hbm, hbm, vmem, vmem, vmem],
        out_specs=(hbm,) * 8 + (vmem,) * 6,
        scratch_shapes=[
            pltpu.VMEM(gate_w.shape, bf16), pltpu.VMEM(up_w.shape, bf16), pltpu.VMEM(down_w.shape, bf16),
            pltpu.VMEM(gate_w.shape[::-1], bf16), pltpu.VMEM(up_w.shape[::-1], bf16),
            pltpu.VMEM(down_w.shape[::-1], bf16),
            pltpu.VMEM((units, rows, lanes), bf16), pltpu.VMEM((members, units, rows, lanes), bf16),
            pltpu.VMEM((lanes, width), bf16),
            *buffers,
            pltpu.VMEM((units, rows, width), bf16),
            pltpu.VMEM((2, every, width), bf16), pltpu.VMEM((2, every, hidden_dim), bf16),
            pltpu.VMEM((2, every, hidden_dim), bf16), pltpu.VMEM((2, every, hidden_dim), bf16),
            pltpu.VMEM((2, every, lanes), f32), pltpu.VMEM((members, rows, lanes), f32),
            dma((3,)), dma((3,)), dma((members - 1,)), dma((members - 1,)), dma((units,)),
            dma((units,)), dma((units,)), dma((5, 2)),
            *sems,
        ],
        cost_estimate=pl.CostEstimate(
            flops=6 * units * members * rows * width * hidden_dim, bytes_accessed=500_000_000, transcendentals=0),
        compiler_params=pltpu.CompilerParams(
            collective_id=0, has_side_effects=True, vmem_limit_bytes=56 * 1024 * 1024),
    )(tokens, ids, gate_w, up_w, down_w, router_t, head, labels)


def backward_kernel(sizes, top, hid, dgate, dup, fac, normed, own_in, mix, slope, gate, up, down, router_t, head_in, loss_in,
                    grad_o, agate_o, aup_o, router_o, head_o, mean_o,
                    gate_v, up_v, down_v, hid_v, dgate_v, dup_v, fac_v, normed_v, own, router, common, normed_own,
                    routed, parted, parted_all, head_part, head_all, loss_all, loss_o,
                    gath, parts, stage, sums, back, out_rows, total_v,
                    agate_t, aup_t, route_t,
                    w_sem, i_sem, t_sem, z_send, z_recv, o_sem, q_send, q_recv, h_send, h_recv, l_send, l_recv,
                    b_send, b_recv, c_send, c_recv, *sems):
    sections, experts, cores = sizes
    units, rows, width = own.shape
    hidden_dim = gate_v.shape[0]
    expert_count = router_t.shape[0]
    s = lax.axis_index("section")
    last = sections - 1
    ex = Exchange(sizes, own, gath, parts, stage, sums, back, sems)
    e, d, me = ex.e, ex.d, ex.me
    members = experts * cores
    every = members * rows
    slabs, slab = ex.slabs, ex.wide

    loads = [pltpu.make_async_copy(a, b, w_sem.at[n]) for n, (a, b) in enumerate((
        (down, down_v), (gate, gate_v), (up, up_v)))]

    def reads(m):
        side = m % 2
        pairs = ((hid, hid_v), (dgate, dgate_v), (dup, dup_v), (fac, fac_v), (normed, normed_v))
        return [pltpu.make_async_copy(a.at[m], b.at[side], i_sem.at[n, side]) for n, (a, b) in enumerate(pairs)]

    for load in loads:
        load.start()
    for m in range(min(2, units)):
        for copy in reads(m):
            copy.start()

    def take(m):
        return pltpu.make_async_copy(top.at[m], own.at[m], t_sem.at[m])

    @pl.when(s == last)
    def _():
        for m in range(units):
            take(m).start()

    router[...] = tall(router_t)
    routed[...] = jnp.zeros_like(routed)
    meet(sizes, -1)

    def other(off):
        to = lax.rem(me + off, members)
        return to, {"expert": to // cores, "dp": lax.rem(to, cores)}

    def head_piece(off):
        to, device = other(off)
        return pltpu.make_async_remote_copy(
            src_ref=head_in.at[to], dst_ref=head_part.at[me], send_sem=h_send.at[off - 1],
            recv_sem=h_recv.at[off - 1], device_id=device, device_id_type=MESH)

    def loss_piece(off):
        to, device = other(off)
        return pltpu.make_async_remote_copy(
            src_ref=loss_in, dst_ref=loss_all.at[me], send_sem=l_send.at[off - 1],
            recv_sem=l_recv.at[off - 1], device_id=device, device_id_type=MESH)

    def head_whole(off):
        to, device = other(off)
        return pltpu.make_async_remote_copy(
            src_ref=head_all.at[me], dst_ref=head_all.at[me], send_sem=b_send.at[off - 1],
            recv_sem=b_recv.at[off - 1], device_id=device, device_id_type=MESH)

    def router_part(off):
        to, device = other(off)
        return pltpu.make_async_remote_copy(
            src_ref=parted, dst_ref=parted_all.at[me], send_sem=q_send.at[off - 1],
            recv_sem=q_recv.at[off - 1], device_id=device, device_id_type=MESH)

    down_section = {"section": lax.rem(s + sections - 1, sections)}

    def chain():
        return [
            pltpu.make_async_remote_copy(
                src_ref=head_all.at[me], dst_ref=head_all.at[me], send_sem=c_send.at[0], recv_sem=c_recv.at[0],
                device_id=down_section, device_id_type=MESH),
            pltpu.make_async_remote_copy(
                src_ref=loss_o, dst_ref=loss_o, send_sem=c_send.at[1], recv_sem=c_recv.at[1],
                device_id=down_section, device_id_type=MESH),
        ]

    def head_sums():
        @pl.when(s == last)
        def _():
            for off in range(1, members):
                head_piece(off).start()
                loss_piece(off).start()
            head_part[me] = head_in[me]
            loss_all[me] = loss_in[...]
            for off in range(1, members):
                head_piece(off).wait()
                loss_piece(off).wait()
            value, loss = head_part[0].astype(f32), loss_all[0]
            for n in range(1, members):
                value, loss = value + head_part[n].astype(f32), loss + loss_all[n]
            head_all[me] = value.astype(bf16)
            loss_o[...] = loss

        @pl.when(s != last)
        def _():
            for copy in chain():
                copy.wait_recv()

        @pl.when(s != 0)
        def _():
            for copy in chain():
                copy.start()

        for off in range(1, members):
            head_whole(off).start()

    def shift(m):
        return pltpu.make_async_remote_copy(
            src_ref=out_rows.at[m], dst_ref=own.at[m], send_sem=z_send.at[m], recv_sem=z_recv.at[m],
            device_id={"section": lax.rem(s + sections - 1, sections)}, device_id_type=MESH)

    def begin(m):
        @pl.when(s == last)
        def _():
            take(m).wait()

        @pl.when(s != last)
        def _():
            shift(m).wait_recv()

        ex.spread(m)

    def writes(m):
        side = m % 2
        pairs = ((agate_t, agate_o), (aup_t, aup_o))
        return [pltpu.make_async_copy(a.at[side], b.at[m], o_sem.at[n, side])
                for n, (a, b) in enumerate(pairs)]

    def keep_grad(m):
        return pltpu.make_async_copy(gath.at[m % 3], grad_o.at[m], o_sem.at[2, 0])

    lane = lax.broadcasted_iota(jnp.int32, (every, lanes), 1)

    def widen(m):
        slot = m % 2

        @pl.when(m >= 2)
        def _():
            for copy in writes(m):
                copy.wait()

        for copy in reads(m):
            copy.wait()
        grads = gath[m % 3].reshape(every, width)
        gain = jnp.zeros((every, 1), f32)
        wide = 256 if hidden_dim % 256 == 0 else hidden_dim
        for j in range(0, hidden_dim, wide):
            cols = slice(j, j + wide)
            down_grad = dot_plain(grads, down_v[:, cols])
            agate_t[slot, :, cols] = (down_grad * dgate_v[slot, :, cols].astype(f32)).astype(bf16)
            aup_t[slot, :, cols] = (down_grad * dup_v[slot, :, cols].astype(f32)).astype(bf16)
            gain = gain + jnp.sum(down_grad * hid_v[slot, :, cols].astype(f32), axis=-1, keepdims=True)
        route_t[slot] = jnp.where(lane == me, gain * fac_v[slot], 0.0).astype(bf16)

    def record(m):
        slot = m % 2
        for copy in writes(m):
            copy.start()
        tile = 512 if width % 512 == 0 else width
        for i in range(0, width, tile):
            cols = slice(i, i + tile)
            routed[:, cols] = routed[:, cols] + contract_first(route_t[slot], normed_v[slot, :, cols])

    def tidy(m):
        @pl.when(m + 2 < units)
        def _():
            for copy in reads(m + 2):
                copy.start()

        ex.passed_on(m)

        @pl.when(m >= 1)
        def _():
            ex.gathered(m - 1)

        @pl.when((m >= 1) & (s != 0))
        def _():
            ex.returned(m - 1)

    def narrow(m):
        slot = m % 2

        def keep(j, value):
            total_v[slot, :, j * slab:(j + 1) * slab] = value

        tile = 512 if slab % 512 == 0 else slab
        for j in range(slabs):
            for i in range(0, slab, tile):
                cols = slice(j * slab + i, j * slab + i + tile)
                part = (dot_plain(agate_t[slot], gate_v[:, cols])
                        + dot_plain(aup_t[slot], up_v[:, cols])
                        + dot_plain(route_t[slot], router[:, cols]))
                part = part.astype(bf16).reshape(experts, cores, rows, tile)
                for c in range(cores):
                    parts[slot, j, c, :, :, i:i + tile] = part[:, c]
            ex.share(m, j).start()
        for j in range(slabs):
            ex.settle(m, j, keep)
        record(m)
        tidy(m)

    def finish(m):
        slot = m % 2

        grad_f = own[m].astype(f32)
        shared = jnp.sum(grad_f * mix[m], axis=-1, keepdims=True)
        common[m] = (slope[m] * shared).astype(bf16)
        hidden_f = own_in[m].astype(f32)
        inv_rms = lax.rsqrt(jnp.mean(hidden_f * hidden_f, axis=-1, keepdims=True) + norm_eps)
        normed_f = hidden_f * inv_rms
        normed_own[m] = normed_f.astype(bf16)

        @pl.when(s != 0)
        def _():
            total_v[slot] = total_v[slot] - dot_plain(common[m], router[...])
            ex.given(m)
            values = []
            for j in range(slabs):
                value = total_v[slot, :, j * slab:(j + 1) * slab]
                for k in range(1, experts):
                    value = value + back[slot, j, k - 1].astype(f32)
                values.append(value)
            grad_normed = jnp.concatenate(values, axis=-1)
            out_rows[m] = (
                own[m].astype(f32)
                + inv_rms * (grad_normed
                             - normed_f * jnp.mean(grad_normed * normed_f, axis=-1, keepdims=True))
            ).astype(bf16)
            shift(m).start()

    begin(0)
    for load in loads:
        load.wait()

    def unit(m, _):
        ex.arrive(m, lambda block: None)
        keep_grad(m).start()

        @pl.when(m + 1 < units)
        def _():
            begin(m + 1)

        @pl.when((s == 0) & (m == units - 1))
        def _():
            head_sums()

        widen(m)
        keep_grad(m).wait()

        @pl.when(m >= 1)
        def _():
            finish(m - 1)

        @pl.when(s != 0)
        def _():
            narrow(m)

        @pl.when(s == 0)
        def _():
            record(m)
            tidy(m)

        return 0

    lax.fori_loop(0, units, unit, 0)
    finish(units - 1)

    mine = routed[pl.ds(0, expert_count)] - contract_first(
        common[...].reshape(units * rows, lanes), normed_own[...].reshape(units * rows, width))[:expert_count]
    half = width // 2
    parted[...] = jnp.concatenate([mine[:, :half], mine[:, half:]], axis=0).astype(bf16)
    parted_all[me] = parted[...]
    for off in range(1, members):
        router_part(off).start()

    @pl.when(s != 0)
    def _():
        head_sums()
        ex.returned(units - 1)
        for m in range(units):
            shift(m).wait_send()
        for copy in chain():
            copy.wait_send()

    ex.gathered(units - 1)
    for off in range(1, members):
        head_whole(off).wait()
    head_o[...] = head_all[...].astype(f32)
    mean_o[0, 0] = loss_o[0, 0] / (units * every)
    for off in range(1, members):
        router_part(off).wait()
    value = parted_all[0].astype(f32)
    for n in range(1, members):
        value = value + parted_all[n].astype(f32)
    router_o[:, :half] = value[:expert_count]
    router_o[:, half:] = value[expert_count:]

    for m in range(max(0, units - 2), units):
        for copy in writes(m):
            copy.wait()


def backward(sizes, top, hid, dgate, dup, fac, normed, own_in, mix, slope, gate_w, up_w, down_w, router_t, head, loss):
    sections, experts, cores = sizes
    units, rows, width = top.shape
    hidden_dim = gate_w.shape[0]
    members = experts * cores
    every = members * rows
    vmem, hbm = pl.BlockSpec(memory_space=pltpu.VMEM), pl.BlockSpec(memory_space=pl.ANY)
    buffers, sems = exchange_scratch(experts, cores, rows, width)

    def shaped(shape, dtype):
        return jax.ShapeDtypeStruct(shape, dtype)

    acts = (units, every, hidden_dim)
    return pl.pallas_call(
        functools.partial(backward_kernel, sizes),
        out_shape=(
            shaped((units, members, rows, width), bf16), shaped(acts, bf16), shaped(acts, bf16),
            shaped(router_t.shape, f32), shaped(head.shape, f32), shaped((1, 1), f32),
        ),
        in_specs=[hbm] * 6 + [vmem] * 3 + [hbm] * 3 + [vmem] * 3,
        out_specs=(hbm,) * 3 + (vmem,) * 2 + (pl.BlockSpec(memory_space=pltpu.SMEM),),
        scratch_shapes=[
            pltpu.VMEM(gate_w.shape, bf16), pltpu.VMEM(up_w.shape, bf16), pltpu.VMEM(down_w.shape, bf16),
            pltpu.VMEM((2, every, hidden_dim), bf16), pltpu.VMEM((2, every, hidden_dim), bf16),
            pltpu.VMEM((2, every, hidden_dim), bf16), pltpu.VMEM((2, every, lanes), f32),
            pltpu.VMEM((2, every, width), bf16), pltpu.VMEM((units, rows, width), bf16),
            pltpu.VMEM((lanes, width), bf16), pltpu.VMEM((units, rows, lanes), bf16),
            pltpu.VMEM((units, rows, width), bf16),
            pltpu.VMEM((lanes, width), f32), pltpu.VMEM((2 * router_t.shape[0], width // 2), bf16),
            pltpu.VMEM((members, 2 * router_t.shape[0], width // 2), bf16),
            pltpu.VMEM(head.shape, bf16), pltpu.VMEM(head.shape, bf16), pltpu.VMEM((members,) + loss.shape, f32),
            pltpu.VMEM(loss.shape, f32),
            *buffers,
            pltpu.VMEM((units, rows, width), bf16), pltpu.VMEM((2, rows, width), f32),
            pltpu.VMEM((2, every, hidden_dim), bf16), pltpu.VMEM((2, every, hidden_dim), bf16),
            pltpu.VMEM((2, every, lanes), bf16),
            dma((3,)), dma((5, 2)), dma((units,)), dma((units,)), dma((units,)), dma((3, 2)),
            *[dma((members - 1,))] * 8, dma((2,)), dma((2,)),
            *sems,
        ],
        cost_estimate=pl.CostEstimate(
            flops=6 * units * members * rows * width * hidden_dim, bytes_accessed=500_000_000, transcendentals=0),
        compiler_params=pltpu.CompilerParams(
            collective_id=1, has_side_effects=True, vmem_limit_bytes=56 * 1024 * 1024),
    )(top, hid, dgate, dup, fac, normed, own_in, mix, slope, gate_w, up_w, down_w, router_t, head, loss)


def shards(sizes, tokens, expert_ids, labels, router, class_head, w_gate, w_up, w_down):
    sections, experts, cores = sizes
    members = experts * cores
    micro_count, tok_rows, width = tokens.shape
    gate_w, up_w, down_w = w_gate[0, 0], w_up[0, 0], w_down[0, 0]
    hidden_dim = gate_w.shape[1]
    rows = max(row_step, min(tok_rows, tok_rows * 2 // members))
    units = micro_count * tok_rows // rows

    router_t = router[0].T
    ids = jnp.transpose(expert_ids[0], (0, 2, 1))
    normed, hid, dgate, dup, fac, gate_f, up_f, down_f, own_in, mix, slope, top, head_term, loss_term = forward(
        sizes, tokens.reshape(units, rows, width), ids, gate_w, up_w, down_w, router_t, class_head,
        labels)
    grad_all, agate, aup, router_sum, head_total, mean_loss = backward(
        sizes, top, hid, dgate, dup, fac, normed, own_in, mix, slope, gate_f, up_f, down_f, router_t,
        head_term, loss_term)

    every = units * members * rows
    normed = normed.reshape(every, width)
    grad_gate = contract_first(normed, agate.reshape(every, hidden_dim)).astype(bf16)
    grad_up = contract_first(normed, aup.reshape(every, hidden_dim)).astype(bf16)
    grad_down = contract_first(hid.reshape(every, hidden_dim), grad_all.reshape(every, width)).astype(bf16)
    return (
        mean_loss.reshape(()),
        head_total.reshape(width, -1),
        router_sum.T[None],
        grad_gate[None, None],
        grad_up[None, None],
        grad_down[None, None],
    )


def solution(mesh):
    sizes = tuple(mesh.shape[axis] for axis in ("section", "expert", "dp"))
    return jax.shard_map(
        functools.partial(shards, sizes),
        mesh=mesh,
        in_specs=(
            P(None, ("expert", "dp"), None),
            P("section", None, ("expert", "dp"), None),
            P(None, ("expert", "dp")),
            P("section", None, None),
            P(),
            P("section", ("expert", "dp"), None, None),
            P("section", ("expert", "dp"), None, None),
            P("section", ("expert", "dp"), None, None),
        ),
        out_specs=(
            P(),
            P(),
            P("section", None, None),
            P("section", ("expert", "dp"), None, None),
            P("section", ("expert", "dp"), None, None),
            P("section", ("expert", "dp"), None, None),
        ),
        check_vma=False,
    )
```

```python
import functools

import jax
import jax.numpy as jnp
from jax import lax
from jax.experimental import pallas as pl
from jax.experimental.pallas import tpu as pltpu
from jax.sharding import PartitionSpec as P

soft_cap = 30.0
norm_eps = 1e-06
lanes = 128
row_step = 16
MESH = pl.DeviceIdType.MESH
dma = pltpu.SemaphoreType.DMA
bf16 = jnp.bfloat16
f32 = jnp.float32


def capped(values):
    return soft_cap * jnp.tanh(values / soft_cap)


def dot_plain(left, right):
    return jnp.dot(left, right, preferred_element_type=f32)


def contract_first(left, right):
    return lax.dot_general(left, right, (((0,), (0,)), ((), ())), preferred_element_type=f32)


def contract_last(left, right):
    return lax.dot_general(left, right, (((1,), (1,)), ((), ())), preferred_element_type=f32)


def partner(e, k, count):
    total, bit = 0, 1
    while bit < count:
        a, b = (e // bit) % 2, (k // bit) % 2
        total = total + (a + b - 2 * a * b) * bit
        bit *= 2
    return total


class Exchange:
    def __init__(self, sizes, own, gath, parts, stage, sums, back, sems):
        self.sizes, self.own, self.gath = sizes, own, gath
        self.parts, self.stage, self.sums, self.back = parts, stage, sums, back
        (self.x_send, self.x_recv, self.d_send, self.d_recv, self.f_send, self.f_recv,
         self.p_send, self.p_recv, self.r_send, self.r_recv) = sems
        self.e, self.d = lax.axis_index("expert"), lax.axis_index("dp")
        self.me = self.e * 2 + self.d
        self.slabs, self.wide = parts.shape[1], parts.shape[-1]

    def chip(self, k):
        return partner(self.e, k, self.sizes[1])

    def across(self, m, k):
        slot = m % 3
        return pltpu.make_async_remote_copy(
            src_ref=self.own.at[m], dst_ref=self.gath.at[slot, self.me],
            send_sem=self.x_send.at[slot, k - 1], recv_sem=self.x_recv.at[slot, k - 1],
            device_id={"expert": self.chip(k)}, device_id_type=MESH)

    def beside(self, m):
        slot = m % 3
        return pltpu.make_async_remote_copy(
            src_ref=self.own.at[m], dst_ref=self.gath.at[slot, self.me],
            send_sem=self.d_send.at[slot], recv_sem=self.d_recv.at[slot],
            device_id={"dp": 1 - self.d}, device_id_type=MESH)

    def onward(self, m, k):
        slot = m % 3
        block = self.chip(k) * 2 + self.d
        return pltpu.make_async_remote_copy(
            src_ref=self.gath.at[slot, block], dst_ref=self.gath.at[slot, block],
            send_sem=self.f_send.at[slot, k - 1], recv_sem=self.f_recv.at[slot, k - 1],
            device_id={"dp": 1 - self.d}, device_id_type=MESH)

    def share(self, m, j):
        slot = m % 2
        return pltpu.make_async_remote_copy(
            src_ref=self.parts.at[slot, j, 1 - self.d], dst_ref=self.stage.at[slot, j],
            send_sem=self.p_send.at[slot, j], recv_sem=self.p_recv.at[slot, j],
            device_id={"dp": 1 - self.d}, device_id_type=MESH)

    def give(self, m, j, k):
        slot = m % 2
        return pltpu.make_async_remote_copy(
            src_ref=self.sums.at[slot, j, k - 1], dst_ref=self.back.at[slot, j, k - 1],
            send_sem=self.r_send.at[slot, j, k - 1], recv_sem=self.r_recv.at[slot, j, k - 1],
            device_id={"expert": self.chip(k)}, device_id_type=MESH)

    def spread(self, m):
        for k in sorted(range(1, self.sizes[1]), key=lambda k: -bin(k).count("1")):
            self.across(m, k).start()
        self.beside(m).start()
        self.gath[m % 3, self.me] = self.own[m]

    def arrive(self, m, use):
        experts = self.sizes[1]
        use(self.me)
        self.beside(m).wait_recv()
        use(self.e * 2 + 1 - self.d)
        for k in range(1, experts):
            self.across(m, k).wait_recv()
            self.onward(m, k).start()
            use(self.chip(k) * 2 + self.d)
        for k in range(1, experts):
            self.onward(m, k).wait_recv()
            use(self.chip(k) * 2 + 1 - self.d)

    def passed_on(self, m):
        for k in range(1, self.sizes[1]):
            self.onward(m, k).wait_send()

    def settle(self, m, j, keep_own):
        slot = m % 2
        experts = self.sizes[1]
        self.share(m, j).wait_recv()
        for k in range(experts - 1, -1, -1):
            chip = self.chip(k)
            value = self.parts[slot, j, self.d, chip].astype(f32) + self.stage[slot, j, chip].astype(f32)
            if k == 0:
                keep_own(j, value)
            else:
                self.sums[slot, j, k - 1] = value.astype(bf16)
                self.give(m, j, k).start()

    def gathered(self, m):
        self.beside(m).wait_send()
        for k in range(1, self.sizes[1]):
            self.across(m, k).wait_send()

    def given(self, m):
        for j in range(self.slabs):
            for k in range(1, self.sizes[1]):
                self.give(m, j, k).wait_recv()

    def returned(self, m):
        for j in range(self.slabs):
            self.share(m, j).wait_send()
            for k in range(1, self.sizes[1]):
                self.give(m, j, k).wait_send()


def tall(router_t):
    rows = router_t[...].astype(f32)
    return jnp.concatenate([rows, jnp.zeros((lanes - rows.shape[0], rows.shape[1]), f32)], axis=0).astype(bf16)


def meet(sizes, step):
    sections, experts, cores = sizes
    s, e, d = lax.axis_index("section"), lax.axis_index("expert"), lax.axis_index("dp")
    me = e * cores + d
    first, last = (0, sections - 1) if step > 0 else (sections - 1, 0)
    barrier = pltpu.get_barrier_semaphore()
    count = experts * cores - 1
    for off in range(1, experts * cores):
        other = lax.rem(me + off, experts * cores)
        pl.semaphore_signal(
            barrier, inc=1, device_id={"expert": other // cores, "dp": lax.rem(other, cores)},
            device_id_type=MESH)

    @pl.when(s != first)
    def _():
        pl.semaphore_signal(barrier, inc=1, device_id={"section": s - step}, device_id_type=MESH)

    pl.semaphore_wait(barrier, count + (s != last).astype(jnp.int32))


def forward_kernel(sizes, tokens, ids, gate, up, down, router_t, head, labels,
                   normed_o, hid_o, dgate_o, dup_o, fac_o, gate_o, up_o, down_o, own, mix, slope_o, top_o, head_o, loss_o,
                   gate_v, up_v, down_v, gate_f, up_f, down_f, mask, mask_all, router, gath, parts, stage, sums, back, out_rows,
                   normed_t, hid_t, dgate_t, dup_t, fac_t, slope_t,
                   w_sem, f_sem, k_send, k_recv, t_sem, z_send, z_recv, o_sem, *sems):
    sections, experts, cores = sizes
    units, rows, width = own.shape
    hidden_dim = gate_v.shape[1]
    s = lax.axis_index("section")
    last = sections - 1
    ex = Exchange(sizes, own, gath, parts, stage, sums, back, sems)
    e, d, me = ex.e, ex.d, ex.me
    members = experts * cores
    every = members * rows
    slabs, slab = ex.slabs, ex.wide

    loads = [pltpu.make_async_copy(a, b, w_sem.at[n])
             for n, (a, b) in enumerate(((gate, gate_v), (up, up_v), (down, down_v)))]
    for load in loads:
        load.start()

    def take(m):
        return pltpu.make_async_copy(tokens.at[m], own.at[m], t_sem.at[m])

    @pl.when(s == 0)
    def _():
        for m in range(units):
            take(m).start()

    micro_count, _, micro_rows = ids.shape
    expert_row = lax.broadcasted_iota(jnp.int32, (lanes, micro_rows), 0)
    marks = []
    for n in range(micro_count):
        named = expert_row == ids[n, 0:1]
        for k in range(1, ids.shape[1]):
            named = named | (expert_row == ids[n, k:k + 1])
        marks.append(jnp.where(named, 1.0, 0.0).T)
    mask[...] = jnp.concatenate(marks, axis=0).astype(bf16).reshape(units, rows, lanes)
    router[...] = tall(router_t)
    meet(sizes, 1)

    def tell(off):
        other = lax.rem(me + off, members)
        return pltpu.make_async_remote_copy(
            src_ref=mask, dst_ref=mask_all.at[me], send_sem=k_send.at[off - 1], recv_sem=k_recv.at[off - 1],
            device_id={"expert": other // cores, "dp": lax.rem(other, cores)}, device_id_type=MESH)

    def shift(m):
        return pltpu.make_async_remote_copy(
            src_ref=out_rows.at[m], dst_ref=own.at[m], send_sem=z_send.at[m], recv_sem=z_recv.at[m],
            device_id={"section": lax.rem(s + 1, sections)}, device_id_type=MESH)

    def begin(m):
        @pl.when(s == 0)
        def _():
            take(m).wait()

        @pl.when(s != 0)
        def _():
            shift(m).wait_recv()

        ex.spread(m)

    def writes(m):
        side = m % 2
        pairs = ((normed_t, normed_o), (hid_t, hid_o), (dgate_t, dgate_o), (dup_t, dup_o), (fac_t, fac_o))
        return [pltpu.make_async_copy(a.at[side], b.at[m], o_sem.at[n, side])
                for n, (a, b) in enumerate(pairs)]

    lane = lax.broadcasted_iota(jnp.int32, (every, lanes), 1)

    def enter(m):
        slot = m % 2

        @pl.when(m >= 2)
        def _():
            for copy in writes(m):
                copy.wait()

        def norm_block(block):
            def norm(r, _):
                at = pl.ds(pl.multiple_of(r * row_step, row_step), row_step)
                values = gath[m % 3, block, at].astype(f32)
                inv = lax.rsqrt(jnp.mean(values * values, axis=-1, keepdims=True) + norm_eps)
                normed_t[slot, pl.ds(pl.multiple_of(block * rows + r * row_step, row_step), row_step)] = (
                    values * inv).astype(bf16)
                return 0
            lax.fori_loop(0, rows // row_step, norm, 0)

        ex.arrive(m, norm_block)

    def widen(m):
        slot = m % 2
        chosen = capped(contract_last(normed_t[slot], router[...]))
        named = mask_all[:, m].reshape(every, lanes).astype(f32)
        weights = jnp.exp(chosen) * named
        probs = weights / jnp.sum(weights, axis=-1, keepdims=True)
        scaled = chosen / soft_cap
        bend = 1.0 - scaled * scaled
        mine = jnp.sum(jnp.where(lane == me, probs, 0.0), axis=-1, keepdims=True)

        wide = 256 if hidden_dim % 256 == 0 else hidden_dim
        for j in range(0, hidden_dim, wide):
            cols = slice(j, j + wide)
            gate_act = dot_plain(normed_t[slot], gate_v[:, cols])
            up_act = dot_plain(normed_t[slot], up_v[:, cols])
            sig = jax.nn.sigmoid(gate_act)
            silu = mine * (gate_act * sig)
            hid_t[slot, :, cols] = (silu * up_act).astype(bf16)
            dgate_t[slot, :, cols] = (mine * up_act * sig * (1.0 + gate_act * (1.0 - sig))).astype(bf16)
            dup_t[slot, :, cols] = silu.astype(bf16)
        return probs, bend

    def narrow(m, probs, bend):
        slot = m % 2

        def keep(j, value):
            mix[m, :, j * slab:(j + 1) * slab] = value

        tile = 512 if slab % 512 == 0 else slab
        for j in range(slabs):
            for i in range(0, slab, tile):
                part = dot_plain(hid_t[slot], down_v[:, j * slab + i:j * slab + i + tile]).astype(bf16)
                part = part.reshape(experts, cores, rows, tile)
                for c in range(cores):
                    parts[slot, j, c, :, :, i:i + tile] = part[:, c]
            ex.share(m, j).start()
        for j in range(slabs):
            ex.settle(m, j, keep)
        fac_t[slot] = jnp.broadcast_to(
            jnp.sum(jnp.where(lane == me, bend, 0.0), axis=-1, keepdims=True), (every, lanes))
        slope_t[...] = (probs * bend).reshape(members, rows, lanes)
        slope_o[m] = slope_t[me]
        for copy in writes(m):
            copy.start()
        ex.passed_on(m)

        @pl.when(m >= 1)
        def _():
            ex.gathered(m - 1)
            ex.returned(m - 1)


    def finish(m):
        slot = m % 2
        ex.given(m)

        def total(r, _):
            at = pl.ds(pl.multiple_of(r * row_step, row_step), row_step)
            for j in range(slabs):
                cols = slice(j * slab, (j + 1) * slab)
                value = mix[m, at, cols]
                for k in range(1, experts):
                    value = value + back[slot, j, k - 1, at].astype(f32)
                mix[m, at, cols] = value
                out_rows[m, at, cols] = (own[m, at, cols].astype(f32) + value).astype(bf16)
            return 0
        lax.fori_loop(0, rows // row_step, total, 0)

        @pl.when(s != last)
        def _():
            shift(m).start()

    flips = [pltpu.make_async_copy(a, b, f_sem.at[n])
             for n, (a, b) in enumerate(((gate_f, gate_o), (up_f, up_o), (down_f, down_o)))]

    def turn(source, target):
        tall_by = 256 if source.shape[0] % 256 == 0 else source.shape[0]

        def step(r, _):
            at = pl.ds(pl.multiple_of(r * tall_by, tall_by), tall_by)
            target[:, at] = source[at].astype(f32).T.astype(bf16)
            return 0
        lax.fori_loop(0, source.shape[0] // tall_by, step, 0)

    def flip():
        turn(gate_v, gate_f)
        turn(up_v, up_f)
        turn(down_v, down_f)
        for copy in flips:
            copy.start()

    mask_all[me] = mask[...]
    for off in range(1, members):
        tell(off).start()

    @pl.when(s == 0)
    def _():
        begin(0)

    for load in loads:
        load.wait()

    @pl.when(s != 0)
    def _():
        flip()
        begin(0)

    for off in range(1, members):
        tell(off).wait()

    def unit(m, _):
        enter(m)

        @pl.when(m + 1 < units)
        def _():
            begin(m + 1)

        probs, bend = widen(m)

        @pl.when(m >= 1)
        def _():
            finish(m - 1)

        narrow(m, probs, bend)
        return 0

    lax.fori_loop(0, units, unit, 0)
    finish(units - 1)

    @pl.when(s == 0)
    def _():
        flip()

    ex.gathered(units - 1)
    ex.returned(units - 1)

    @pl.when(s != last)
    def _():
        head_o[...] = jnp.zeros_like(head_o)
        loss_o[...] = jnp.zeros_like(loss_o)
        for m in range(units):
            shift(m).wait_send()

    @pl.when(s == last)
    def _():
        final = out_rows[...].reshape(units * rows, width)
        class_logits = capped(dot_plain(final, head[...]))
        class_weights = jnp.exp(class_logits)
        class_total = jnp.sum(class_weights, axis=-1, keepdims=True)
        class_row = lax.broadcasted_iota(jnp.int32, (class_logits.shape[1], labels.shape[1]), 0)
        label_hot = jnp.concatenate(
            [jnp.where(class_row == labels[n:n + 1], 1.0, 0.0).T for n in range(labels.shape[0])], axis=0)
        loss = jnp.log(class_total) - jnp.sum(label_hot * class_logits, axis=-1, keepdims=True)
        scaled = class_logits / soft_cap
        grad_logits = ((class_weights / class_total - label_hot) * (1.0 - scaled * scaled)).astype(bf16)
        top_o[...] = contract_last(grad_logits, head[...]).astype(bf16).reshape(units, rows, width)
        head_o[...] = contract_first(final, grad_logits).reshape(head_o.shape).astype(bf16)
        loss_o[...] = jnp.full(loss_o.shape, jnp.sum(loss), f32)

    for m in range(max(0, units - 2), units):
        for copy in writes(m):
            copy.wait()
    for copy in flips:
        copy.wait()


def exchange_scratch(experts, cores, rows, width):
    slabs = 2 if width % 256 == 0 else 1
    slab = width // slabs
    return [
        pltpu.VMEM((3, experts * cores, rows, width), bf16),
        pltpu.VMEM((2, slabs, cores, experts, rows, slab), bf16),
        pltpu.VMEM((2, slabs, experts, rows, slab), bf16),
        pltpu.VMEM((2, slabs, experts - 1, rows, slab), bf16),
        pltpu.VMEM((2, slabs, experts - 1, rows, slab), bf16),
    ], [
        dma((3, experts - 1)), dma((3, experts - 1)), dma((3,)), dma((3,)),
        dma((3, experts - 1)), dma((3, experts - 1)), dma((2, slabs)), dma((2, slabs)),
        dma((2, slabs, experts - 1)), dma((2, slabs, experts - 1)),
    ]


def forward(sizes, tokens, ids, gate_w, up_w, down_w, router_t, head, labels):
    sections, experts, cores = sizes
    units, rows, width = tokens.shape
    hidden_dim = gate_w.shape[1]
    members = experts * cores
    every = members * rows
    vmem, hbm = pl.BlockSpec(memory_space=pltpu.VMEM), pl.BlockSpec(memory_space=pl.ANY)
    buffers, sems = exchange_scratch(experts, cores, rows, width)

    def shaped(shape, dtype):
        return jax.ShapeDtypeStruct(shape, dtype)

    acts = (units, every, hidden_dim)
    return pl.pallas_call(
        functools.partial(forward_kernel, sizes),
        out_shape=(
            shaped((units, every, width), bf16), shaped(acts, bf16), shaped(acts, bf16),
            shaped(acts, bf16), shaped((units, every, lanes), f32),
            shaped(gate_w.shape[::-1], bf16), shaped(up_w.shape[::-1], bf16), shaped(down_w.shape[::-1], bf16),
            shaped((units, rows, width), bf16), shaped((units, rows, width), f32),
            shaped((units, rows, lanes), f32), shaped((units, rows, width), bf16),
            shaped((members, width // members, head.shape[1]), bf16), shaped((8, lanes), f32),
        ),
        in_specs=[hbm, vmem, hbm, hbm, hbm, vmem, vmem, vmem],
        out_specs=(hbm,) * 8 + (vmem,) * 6,
        scratch_shapes=[
            pltpu.VMEM(gate_w.shape, bf16), pltpu.VMEM(up_w.shape, bf16), pltpu.VMEM(down_w.shape, bf16),
            pltpu.VMEM(gate_w.shape[::-1], bf16), pltpu.VMEM(up_w.shape[::-1], bf16),
            pltpu.VMEM(down_w.shape[::-1], bf16),
            pltpu.VMEM((units, rows, lanes), bf16), pltpu.VMEM((members, units, rows, lanes), bf16),
            pltpu.VMEM((lanes, width), bf16),
            *buffers,
            pltpu.VMEM((units, rows, width), bf16),
            pltpu.VMEM((2, every, width), bf16), pltpu.VMEM((2, every, hidden_dim), bf16),
            pltpu.VMEM((2, every, hidden_dim), bf16), pltpu.VMEM((2, every, hidden_dim), bf16),
            pltpu.VMEM((2, every, lanes), f32), pltpu.VMEM((members, rows, lanes), f32),
            dma((3,)), dma((3,)), dma((members - 1,)), dma((members - 1,)), dma((units,)),
            dma((units,)), dma((units,)), dma((5, 2)),
            *sems,
        ],
        cost_estimate=pl.CostEstimate(
            flops=6 * units * members * rows * width * hidden_dim, bytes_accessed=500_000_000, transcendentals=0),
        compiler_params=pltpu.CompilerParams(
            collective_id=0, has_side_effects=True, vmem_limit_bytes=56 * 1024 * 1024),
    )(tokens, ids, gate_w, up_w, down_w, router_t, head, labels)


def backward_kernel(sizes, top, hid, dgate, dup, fac, normed, own_in, mix, slope, gate, up, down, router_t, head_in, loss_in,
                    grad_o, agate_o, aup_o, router_o, head_o, mean_o,
                    gate_v, up_v, down_v, hid_v, dgate_v, dup_v, fac_v, normed_v, own, router, common, normed_own,
                    routed, parted, parted_all, head_part, head_all, loss_all, loss_o,
                    gath, parts, stage, sums, back, out_rows, total_v,
                    agate_t, aup_t, route_t,
                    w_sem, i_sem, t_sem, z_send, z_recv, o_sem, q_send, q_recv, h_send, h_recv, l_send, l_recv,
                    b_send, b_recv, c_send, c_recv, *sems):
    sections, experts, cores = sizes
    units, rows, width = own.shape
    hidden_dim = gate_v.shape[0]
    expert_count = router_t.shape[0]
    s = lax.axis_index("section")
    last = sections - 1
    ex = Exchange(sizes, own, gath, parts, stage, sums, back, sems)
    e, d, me = ex.e, ex.d, ex.me
    members = experts * cores
    every = members * rows
    slabs, slab = ex.slabs, ex.wide

    loads = [pltpu.make_async_copy(a, b, w_sem.at[n]) for n, (a, b) in enumerate((
        (down, down_v), (gate, gate_v), (up, up_v)))]

    def reads(m):
        side = m % 2
        pairs = ((hid, hid_v), (dgate, dgate_v), (dup, dup_v), (fac, fac_v), (normed, normed_v))
        return [pltpu.make_async_copy(a.at[m], b.at[side], i_sem.at[n, side]) for n, (a, b) in enumerate(pairs)]

    for load in loads:
        load.start()
    for m in range(min(2, units)):
        for copy in reads(m):
            copy.start()

    def take(m):
        return pltpu.make_async_copy(top.at[m], own.at[m], t_sem.at[m])

    @pl.when(s == last)
    def _():
        for m in range(units):
            take(m).start()

    router[...] = tall(router_t)
    routed[...] = jnp.zeros_like(routed)
    meet(sizes, -1)

    def other(off):
        to = lax.rem(me + off, members)
        return to, {"expert": to // cores, "dp": lax.rem(to, cores)}

    def head_piece(off):
        to, device = other(off)
        return pltpu.make_async_remote_copy(
            src_ref=head_in.at[to], dst_ref=head_part.at[me], send_sem=h_send.at[off - 1],
            recv_sem=h_recv.at[off - 1], device_id=device, device_id_type=MESH)

    def loss_piece(off):
        to, device = other(off)
        return pltpu.make_async_remote_copy(
            src_ref=loss_in, dst_ref=loss_all.at[me], send_sem=l_send.at[off - 1],
            recv_sem=l_recv.at[off - 1], device_id=device, device_id_type=MESH)

    def head_whole(off):
        to, device = other(off)
        return pltpu.make_async_remote_copy(
            src_ref=head_all.at[me], dst_ref=head_all.at[me], send_sem=b_send.at[off - 1],
            recv_sem=b_recv.at[off - 1], device_id=device, device_id_type=MESH)

    def router_part(off):
        to, device = other(off)
        return pltpu.make_async_remote_copy(
            src_ref=parted, dst_ref=parted_all.at[me], send_sem=q_send.at[off - 1],
            recv_sem=q_recv.at[off - 1], device_id=device, device_id_type=MESH)

    down_section = {"section": lax.rem(s + sections - 1, sections)}

    def chain():
        return [
            pltpu.make_async_remote_copy(
                src_ref=head_all.at[me], dst_ref=head_all.at[me], send_sem=c_send.at[0], recv_sem=c_recv.at[0],
                device_id=down_section, device_id_type=MESH),
            pltpu.make_async_remote_copy(
                src_ref=loss_o, dst_ref=loss_o, send_sem=c_send.at[1], recv_sem=c_recv.at[1],
                device_id=down_section, device_id_type=MESH),
        ]

    def head_sums():
        @pl.when(s == last)
        def _():
            for off in range(1, members):
                head_piece(off).start()
                loss_piece(off).start()
            head_part[me] = head_in[me]
            loss_all[me] = loss_in[...]
            for off in range(1, members):
                head_piece(off).wait()
                loss_piece(off).wait()
            value, loss = head_part[0].astype(f32), loss_all[0]
            for n in range(1, members):
                value, loss = value + head_part[n].astype(f32), loss + loss_all[n]
            head_all[me] = value.astype(bf16)
            loss_o[...] = loss

        @pl.when(s != last)
        def _():
            for copy in chain():
                copy.wait_recv()

        @pl.when(s != 0)
        def _():
            for copy in chain():
                copy.start()

        for off in range(1, members):
            head_whole(off).start()

    def shift(m):
        return pltpu.make_async_remote_copy(
            src_ref=out_rows.at[m], dst_ref=own.at[m], send_sem=z_send.at[m], recv_sem=z_recv.at[m],
            device_id={"section": lax.rem(s + sections - 1, sections)}, device_id_type=MESH)

    def begin(m):
        @pl.when(s == last)
        def _():
            take(m).wait()

        @pl.when(s != last)
        def _():
            shift(m).wait_recv()

        ex.spread(m)

    def writes(m):
        side = m % 2
        pairs = ((agate_t, agate_o), (aup_t, aup_o))
        return [pltpu.make_async_copy(a.at[side], b.at[m], o_sem.at[n, side])
                for n, (a, b) in enumerate(pairs)]

    def keep_grad(m):
        return pltpu.make_async_copy(gath.at[m % 3], grad_o.at[m], o_sem.at[2, 0])

    lane = lax.broadcasted_iota(jnp.int32, (every, lanes), 1)

    def widen(m):
        slot = m % 2

        @pl.when(m >= 2)
        def _():
            for copy in writes(m):
                copy.wait()

        for copy in reads(m):
            copy.wait()
        grads = gath[m % 3].reshape(every, width)
        gain = jnp.zeros((every, 1), f32)
        wide = 256 if hidden_dim % 256 == 0 else hidden_dim
        for j in range(0, hidden_dim, wide):
            cols = slice(j, j + wide)
            down_grad = dot_plain(grads, down_v[:, cols])
            agate_t[slot, :, cols] = (down_grad * dgate_v[slot, :, cols].astype(f32)).astype(bf16)
            aup_t[slot, :, cols] = (down_grad * dup_v[slot, :, cols].astype(f32)).astype(bf16)
            gain = gain + jnp.sum(down_grad * hid_v[slot, :, cols].astype(f32), axis=-1, keepdims=True)
        route_t[slot] = jnp.where(lane == me, gain * fac_v[slot], 0.0).astype(bf16)

    def record(m):
        slot = m % 2
        for copy in writes(m):
            copy.start()
        tile = 512 if width % 512 == 0 else width
        for i in range(0, width, tile):
            cols = slice(i, i + tile)
            routed[:, cols] = routed[:, cols] + contract_first(route_t[slot], normed_v[slot, :, cols])

    def tidy(m):
        @pl.when(m + 2 < units)
        def _():
            for copy in reads(m + 2):
                copy.start()

        ex.passed_on(m)

        @pl.when(m >= 1)
        def _():
            ex.gathered(m - 1)

        @pl.when((m >= 1) & (s != 0))
        def _():
            ex.returned(m - 1)

    def narrow(m):
        slot = m % 2

        def keep(j, value):
            total_v[slot, :, j * slab:(j + 1) * slab] = value

        tile = 512 if slab % 512 == 0 else slab
        for j in range(slabs):
            for i in range(0, slab, tile):
                cols = slice(j * slab + i, j * slab + i + tile)
                part = (dot_plain(agate_t[slot], gate_v[:, cols])
                        + dot_plain(aup_t[slot], up_v[:, cols])
                        + dot_plain(route_t[slot], router[:, cols]))
                part = part.astype(bf16).reshape(experts, cores, rows, tile)
                for c in range(cores):
                    parts[slot, j, c, :, :, i:i + tile] = part[:, c]
            ex.share(m, j).start()
        for j in range(slabs):
            ex.settle(m, j, keep)
        record(m)
        tidy(m)

    def finish(m):
        slot = m % 2

        grad_f = own[m].astype(f32)
        shared = jnp.sum(grad_f * mix[m], axis=-1, keepdims=True)
        common[m] = (slope[m] * shared).astype(bf16)
        hidden_f = own_in[m].astype(f32)
        inv_rms = lax.rsqrt(jnp.mean(hidden_f * hidden_f, axis=-1, keepdims=True) + norm_eps)
        normed_f = hidden_f * inv_rms
        normed_own[m] = normed_f.astype(bf16)

        @pl.when(s != 0)
        def _():
            total_v[slot] = total_v[slot] - dot_plain(common[m], router[...])
            ex.given(m)
            values = []
            for j in range(slabs):
                value = total_v[slot, :, j * slab:(j + 1) * slab]
                for k in range(1, experts):
                    value = value + back[slot, j, k - 1].astype(f32)
                values.append(value)
            grad_normed = jnp.concatenate(values, axis=-1)
            out_rows[m] = (
                own[m].astype(f32)
                + inv_rms * (grad_normed
                             - normed_f * jnp.mean(grad_normed * normed_f, axis=-1, keepdims=True))
            ).astype(bf16)
            shift(m).start()

    begin(0)
    for load in loads:
        load.wait()

    def unit(m, _):
        ex.arrive(m, lambda block: None)
        keep_grad(m).start()

        @pl.when(m + 1 < units)
        def _():
            begin(m + 1)

        @pl.when((s == 0) & (m == units - 1))
        def _():
            head_sums()

        widen(m)
        keep_grad(m).wait()

        @pl.when(m >= 1)
        def _():
            finish(m - 1)

        @pl.when(s != 0)
        def _():
            narrow(m)

        @pl.when(s == 0)
        def _():
            record(m)
            tidy(m)

        return 0

    lax.fori_loop(0, units, unit, 0)
    finish(units - 1)

    mine = routed[pl.ds(0, expert_count)] - contract_first(
        common[...].reshape(units * rows, lanes), normed_own[...].reshape(units * rows, width))[:expert_count]
    half = width // 2
    parted[...] = jnp.concatenate([mine[:, :half], mine[:, half:]], axis=0).astype(bf16)
    parted_all[me] = parted[...]
    for off in range(1, members):
        router_part(off).start()

    @pl.when(s != 0)
    def _():
        head_sums()
        ex.returned(units - 1)
        for m in range(units):
            shift(m).wait_send()
        for copy in chain():
            copy.wait_send()

    ex.gathered(units - 1)
    for off in range(1, members):
        head_whole(off).wait()
    head_o[...] = head_all[...].astype(f32)
    mean_o[0, 0] = loss_o[0, 0] / (units * every)
    for off in range(1, members):
        router_part(off).wait()
    value = parted_all[0].astype(f32)
    for n in range(1, members):
        value = value + parted_all[n].astype(f32)
    router_o[:, :half] = value[:expert_count]
    router_o[:, half:] = value[expert_count:]

    for m in range(max(0, units - 2), units):
        for copy in writes(m):
            copy.wait()


def backward(sizes, top, hid, dgate, dup, fac, normed, own_in, mix, slope, gate_w, up_w, down_w, router_t, head, loss):
    sections, experts, cores = sizes
    units, rows, width = top.shape
    hidden_dim = gate_w.shape[0]
    members = experts * cores
    every = members * rows
    vmem, hbm = pl.BlockSpec(memory_space=pltpu.VMEM), pl.BlockSpec(memory_space=pl.ANY)
    buffers, sems = exchange_scratch(experts, cores, rows, width)

    def shaped(shape, dtype):
        return jax.ShapeDtypeStruct(shape, dtype)

    acts = (units, every, hidden_dim)
    return pl.pallas_call(
        functools.partial(backward_kernel, sizes),
        out_shape=(
            shaped((units, members, rows, width), bf16), shaped(acts, bf16), shaped(acts, bf16),
            shaped(router_t.shape, f32), shaped(head.shape, f32), shaped((1, 1), f32),
        ),
        in_specs=[hbm] * 6 + [vmem] * 3 + [hbm] * 3 + [vmem] * 3,
        out_specs=(hbm,) * 3 + (vmem,) * 2 + (pl.BlockSpec(memory_space=pltpu.SMEM),),
        scratch_shapes=[
            pltpu.VMEM(gate_w.shape, bf16), pltpu.VMEM(up_w.shape, bf16), pltpu.VMEM(down_w.shape, bf16),
            pltpu.VMEM((2, every, hidden_dim), bf16), pltpu.VMEM((2, every, hidden_dim), bf16),
            pltpu.VMEM((2, every, hidden_dim), bf16), pltpu.VMEM((2, every, lanes), f32),
            pltpu.VMEM((2, every, width), bf16), pltpu.VMEM((units, rows, width), bf16),
            pltpu.VMEM((lanes, width), bf16), pltpu.VMEM((units, rows, lanes), bf16),
            pltpu.VMEM((units, rows, width), bf16),
            pltpu.VMEM((lanes, width), f32), pltpu.VMEM((2 * router_t.shape[0], width // 2), bf16),
            pltpu.VMEM((members, 2 * router_t.shape[0], width // 2), bf16),
            pltpu.VMEM(head.shape, bf16), pltpu.VMEM(head.shape, bf16), pltpu.VMEM((members,) + loss.shape, f32),
            pltpu.VMEM(loss.shape, f32),
            *buffers,
            pltpu.VMEM((units, rows, width), bf16), pltpu.VMEM((2, rows, width), f32),
            pltpu.VMEM((2, every, hidden_dim), bf16), pltpu.VMEM((2, every, hidden_dim), bf16),
            pltpu.VMEM((2, every, lanes), bf16),
            dma((3,)), dma((5, 2)), dma((units,)), dma((units,)), dma((units,)), dma((3, 2)),
            *[dma((members - 1,))] * 8, dma((2,)), dma((2,)),
            *sems,
        ],
        cost_estimate=pl.CostEstimate(
            flops=6 * units * members * rows * width * hidden_dim, bytes_accessed=500_000_000, transcendentals=0),
        compiler_params=pltpu.CompilerParams(
            collective_id=1, has_side_effects=True, vmem_limit_bytes=56 * 1024 * 1024),
    )(top, hid, dgate, dup, fac, normed, own_in, mix, slope, gate_w, up_w, down_w, router_t, head, loss)


def shards(sizes, tokens, expert_ids, labels, router, class_head, w_gate, w_up, w_down):
    sections, experts, cores = sizes
    members = experts * cores
    micro_count, tok_rows, width = tokens.shape
    gate_w, up_w, down_w = w_gate[0, 0], w_up[0, 0], w_down[0, 0]
    hidden_dim = gate_w.shape[1]
    rows = max(row_step, min(tok_rows, tok_rows * 2 // members))
    units = micro_count * tok_rows // rows

    router_t = router[0].T
    ids = jnp.transpose(expert_ids[0], (0, 2, 1))
    normed, hid, dgate, dup, fac, gate_f, up_f, down_f, own_in, mix, slope, top, head_term, loss_term = forward(
        sizes, tokens.reshape(units, rows, width), ids, gate_w, up_w, down_w, router_t, class_head,
        labels)
    grad_all, agate, aup, router_sum, head_total, mean_loss = backward(
        sizes, top, hid, dgate, dup, fac, normed, own_in, mix, slope, gate_f, up_f, down_f, router_t,
        head_term, loss_term)

    every = units * members * rows
    normed = normed.reshape(every, width)
    grad_gate = contract_first(normed, agate.reshape(every, hidden_dim)).astype(bf16)
    grad_up = contract_first(normed, aup.reshape(every, hidden_dim)).astype(bf16)
    grad_down = contract_first(hid.reshape(every, hidden_dim), grad_all.reshape(every, width)).astype(bf16)
    return (
        mean_loss.reshape(()),
        head_total.reshape(width, -1),
        router_sum.T[None],
        grad_gate[None, None],
        grad_up[None, None],
        grad_down[None, None],
    )


def solution(mesh):
    sizes = tuple(mesh.shape[axis] for axis in ("section", "expert", "dp"))
    return jax.shard_map(
        functools.partial(shards, sizes),
        mesh=mesh,
        in_specs=(
            P(None, ("expert", "dp"), None),
            P("section", None, ("expert", "dp"), None),
            P(None, ("expert", "dp")),
            P("section", None, None),
            P(),
            P("section", ("expert", "dp"), None, None),
            P("section", ("expert", "dp"), None, None),
            P("section", ("expert", "dp"), None, None),
        ),
        out_specs=(
            P(),
            P(),
            P("section", None, None),
            P("section", ("expert", "dp"), None, None),
            P("section", ("expert", "dp"), None, None),
            P("section", ("expert", "dp"), None, None),
        ),
        check_vma=False,
    )
```

```python
import functools

import jax
import jax.numpy as jnp
from jax import lax
from jax.experimental import pallas as pl
from jax.experimental.pallas import tpu as pltpu
from jax.sharding import PartitionSpec as P

soft_cap = 30.0
norm_eps = 1e-06
lanes = 128
row_step = 16
MESH = pl.DeviceIdType.MESH
dma = pltpu.SemaphoreType.DMA
bf16 = jnp.bfloat16
f32 = jnp.float32


def capped(values):
    return soft_cap * jnp.tanh(values / soft_cap)


def dot_plain(left, right):
    return jnp.dot(left, right, preferred_element_type=f32)


def contract_first(left, right):
    return lax.dot_general(left, right, (((0,), (0,)), ((), ())), preferred_element_type=f32)


def contract_last(left, right):
    return lax.dot_general(left, right, (((1,), (1,)), ((), ())), preferred_element_type=f32)


def partner(e, k, count):
    total, bit = 0, 1
    while bit < count:
        a, b = (e // bit) % 2, (k // bit) % 2
        total = total + (a + b - 2 * a * b) * bit
        bit *= 2
    return total


class Exchange:
    def __init__(self, sizes, own, gath, parts, stage, sums, back, sems):
        self.sizes, self.own, self.gath = sizes, own, gath
        self.parts, self.stage, self.sums, self.back = parts, stage, sums, back
        (self.x_send, self.x_recv, self.d_send, self.d_recv, self.f_send, self.f_recv,
         self.p_send, self.p_recv, self.r_send, self.r_recv) = sems
        self.e, self.d = lax.axis_index("expert"), lax.axis_index("dp")
        self.me = self.e * 2 + self.d
        self.slabs, self.wide = parts.shape[1], parts.shape[-1]

    def chip(self, k):
        return partner(self.e, k, self.sizes[1])

    def across(self, m, k):
        slot = m % 3
        return pltpu.make_async_remote_copy(
            src_ref=self.own.at[m], dst_ref=self.gath.at[slot, self.me],
            send_sem=self.x_send.at[slot, k - 1], recv_sem=self.x_recv.at[slot, k - 1],
            device_id={"expert": self.chip(k)}, device_id_type=MESH)

    def beside(self, m):
        slot = m % 3
        return pltpu.make_async_remote_copy(
            src_ref=self.own.at[m], dst_ref=self.gath.at[slot, self.me],
            send_sem=self.d_send.at[slot], recv_sem=self.d_recv.at[slot],
            device_id={"dp": 1 - self.d}, device_id_type=MESH)

    def onward(self, m, k):
        slot = m % 3
        block = self.chip(k) * 2 + self.d
        return pltpu.make_async_remote_copy(
            src_ref=self.gath.at[slot, block], dst_ref=self.gath.at[slot, block],
            send_sem=self.f_send.at[slot, k - 1], recv_sem=self.f_recv.at[slot, k - 1],
            device_id={"dp": 1 - self.d}, device_id_type=MESH)

    def share(self, m, j):
        slot = m % 2
        return pltpu.make_async_remote_copy(
            src_ref=self.parts.at[slot, j, 1 - self.d], dst_ref=self.stage.at[slot, j],
            send_sem=self.p_send.at[slot, j], recv_sem=self.p_recv.at[slot, j],
            device_id={"dp": 1 - self.d}, device_id_type=MESH)

    def give(self, m, j, k):
        slot = m % 2
        return pltpu.make_async_remote_copy(
            src_ref=self.sums.at[slot, j, k - 1], dst_ref=self.back.at[slot, j, k - 1],
            send_sem=self.r_send.at[slot, j, k - 1], recv_sem=self.r_recv.at[slot, j, k - 1],
            device_id={"expert": self.chip(k)}, device_id_type=MESH)

    def spread(self, m):
        for k in sorted(range(1, self.sizes[1]), key=lambda k: -bin(k).count("1")):
            self.across(m, k).start()
        self.beside(m).start()
        self.gath[m % 3, self.me] = self.own[m]

    def arrive(self, m, use):
        experts = self.sizes[1]
        use(self.me)
        self.beside(m).wait_recv()
        use(self.e * 2 + 1 - self.d)
        for k in range(1, experts):
            self.across(m, k).wait_recv()
            self.onward(m, k).start()
            use(self.chip(k) * 2 + self.d)
        for k in range(1, experts):
            self.onward(m, k).wait_recv()
            use(self.chip(k) * 2 + 1 - self.d)

    def passed_on(self, m):
        for k in range(1, self.sizes[1]):
            self.onward(m, k).wait_send()

    def settle(self, m, j, keep_own):
        slot = m % 2
        experts = self.sizes[1]
        self.share(m, j).wait_recv()
        for k in range(experts - 1, -1, -1):
            chip = self.chip(k)
            value = self.parts[slot, j, self.d, chip].astype(f32) + self.stage[slot, j, chip].astype(f32)
            if k == 0:
                keep_own(j, value)
            else:
                self.sums[slot, j, k - 1] = value.astype(bf16)
                self.give(m, j, k).start()

    def gathered(self, m):
        self.beside(m).wait_send()
        for k in range(1, self.sizes[1]):
            self.across(m, k).wait_send()

    def given(self, m):
        for j in range(self.slabs):
            for k in range(1, self.sizes[1]):
                self.give(m, j, k).wait_recv()

    def returned(self, m):
        for j in range(self.slabs):
            self.share(m, j).wait_send()
            for k in range(1, self.sizes[1]):
                self.give(m, j, k).wait_send()


def tall(router_t):
    rows = router_t[...].astype(f32)
    return jnp.concatenate([rows, jnp.zeros((lanes - rows.shape[0], rows.shape[1]), f32)], axis=0).astype(bf16)


def meet(sizes, step):
    sections, experts, cores = sizes
    s, e, d = lax.axis_index("section"), lax.axis_index("expert"), lax.axis_index("dp")
    me = e * cores + d
    first, last = (0, sections - 1) if step > 0 else (sections - 1, 0)
    barrier = pltpu.get_barrier_semaphore()
    count = experts * cores - 1
    for off in range(1, experts * cores):
        other = lax.rem(me + off, experts * cores)
        pl.semaphore_signal(
            barrier, inc=1, device_id={"expert": other // cores, "dp": lax.rem(other, cores)},
            device_id_type=MESH)

    @pl.when(s != first)
    def _():
        pl.semaphore_signal(barrier, inc=1, device_id={"section": s - step}, device_id_type=MESH)

    pl.semaphore_wait(barrier, count + (s != last).astype(jnp.int32))


def forward_kernel(sizes, tokens, ids, gate, up, down, router_t, head, labels,
                   normed_o, hid_o, dgate_o, dup_o, fac_o, gate_o, up_o, down_o, own, mix, slope_o, top_o, head_o, loss_o,
                   gate_v, up_v, down_v, gate_f, up_f, down_f, mask, mask_all, router, gath, parts, stage, sums, back, out_rows,
                   normed_t, hid_t, dgate_t, dup_t, fac_t, slope_t,
                   w_sem, f_sem, k_send, k_recv, t_sem, z_send, z_recv, o_sem, *sems):
    sections, experts, cores = sizes
    units, rows, width = own.shape
    hidden_dim = gate_v.shape[1]
    s = lax.axis_index("section")
    last = sections - 1
    ex = Exchange(sizes, own, gath, parts, stage, sums, back, sems)
    e, d, me = ex.e, ex.d, ex.me
    members = experts * cores
    every = members * rows
    slabs, slab = ex.slabs, ex.wide

    loads = [pltpu.make_async_copy(a, b, w_sem.at[n])
             for n, (a, b) in enumerate(((gate, gate_v), (up, up_v), (down, down_v)))]
    for load in loads:
        load.start()

    def take(m):
        return pltpu.make_async_copy(tokens.at[m], own.at[m], t_sem.at[m])

    @pl.when(s == 0)
    def _():
        for m in range(units):
            take(m).start()

    micro_count, _, micro_rows = ids.shape
    expert_row = lax.broadcasted_iota(jnp.int32, (lanes, micro_rows), 0)
    marks = []
    for n in range(micro_count):
        named = expert_row == ids[n, 0:1]
        for k in range(1, ids.shape[1]):
            named = named | (expert_row == ids[n, k:k + 1])
        marks.append(jnp.where(named, 1.0, 0.0).T)
    mask[...] = jnp.concatenate(marks, axis=0).astype(bf16).reshape(units, rows, lanes)
    router[...] = tall(router_t)
    meet(sizes, 1)

    def tell(off):
        other = lax.rem(me + off, members)
        return pltpu.make_async_remote_copy(
            src_ref=mask, dst_ref=mask_all.at[me], send_sem=k_send.at[off - 1], recv_sem=k_recv.at[off - 1],
            device_id={"expert": other // cores, "dp": lax.rem(other, cores)}, device_id_type=MESH)

    def shift(m, j):
        cols = pl.ds(j * slab, slab)
        return pltpu.make_async_remote_copy(
            src_ref=out_rows.at[m, :, cols], dst_ref=own.at[m, :, cols],
            send_sem=z_send.at[m, j], recv_sem=z_recv.at[m, j],
            device_id={"section": lax.rem(s + 1, sections)}, device_id_type=MESH)

    def begin(m):
        @pl.when(s == 0)
        def _():
            take(m).wait()

        @pl.when(s != 0)
        def _():
            for j in range(slabs):
                shift(m, j).wait_recv()

        ex.spread(m)

    def writes(m):
        side = m % 2
        pairs = ((normed_t, normed_o), (hid_t, hid_o), (dgate_t, dgate_o), (dup_t, dup_o), (fac_t, fac_o))
        return [pltpu.make_async_copy(a.at[side], b.at[m], o_sem.at[n, side])
                for n, (a, b) in enumerate(pairs)]

    lane = lax.broadcasted_iota(jnp.int32, (every, lanes), 1)

    def enter(m):
        slot = m % 2

        @pl.when(m >= 2)
        def _():
            for copy in writes(m):
                copy.wait()

        def norm_block(block):
            def norm(r, _):
                at = pl.ds(pl.multiple_of(r * row_step, row_step), row_step)
                values = gath[m % 3, block, at].astype(f32)
                inv = lax.rsqrt(jnp.mean(values * values, axis=-1, keepdims=True) + norm_eps)
                normed_t[slot, pl.ds(pl.multiple_of(block * rows + r * row_step, row_step), row_step)] = (
                    values * inv).astype(bf16)
                return 0
            lax.fori_loop(0, rows // row_step, norm, 0)

        ex.arrive(m, norm_block)

    def widen(m):
        slot = m % 2
        chosen = capped(contract_last(normed_t[slot], router[...]))
        named = mask_all[:, m].reshape(every, lanes).astype(f32)
        weights = jnp.exp(chosen) * named
        probs = weights / jnp.sum(weights, axis=-1, keepdims=True)
        scaled = chosen / soft_cap
        bend = 1.0 - scaled * scaled
        mine = jnp.sum(jnp.where(lane == me, probs, 0.0), axis=-1, keepdims=True)

        wide = 256 if hidden_dim % 256 == 0 else hidden_dim
        for j in range(0, hidden_dim, wide):
            cols = slice(j, j + wide)
            gate_act = dot_plain(normed_t[slot], gate_v[:, cols])
            up_act = dot_plain(normed_t[slot], up_v[:, cols])
            sig = jax.nn.sigmoid(gate_act)
            silu = mine * (gate_act * sig)
            hid_t[slot, :, cols] = (silu * up_act).astype(bf16)
            dgate_t[slot, :, cols] = (mine * up_act * sig * (1.0 + gate_act * (1.0 - sig))).astype(bf16)
            dup_t[slot, :, cols] = silu.astype(bf16)
        return probs, bend

    def narrow(m, probs, bend):
        slot = m % 2

        def keep(j, value):
            mix[m, :, j * slab:(j + 1) * slab] = value

        tile = 512 if slab % 512 == 0 else slab
        for j in range(slabs):
            for i in range(0, slab, tile):
                part = dot_plain(hid_t[slot], down_v[:, j * slab + i:j * slab + i + tile]).astype(bf16)
                part = part.reshape(experts, cores, rows, tile)
                for c in range(cores):
                    parts[slot, j, c, :, :, i:i + tile] = part[:, c]
            ex.share(m, j).start()
        for j in range(slabs):
            ex.settle(m, j, keep)
        fac_t[slot] = jnp.broadcast_to(
            jnp.sum(jnp.where(lane == me, bend, 0.0), axis=-1, keepdims=True), (every, lanes))
        slope_t[...] = (probs * bend).reshape(members, rows, lanes)
        slope_o[m] = slope_t[me]
        for copy in writes(m):
            copy.start()
        ex.passed_on(m)

        @pl.when(m >= 1)
        def _():
            ex.gathered(m - 1)
            ex.returned(m - 1)


    def finish(m):
        slot = m % 2
        for j in range(slabs):
            for k in range(1, experts):
                ex.give(m, j, k).wait_recv()
            cols = slice(j * slab, (j + 1) * slab)
            value = mix[m, :, cols]
            for k in range(1, experts):
                value = value + back[slot, j, k - 1].astype(f32)
            mix[m, :, cols] = value
            out_rows[m, :, cols] = (own[m, :, cols].astype(f32) + value).astype(bf16)

            @pl.when(s != last)
            def _():
                shift(m, j).start()

    flips = [pltpu.make_async_copy(a, b, f_sem.at[n])
             for n, (a, b) in enumerate(((gate_f, gate_o), (up_f, up_o), (down_f, down_o)))]

    def turn(source, target):
        tall_by = 256 if source.shape[0] % 256 == 0 else source.shape[0]

        def step(r, _):
            at = pl.ds(pl.multiple_of(r * tall_by, tall_by), tall_by)
            target[:, at] = source[at].astype(f32).T.astype(bf16)
            return 0
        lax.fori_loop(0, source.shape[0] // tall_by, step, 0)

    def flip():
        turn(gate_v, gate_f)
        turn(up_v, up_f)
        turn(down_v, down_f)
        for copy in flips:
            copy.start()

    mask_all[me] = mask[...]
    for off in range(1, members):
        tell(off).start()

    @pl.when(s == 0)
    def _():
        begin(0)

    for load in loads:
        load.wait()

    @pl.when(s != 0)
    def _():
        flip()
        begin(0)

    for off in range(1, members):
        tell(off).wait()

    def unit(m, _):
        enter(m)

        @pl.when(m + 1 < units)
        def _():
            begin(m + 1)

        probs, bend = widen(m)

        @pl.when(m >= 1)
        def _():
            finish(m - 1)

        narrow(m, probs, bend)
        return 0

    lax.fori_loop(0, units, unit, 0)
    finish(units - 1)

    @pl.when(s == 0)
    def _():
        flip()

    ex.gathered(units - 1)
    ex.returned(units - 1)

    @pl.when(s != last)
    def _():
        head_o[...] = jnp.zeros_like(head_o)
        loss_o[...] = jnp.zeros_like(loss_o)
        for m in range(units):
            for j in range(slabs):
                shift(m, j).wait_send()

    @pl.when(s == last)
    def _():
        final = out_rows[...].reshape(units * rows, width)
        class_logits = capped(dot_plain(final, head[...]))
        class_weights = jnp.exp(class_logits)
        class_total = jnp.sum(class_weights, axis=-1, keepdims=True)
        class_row = lax.broadcasted_iota(jnp.int32, (class_logits.shape[1], labels.shape[1]), 0)
        label_hot = jnp.concatenate(
            [jnp.where(class_row == labels[n:n + 1], 1.0, 0.0).T for n in range(labels.shape[0])], axis=0)
        loss = jnp.log(class_total) - jnp.sum(label_hot * class_logits, axis=-1, keepdims=True)
        scaled = class_logits / soft_cap
        grad_logits = ((class_weights / class_total - label_hot) * (1.0 - scaled * scaled)).astype(bf16)
        top_o[...] = contract_last(grad_logits, head[...]).astype(bf16).reshape(units, rows, width)
        head_o[...] = contract_first(final, grad_logits).reshape(head_o.shape).astype(bf16)
        loss_o[...] = jnp.full(loss_o.shape, jnp.sum(loss), f32)

    for m in range(max(0, units - 2), units):
        for copy in writes(m):
            copy.wait()
    for copy in flips:
        copy.wait()


def exchange_scratch(experts, cores, rows, width):
    slabs = 2 if width % 256 == 0 else 1
    slab = width // slabs
    return [
        pltpu.VMEM((3, experts * cores, rows, width), bf16),
        pltpu.VMEM((2, slabs, cores, experts, rows, slab), bf16),
        pltpu.VMEM((2, slabs, experts, rows, slab), bf16),
        pltpu.VMEM((2, slabs, experts - 1, rows, slab), bf16),
        pltpu.VMEM((2, slabs, experts - 1, rows, slab), bf16),
    ], [
        dma((3, experts - 1)), dma((3, experts - 1)), dma((3,)), dma((3,)),
        dma((3, experts - 1)), dma((3, experts - 1)), dma((2, slabs)), dma((2, slabs)),
        dma((2, slabs, experts - 1)), dma((2, slabs, experts - 1)),
    ]


def forward(sizes, tokens, ids, gate_w, up_w, down_w, router_t, head, labels):
    sections, experts, cores = sizes
    units, rows, width = tokens.shape
    hidden_dim = gate_w.shape[1]
    members = experts * cores
    every = members * rows
    vmem, hbm = pl.BlockSpec(memory_space=pltpu.VMEM), pl.BlockSpec(memory_space=pl.ANY)
    buffers, sems = exchange_scratch(experts, cores, rows, width)

    def shaped(shape, dtype):
        return jax.ShapeDtypeStruct(shape, dtype)

    acts = (units, every, hidden_dim)
    return pl.pallas_call(
        functools.partial(forward_kernel, sizes),
        out_shape=(
            shaped((units, every, width), bf16), shaped(acts, bf16), shaped(acts, bf16),
            shaped(acts, bf16), shaped((units, every, lanes), f32),
            shaped(gate_w.shape[::-1], bf16), shaped(up_w.shape[::-1], bf16), shaped(down_w.shape[::-1], bf16),
            shaped((units, rows, width), bf16), shaped((units, rows, width), f32),
            shaped((units, rows, lanes), f32), shaped((units, rows, width), bf16),
            shaped((members, width // members, head.shape[1]), bf16), shaped((8, lanes), f32),
        ),
        in_specs=[hbm, vmem, hbm, hbm, hbm, vmem, vmem, vmem],
        out_specs=(hbm,) * 8 + (vmem,) * 6,
        scratch_shapes=[
            pltpu.VMEM(gate_w.shape, bf16), pltpu.VMEM(up_w.shape, bf16), pltpu.VMEM(down_w.shape, bf16),
            pltpu.VMEM(gate_w.shape[::-1], bf16), pltpu.VMEM(up_w.shape[::-1], bf16),
            pltpu.VMEM(down_w.shape[::-1], bf16),
            pltpu.VMEM((units, rows, lanes), bf16), pltpu.VMEM((members, units, rows, lanes), bf16),
            pltpu.VMEM((lanes, width), bf16),
            *buffers,
            pltpu.VMEM((units, rows, width), bf16),
            pltpu.VMEM((2, every, width), bf16), pltpu.VMEM((2, every, hidden_dim), bf16),
            pltpu.VMEM((2, every, hidden_dim), bf16), pltpu.VMEM((2, every, hidden_dim), bf16),
            pltpu.VMEM((2, every, lanes), f32), pltpu.VMEM((members, rows, lanes), f32),
            dma((3,)), dma((3,)), dma((members - 1,)), dma((members - 1,)), dma((units,)),
            dma((units, buffers[1].shape[1])), dma((units, buffers[1].shape[1])), dma((5, 2)),
            *sems,
        ],
        cost_estimate=pl.CostEstimate(
            flops=6 * units * members * rows * width * hidden_dim, bytes_accessed=500_000_000, transcendentals=0),
        compiler_params=pltpu.CompilerParams(
            collective_id=0, has_side_effects=True, vmem_limit_bytes=56 * 1024 * 1024),
    )(tokens, ids, gate_w, up_w, down_w, router_t, head, labels)


def backward_kernel(sizes, top, hid, dgate, dup, fac, normed, own_in, mix, slope, gate, up, down, router_t, head_in, loss_in,
                    grad_o, agate_o, aup_o, router_o, head_o, mean_o,
                    gate_v, up_v, down_v, hid_v, dgate_v, dup_v, fac_v, normed_v, own, router, common, normed_own,
                    routed, parted, parted_all, head_part, head_all, loss_all, loss_o,
                    gath, parts, stage, sums, back, out_rows, total_v,
                    agate_t, aup_t, route_t,
                    w_sem, i_sem, t_sem, z_send, z_recv, o_sem, q_send, q_recv, h_send, h_recv, l_send, l_recv,
                    b_send, b_recv, c_send, c_recv, *sems):
    sections, experts, cores = sizes
    units, rows, width = own.shape
    hidden_dim = gate_v.shape[0]
    expert_count = router_t.shape[0]
    s = lax.axis_index("section")
    last = sections - 1
    ex = Exchange(sizes, own, gath, parts, stage, sums, back, sems)
    e, d, me = ex.e, ex.d, ex.me
    members = experts * cores
    every = members * rows
    slabs, slab = ex.slabs, ex.wide

    loads = [pltpu.make_async_copy(a, b, w_sem.at[n]) for n, (a, b) in enumerate((
        (down, down_v), (gate, gate_v), (up, up_v)))]

    def reads(m):
        side = m % 2
        pairs = ((hid, hid_v), (dgate, dgate_v), (dup, dup_v), (fac, fac_v), (normed, normed_v))
        return [pltpu.make_async_copy(a.at[m], b.at[side], i_sem.at[n, side]) for n, (a, b) in enumerate(pairs)]

    for load in loads:
        load.start()
    for m in range(min(2, units)):
        for copy in reads(m):
            copy.start()

    def take(m):
        return pltpu.make_async_copy(top.at[m], own.at[m], t_sem.at[m])

    @pl.when(s == last)
    def _():
        for m in range(units):
            take(m).start()

    router[...] = tall(router_t)
    routed[...] = jnp.zeros_like(routed)
    meet(sizes, -1)

    def other(off):
        to = lax.rem(me + off, members)
        return to, {"expert": to // cores, "dp": lax.rem(to, cores)}

    def head_piece(off):
        to, device = other(off)
        return pltpu.make_async_remote_copy(
            src_ref=head_in.at[to], dst_ref=head_part.at[me], send_sem=h_send.at[off - 1],
            recv_sem=h_recv.at[off - 1], device_id=device, device_id_type=MESH)

    def loss_piece(off):
        to, device = other(off)
        return pltpu.make_async_remote_copy(
            src_ref=loss_in, dst_ref=loss_all.at[me], send_sem=l_send.at[off - 1],
            recv_sem=l_recv.at[off - 1], device_id=device, device_id_type=MESH)

    def head_whole(off):
        to, device = other(off)
        return pltpu.make_async_remote_copy(
            src_ref=head_all.at[me], dst_ref=head_all.at[me], send_sem=b_send.at[off - 1],
            recv_sem=b_recv.at[off - 1], device_id=device, device_id_type=MESH)

    def router_part(off):
        to, device = other(off)
        return pltpu.make_async_remote_copy(
            src_ref=parted, dst_ref=parted_all.at[me], send_sem=q_send.at[off - 1],
            recv_sem=q_recv.at[off - 1], device_id=device, device_id_type=MESH)

    down_section = {"section": lax.rem(s + sections - 1, sections)}

    def chain():
        return [
            pltpu.make_async_remote_copy(
                src_ref=head_all.at[me], dst_ref=head_all.at[me], send_sem=c_send.at[0], recv_sem=c_recv.at[0],
                device_id=down_section, device_id_type=MESH),
            pltpu.make_async_remote_copy(
                src_ref=loss_o, dst_ref=loss_o, send_sem=c_send.at[1], recv_sem=c_recv.at[1],
                device_id=down_section, device_id_type=MESH),
        ]

    def head_sums():
        @pl.when(s == last)
        def _():
            for off in range(1, members):
                head_piece(off).start()
                loss_piece(off).start()
            head_part[me] = head_in[me]
            loss_all[me] = loss_in[...]
            for off in range(1, members):
                head_piece(off).wait()
                loss_piece(off).wait()
            value, loss = head_part[0].astype(f32), loss_all[0]
            for n in range(1, members):
                value, loss = value + head_part[n].astype(f32), loss + loss_all[n]
            head_all[me] = value.astype(bf16)
            loss_o[...] = loss

        @pl.when(s != last)
        def _():
            for copy in chain():
                copy.wait_recv()

        @pl.when(s != 0)
        def _():
            for copy in chain():
                copy.start()

        for off in range(1, members):
            head_whole(off).start()

    def shift(m):
        return pltpu.make_async_remote_copy(
            src_ref=out_rows.at[m], dst_ref=own.at[m], send_sem=z_send.at[m], recv_sem=z_recv.at[m],
            device_id={"section": lax.rem(s + sections - 1, sections)}, device_id_type=MESH)

    def begin(m):
        @pl.when(s == last)
        def _():
            take(m).wait()

        @pl.when(s != last)
        def _():
            shift(m).wait_recv()

        ex.spread(m)

    def writes(m):
        side = m % 2
        pairs = ((agate_t, agate_o), (aup_t, aup_o))
        return [pltpu.make_async_copy(a.at[side], b.at[m], o_sem.at[n, side])
                for n, (a, b) in enumerate(pairs)]

    def keep_grad(m):
        return pltpu.make_async_copy(gath.at[m % 3], grad_o.at[m], o_sem.at[2, 0])

    lane = lax.broadcasted_iota(jnp.int32, (every, lanes), 1)

    def widen(m):
        slot = m % 2

        @pl.when(m >= 2)
        def _():
            for copy in writes(m):
                copy.wait()

        for copy in reads(m):
            copy.wait()
        grads = gath[m % 3].reshape(every, width)
        gain = jnp.zeros((every, 1), f32)
        wide = 256 if hidden_dim % 256 == 0 else hidden_dim
        for j in range(0, hidden_dim, wide):
            cols = slice(j, j + wide)
            down_grad = dot_plain(grads, down_v[:, cols])
            agate_t[slot, :, cols] = (down_grad * dgate_v[slot, :, cols].astype(f32)).astype(bf16)
            aup_t[slot, :, cols] = (down_grad * dup_v[slot, :, cols].astype(f32)).astype(bf16)
            gain = gain + jnp.sum(down_grad * hid_v[slot, :, cols].astype(f32), axis=-1, keepdims=True)
        route_t[slot] = jnp.where(lane == me, gain * fac_v[slot], 0.0).astype(bf16)

    def record(m):
        slot = m % 2
        for copy in writes(m):
            copy.start()
        tile = 512 if width % 512 == 0 else width
        for i in range(0, width, tile):
            cols = slice(i, i + tile)
            routed[:, cols] = routed[:, cols] + contract_first(route_t[slot], normed_v[slot, :, cols])

    def tidy(m):
        @pl.when(m + 2 < units)
        def _():
            for copy in reads(m + 2):
                copy.start()

        ex.passed_on(m)

        @pl.when(m >= 1)
        def _():
            ex.gathered(m - 1)

        @pl.when((m >= 1) & (s != 0))
        def _():
            ex.returned(m - 1)

    def narrow(m):
        slot = m % 2

        def keep(j, value):
            total_v[slot, :, j * slab:(j + 1) * slab] = value

        tile = 512 if slab % 512 == 0 else slab
        for j in range(slabs):
            for i in range(0, slab, tile):
                cols = slice(j * slab + i, j * slab + i + tile)
                part = (dot_plain(agate_t[slot], gate_v[:, cols])
                        + dot_plain(aup_t[slot], up_v[:, cols])
                        + dot_plain(route_t[slot], router[:, cols]))
                part = part.astype(bf16).reshape(experts, cores, rows, tile)
                for c in range(cores):
                    parts[slot, j, c, :, :, i:i + tile] = part[:, c]
            ex.share(m, j).start()
        for j in range(slabs):
            ex.settle(m, j, keep)
        record(m)
        tidy(m)

    def finish(m):
        slot = m % 2

        grad_f = own[m].astype(f32)
        shared = jnp.sum(grad_f * mix[m], axis=-1, keepdims=True)
        common[m] = (slope[m] * shared).astype(bf16)
        hidden_f = own_in[m].astype(f32)
        inv_rms = lax.rsqrt(jnp.mean(hidden_f * hidden_f, axis=-1, keepdims=True) + norm_eps)
        normed_f = hidden_f * inv_rms
        normed_own[m] = normed_f.astype(bf16)

        @pl.when(s != 0)
        def _():
            total_v[slot] = total_v[slot] - dot_plain(common[m], router[...])
            ex.given(m)
            values = []
            for j in range(slabs):
                value = total_v[slot, :, j * slab:(j + 1) * slab]
                for k in range(1, experts):
                    value = value + back[slot, j, k - 1].astype(f32)
                values.append(value)
            grad_normed = jnp.concatenate(values, axis=-1)
            out_rows[m] = (
                own[m].astype(f32)
                + inv_rms * (grad_normed
                             - normed_f * jnp.mean(grad_normed * normed_f, axis=-1, keepdims=True))
            ).astype(bf16)
            shift(m).start()

    begin(0)
    for load in loads:
        load.wait()

    def unit(m, _):
        ex.arrive(m, lambda block: None)
        keep_grad(m).start()

        @pl.when(m + 1 < units)
        def _():
            begin(m + 1)

        @pl.when((s == 0) & (m == units - 1))
        def _():
            head_sums()

        widen(m)
        keep_grad(m).wait()

        @pl.when(m >= 1)
        def _():
            finish(m - 1)

        @pl.when(s != 0)
        def _():
            narrow(m)

        @pl.when(s == 0)
        def _():
            record(m)
            tidy(m)

        return 0

    lax.fori_loop(0, units, unit, 0)
    finish(units - 1)

    mine = routed[pl.ds(0, expert_count)] - contract_first(
        common[...].reshape(units * rows, lanes), normed_own[...].reshape(units * rows, width))[:expert_count]
    half = width // 2
    parted[...] = jnp.concatenate([mine[:, :half], mine[:, half:]], axis=0).astype(bf16)
    parted_all[me] = parted[...]
    for off in range(1, members):
        router_part(off).start()

    @pl.when(s != 0)
    def _():
        head_sums()
        ex.returned(units - 1)
        for m in range(units):
            shift(m).wait_send()
        for copy in chain():
            copy.wait_send()

    ex.gathered(units - 1)
    for off in range(1, members):
        head_whole(off).wait()
    head_o[...] = head_all[...].astype(f32)
    mean_o[0, 0] = loss_o[0, 0] / (units * every)
    for off in range(1, members):
        router_part(off).wait()
    value = parted_all[0].astype(f32)
    for n in range(1, members):
        value = value + parted_all[n].astype(f32)
    router_o[:, :half] = value[:expert_count]
    router_o[:, half:] = value[expert_count:]

    for m in range(max(0, units - 2), units):
        for copy in writes(m):
            copy.wait()


def backward(sizes, top, hid, dgate, dup, fac, normed, own_in, mix, slope, gate_w, up_w, down_w, router_t, head, loss):
    sections, experts, cores = sizes
    units, rows, width = top.shape
    hidden_dim = gate_w.shape[0]
    members = experts * cores
    every = members * rows
    vmem, hbm = pl.BlockSpec(memory_space=pltpu.VMEM), pl.BlockSpec(memory_space=pl.ANY)
    buffers, sems = exchange_scratch(experts, cores, rows, width)

    def shaped(shape, dtype):
        return jax.ShapeDtypeStruct(shape, dtype)

    acts = (units, every, hidden_dim)
    return pl.pallas_call(
        functools.partial(backward_kernel, sizes),
        out_shape=(
            shaped((units, members, rows, width), bf16), shaped(acts, bf16), shaped(acts, bf16),
            shaped(router_t.shape, f32), shaped(head.shape, f32), shaped((1, 1), f32),
        ),
        in_specs=[hbm] * 6 + [vmem] * 3 + [hbm] * 3 + [vmem] * 3,
        out_specs=(hbm,) * 3 + (vmem,) * 2 + (pl.BlockSpec(memory_space=pltpu.SMEM),),
        scratch_shapes=[
            pltpu.VMEM(gate_w.shape, bf16), pltpu.VMEM(up_w.shape, bf16), pltpu.VMEM(down_w.shape, bf16),
            pltpu.VMEM((2, every, hidden_dim), bf16), pltpu.VMEM((2, every, hidden_dim), bf16),
            pltpu.VMEM((2, every, hidden_dim), bf16), pltpu.VMEM((2, every, lanes), f32),
            pltpu.VMEM((2, every, width), bf16), pltpu.VMEM((units, rows, width), bf16),
            pltpu.VMEM((lanes, width), bf16), pltpu.VMEM((units, rows, lanes), bf16),
            pltpu.VMEM((units, rows, width), bf16),
            pltpu.VMEM((lanes, width), f32), pltpu.VMEM((2 * router_t.shape[0], width // 2), bf16),
            pltpu.VMEM((members, 2 * router_t.shape[0], width // 2), bf16),
            pltpu.VMEM(head.shape, bf16), pltpu.VMEM(head.shape, bf16), pltpu.VMEM((members,) + loss.shape, f32),
            pltpu.VMEM(loss.shape, f32),
            *buffers,
            pltpu.VMEM((units, rows, width), bf16), pltpu.VMEM((2, rows, width), f32),
            pltpu.VMEM((2, every, hidden_dim), bf16), pltpu.VMEM((2, every, hidden_dim), bf16),
            pltpu.VMEM((2, every, lanes), bf16),
            dma((3,)), dma((5, 2)), dma((units,)), dma((units,)), dma((units,)), dma((3, 2)),
            *[dma((members - 1,))] * 8, dma((2,)), dma((2,)),
            *sems,
        ],
        cost_estimate=pl.CostEstimate(
            flops=6 * units * members * rows * width * hidden_dim, bytes_accessed=500_000_000, transcendentals=0),
        compiler_params=pltpu.CompilerParams(
            collective_id=1, has_side_effects=True, vmem_limit_bytes=56 * 1024 * 1024),
    )(top, hid, dgate, dup, fac, normed, own_in, mix, slope, gate_w, up_w, down_w, router_t, head, loss)


def shards(sizes, tokens, expert_ids, labels, router, class_head, w_gate, w_up, w_down):
    sections, experts, cores = sizes
    members = experts * cores
    micro_count, tok_rows, width = tokens.shape
    gate_w, up_w, down_w = w_gate[0, 0], w_up[0, 0], w_down[0, 0]
    hidden_dim = gate_w.shape[1]
    rows = max(row_step, min(tok_rows, tok_rows * 2 // members))
    units = micro_count * tok_rows // rows

    router_t = router[0].T
    ids = jnp.transpose(expert_ids[0], (0, 2, 1))
    normed, hid, dgate, dup, fac, gate_f, up_f, down_f, own_in, mix, slope, top, head_term, loss_term = forward(
        sizes, tokens.reshape(units, rows, width), ids, gate_w, up_w, down_w, router_t, class_head,
        labels)
    grad_all, agate, aup, router_sum, head_total, mean_loss = backward(
        sizes, top, hid, dgate, dup, fac, normed, own_in, mix, slope, gate_f, up_f, down_f, router_t,
        head_term, loss_term)

    every = units * members * rows
    normed = normed.reshape(every, width)
    grad_gate = contract_first(normed, agate.reshape(every, hidden_dim)).astype(bf16)
    grad_up = contract_first(normed, aup.reshape(every, hidden_dim)).astype(bf16)
    grad_down = contract_first(hid.reshape(every, hidden_dim), grad_all.reshape(every, width)).astype(bf16)
    return (
        mean_loss.reshape(()),
        head_total.reshape(width, -1),
        router_sum.T[None],
        grad_gate[None, None],
        grad_up[None, None],
        grad_down[None, None],
    )


def solution(mesh):
    sizes = tuple(mesh.shape[axis] for axis in ("section", "expert", "dp"))
    return jax.shard_map(
        functools.partial(shards, sizes),
        mesh=mesh,
        in_specs=(
            P(None, ("expert", "dp"), None),
            P("section", None, ("expert", "dp"), None),
            P(None, ("expert", "dp")),
            P("section", None, None),
            P(),
            P("section", ("expert", "dp"), None, None),
            P("section", ("expert", "dp"), None, None),
            P("section", ("expert", "dp"), None, None),
        ),
        out_specs=(
            P(),
            P(),
            P("section", None, None),
            P("section", ("expert", "dp"), None, None),
            P("section", ("expert", "dp"), None, None),
            P("section", ("expert", "dp"), None, None),
        ),
        check_vma=False,
    )
```
